32 devices in a mesh: ens: 2 (over core), gx: 4 (over y, x), gy: 4 (over z).
Axes of the slice: x: 2, y: 2, z: 4, core: 2. Of those that a mesh axis runs over, the one named last changes fastest.
Arguments:
- velocity: float32 [2, 2, 1024, 512], P('ens', None, 'gx', 'gy'), may hold values from -6 to 6
- targets: float32 [2, 2, 2, 1024, 512], P('ens', None, None, 'gx', 'gy'), may hold values from -6 to 6
- weight_one: bfloat16 [3, 3, 2, 64], replicated, may hold values from -1.5 to 1.5
- bias_one: float32 [64], replicated, may hold values from -3 to 3
- weight_two: bfloat16 [64, 64], replicated, may hold values from -0.75 to 0.75
- bias_two: float32 [64], replicated, may hold values from -3 to 3
- weight_three: bfloat16 [3, 3, 64, 6], replicated, may hold values from -0.25 to 0.25
Outputs:
- dir_weight_one: float32 [3, 3, 2, 64], replicated
- dir_bias_one: float32 [64], replicated
- dir_weight_two: float32 [64, 64], replicated
- dir_bias_two: float32 [64], replicated
- dir_weight_three: float32 [3, 3, 64, 6], replicated
- mean_loss: float32 [], replicated
- grad_velocity: float32 [2, 2, 1024, 512], P('ens', None, 'gx', 'gy')
The draws below stay inside these ranges and needn't reach their ends.
All inputs are finite; a program needn't handle non-finite values.
Results may differ from the reference program's by a relative error of at most 0.0015.
Values sent between devices are 32-bit elements; how exact they have to be, the bound alone decides.
No kernel may reach another device: no remote copies, remote signals or barrier semaphores. Data moves between devices by JAX's collectives and lax.ppermute only.
A program may use at most 256 MiB of HBM per device.

```python
import jax
import jax.numpy as jnp
from jax import lax

CX = 256
STEPS = 2
SWEEPS = 16
HID = 64
NOUT = 6
TRAJ = 2
NX = 1024
NY = 512
N_GX = 4


def shard_levels(key, dims, cuts, smallest, largest):
    loudness = 1.0
    for position, parts in cuts:
        heights = jax.random.uniform(jax.random.fold_in(jax.random.fold_in(key, 6), position), (parts,), jnp.float32, smallest / len(cuts), largest / len(cuts))
        loudness = loudness * jnp.repeat(jnp.exp(heights), dims[position] // parts).reshape((-1,) + (1,) * (len(dims) - 1 - position))
    return loudness


def centred(rng, extent, scale, most, shards=(), kind=jnp.bfloat16):
    drawn = scale * jax.random.normal(rng, extent, jnp.float32)
    if shards:
        drawn = drawn * shard_levels(rng, extent, shards, -0.22, 0.18)
    return jnp.clip(drawn, -most, most).astype(kind)


def setup_inputs(seed: int = 0) -> dict:
    seeds = jax.random.split(jax.random.key(seed), 8)
    return {
        "velocity": centred(seeds[0], (TRAJ, 2, NX, NY), 1.0, 6.0, ((0, 2), (2, 4), (3, 4)), jnp.float32),
        "targets": centred(seeds[1], (TRAJ, STEPS, 2, NX, NY), 1.0, 6.0, ((0, 2), (3, 4), (4, 4)), jnp.float32),
        "weight_one": centred(seeds[2], (3, 3, 2, HID), 18 ** -0.5, 1.5),
        "bias_one": centred(seeds[3], (HID,), 0.5, 3.0, (), jnp.float32),
        "weight_two": centred(seeds[4], (HID, HID), HID ** -0.5, 0.75),
        "bias_two": centred(seeds[5], (HID,), 0.5, 3.0, (), jnp.float32),
        "weight_three": centred(seeds[6], (3, 3, HID, NOUT), (9 * HID) ** -0.5, 0.25),
    }


TIME_STEP = 0.2
VISCOSITY = 0.05
DRAG_RATE = 0.1
FORCE_WAVES = 4.0
COEF_SCALE = 0.1
EPSILON = 1e-06
RIM_WIDTH = 4
OUTER_WEIGHT = -1.0 / 16.0
INNER_WEIGHT = 9.0 / 16.0
TWO_PI = 6.283185307179586

def product(pattern, left_side, right_side):
    return jnp.einsum(pattern, left_side.astype(jnp.float32), right_side.astype(jnp.float32), precision=lax.Precision.HIGHEST)

def silu_slope(values):
    logistic = jax.nn.sigmoid(values)
    return logistic * (1.0 + values * (1.0 - logistic))

def shifted_stack(source, span_rows, span_cols):
    pieces = []
    for offset_row in range(3):
        for offset_col in range(3):
            pieces.append(source[:, offset_row:offset_row + span_rows, offset_col:offset_col + span_cols])
    return jnp.concatenate(pieces, axis=0)

def network(padded, weight_one, bias_one, weight_two, bias_two, weight_three):
    span_rows = padded.shape[1] - 2
    span_cols = padded.shape[2] - 2
    columns = shifted_stack(padded.astype(jnp.bfloat16), span_rows, span_cols)
    kernel_one = weight_one.reshape(-1, weight_one.shape[3])
    pre_one = product('kh,kxy->hxy', kernel_one, columns) + bias_one[:, None, None]
    hidden_one = jax.nn.silu(pre_one).astype(jnp.bfloat16)
    pre_two = product('hg,hxy->gxy', weight_two, hidden_one) + bias_two[:, None, None]
    hidden_two = jax.nn.silu(pre_two).astype(jnp.bfloat16)
    kernel_three = weight_three.reshape(9, weight_three.shape[2], weight_three.shape[3])
    tap_terms = product('khn,hxy->knxy', kernel_three, hidden_two)
    summed = tap_terms[0, :, 0:span_rows - 2, 0:span_cols - 2]
    for tap_index in range(1, 9):
        offset_row = tap_index // 3
        offset_col = tap_index % 3
        summed = summed + tap_terms[tap_index, :, offset_row:offset_row + span_rows - 2, offset_col:offset_col + span_cols - 2]
    coefficients = COEF_SCALE * summed
    return (columns, kernel_one, pre_one, hidden_one, pre_two, hidden_two, kernel_three, coefficients)

def network_backward(saved_values, weight_two, grad_coef):
    columns, kernel_one, pre_one, hidden_one, pre_two, hidden_two, kernel_three, coefficients = saved_values
    grad_taps = (COEF_SCALE * grad_coef).astype(jnp.bfloat16)
    span_rows = hidden_two.shape[1]
    span_cols = hidden_two.shape[2]
    inner_rows = span_rows - 2
    inner_cols = span_cols - 2
    padded_taps = jnp.pad(grad_taps, ((0, 0), (2, 2), (2, 2)))
    three_parts = []
    spread = []
    for tap_index in range(9):
        offset_row = tap_index // 3
        offset_col = tap_index % 3
        window = hidden_two[:, offset_row:offset_row + inner_rows, offset_col:offset_col + inner_cols]
        three_parts.append(product('hxy,nxy->hn', window, grad_taps))
        spread.append(padded_taps[:, 2 - offset_row:2 - offset_row + span_rows, 2 - offset_col:2 - offset_col + span_cols])
    grad_three = jnp.stack(three_parts).reshape(3, 3, hidden_two.shape[0], grad_taps.shape[0])
    spread_taps = jnp.stack(spread)
    grad_hidden_two = product('khn,knxy->hxy', kernel_three, spread_taps)
    grad_pre_two = (grad_hidden_two * silu_slope(pre_two)).astype(jnp.bfloat16)
    grad_two = product('hxy,gxy->hg', hidden_one, grad_pre_two)
    grad_bias_two = lax.optimization_barrier(jnp.sum(grad_pre_two.astype(jnp.float32), axis=(1, 2)))
    grad_hidden_one = product('hg,gxy->hxy', weight_two, grad_pre_two)
    grad_pre_one = (grad_hidden_one * silu_slope(pre_one)).astype(jnp.bfloat16)
    channels = columns.shape[0] // 9
    grad_one = product('kxy,hxy->kh', columns, grad_pre_one).reshape(3, 3, channels, grad_pre_one.shape[0])
    grad_bias_one = lax.optimization_barrier(jnp.sum(grad_pre_one.astype(jnp.float32), axis=(1, 2)))
    grad_columns = product('kh,hxy->kxy', kernel_one, grad_pre_one)
    grad_input = jnp.zeros((channels, span_rows + 2, span_cols + 2), jnp.float32)
    for tap_index in range(9):
        offset_row = tap_index // 3
        offset_col = tap_index % 3
        grad_input = grad_input.at[:, offset_row:offset_row + span_rows, offset_col:offset_col + span_cols].add(grad_columns[tap_index * channels:(tap_index + 1) * channels])
    return (grad_input, (grad_one, grad_bias_one, grad_two, grad_bias_two, grad_three))

def advect(padded, coefficients, forcing):
    current = padded[:, 1:-1, 1:-1]
    span_rows = current.shape[1] - 6
    span_cols = current.shape[2] - 6
    across = current[:, :, 2:span_cols + 4]
    cell_one = across[:, 0:span_rows + 3]
    cell_two = across[:, 1:span_rows + 4]
    cell_three = across[:, 2:span_rows + 5]
    cell_four = across[:, 3:span_rows + 6]
    adjust_one = coefficients[0, 0:span_rows + 3, 1:span_cols + 3]
    adjust_two = coefficients[1, 0:span_rows + 3, 1:span_cols + 3]
    adjust_three = coefficients[2, 0:span_rows + 3, 1:span_cols + 3]
    face_value = (OUTER_WEIGHT + adjust_one) * cell_one + (INNER_WEIGHT + adjust_two) * cell_two + (INNER_WEIGHT + adjust_three) * cell_three + (OUTER_WEIGHT - adjust_one - adjust_two - adjust_three) * cell_four
    face_speed = 0.5 * (cell_two[0] + cell_three[0])
    flux_rows = face_speed * face_value
    change = flux_rows[:, 1:] - flux_rows[:, :-1]
    along_cols = current[:, 2:span_rows + 4, :]
    cell_one = along_cols[:, :, 0:span_cols + 3]
    cell_two = along_cols[:, :, 1:span_cols + 4]
    cell_three = along_cols[:, :, 2:span_cols + 5]
    cell_four = along_cols[:, :, 3:span_cols + 6]
    adjust_one = coefficients[3, 1:span_rows + 3, 0:span_cols + 3]
    adjust_two = coefficients[4, 1:span_rows + 3, 0:span_cols + 3]
    adjust_three = coefficients[5, 1:span_rows + 3, 0:span_cols + 3]
    face_value = (OUTER_WEIGHT + adjust_one) * cell_one + (INNER_WEIGHT + adjust_two) * cell_two + (INNER_WEIGHT + adjust_three) * cell_three + (OUTER_WEIGHT - adjust_one - adjust_two - adjust_three) * cell_four
    face_speed = 0.5 * (cell_two[1] + cell_three[1])
    flux_cols = face_speed * face_value
    change = change + (flux_cols[:, :, 1:] - flux_cols[:, :, :-1])
    center = current[:, 2:span_rows + 4, 2:span_cols + 4]
    laplace = current[:, 1:span_rows + 3, 2:span_cols + 4] + current[:, 3:span_rows + 5, 2:span_cols + 4] + current[:, 2:span_rows + 4, 1:span_cols + 3] + current[:, 2:span_rows + 4, 3:span_cols + 5] - 4.0 * center
    return center - TIME_STEP * change + TIME_STEP * (VISCOSITY * laplace - DRAG_RATE * center + forcing)

def roll_neighbours(field_in):
    return jnp.roll(field_in, -1, 1) + jnp.roll(field_in, 1, 1) + jnp.roll(field_in, -1, 2) + jnp.roll(field_in, 1, 2)

def roll_divergence(velocity_field):
    return 0.5 * (jnp.roll(velocity_field[0:1], -1, 1) - jnp.roll(velocity_field[0:1], 1, 1) + jnp.roll(velocity_field[1:2], -1, 2) - jnp.roll(velocity_field[1:2], 1, 2))

def roll_push(pressure):
    return jnp.concatenate([0.5 * (jnp.roll(pressure, -1, 1) - jnp.roll(pressure, 1, 1)), 0.5 * (jnp.roll(pressure, -1, 2) - jnp.roll(pressure, 1, 2))], axis=0)

def wrap_pad(current):
    return jnp.pad(current, ((0, 0), (RIM_WIDTH, RIM_WIDTH), (RIM_WIDTH, RIM_WIDTH)), mode='wrap')

def forward_step(current, weights, forcing):
    padded = wrap_pad(current)

    def one_block(block_index):
        row_block = lax.dynamic_slice_in_dim(padded, block_index * CX, CX + 2 * RIM_WIDTH, 1)
        saved_values = network(row_block, weights[0], weights[1], weights[2], weights[3], weights[4])
        return advect(row_block, saved_values[-1], forcing)[:, 1:-1, 1:-1]
    blocks = lax.map(one_block, jnp.arange(N_GX, dtype=jnp.int32))
    provisional = jnp.transpose(blocks, (1, 0, 2, 3)).reshape(2, NX, NY)
    divergence_field = roll_divergence(provisional)

    def one_sweep(sweep_index, pressure):
        return 0.25 * roll_neighbours(pressure) - 0.25 * divergence_field
    pressure = lax.fori_loop(0, SWEEPS, one_sweep, -0.25 * divergence_field)
    return provisional - roll_push(pressure)

def fold_wrap(grad_padded):
    middle = grad_padded[:, :, RIM_WIDTH:-RIM_WIDTH]
    middle = middle.at[:, :, :RIM_WIDTH].add(grad_padded[:, :, -RIM_WIDTH:])
    middle = middle.at[:, :, -RIM_WIDTH:].add(grad_padded[:, :, :RIM_WIDTH])
    result = middle[:, RIM_WIDTH:-RIM_WIDTH, :]
    result = result.at[:, :RIM_WIDTH, :].add(middle[:, -RIM_WIDTH:, :])
    result = result.at[:, -RIM_WIDTH:, :].add(middle[:, :RIM_WIDTH, :])
    return result

def backward_step(current, weights, forcing, grad_state):
    grad_pressure = roll_divergence(grad_state)

    def one_sweep(sweep_index, carried):
        cotangent, grad_div = carried
        grad_div = grad_div - 0.25 * cotangent
        return (0.25 * roll_neighbours(cotangent), grad_div)
    cotangent, grad_div = lax.fori_loop(0, SWEEPS, one_sweep, (grad_pressure, jnp.zeros_like(grad_pressure)))
    grad_div = grad_div - 0.25 * cotangent
    unused, divergence_pull = jax.vjp(roll_divergence, grad_state)
    grad_provisional = divergence_pull(grad_div)[0] + grad_state
    padded = wrap_pad(current)
    zero_grads = (jnp.zeros(weights[0].shape, jnp.float32), jnp.zeros(weights[1].shape, jnp.float32), jnp.zeros(weights[2].shape, jnp.float32), jnp.zeros(weights[3].shape, jnp.float32), jnp.zeros(weights[4].shape, jnp.float32))

    def one_block(carried, block_index):
        grad_padded, grad_sums = carried
        start_row = block_index * CX
        row_block = lax.dynamic_slice_in_dim(padded, start_row, CX + 2 * RIM_WIDTH, 1)
        grad_ext = jnp.pad(lax.dynamic_slice_in_dim(grad_provisional, start_row, CX, 1), ((0, 0), (1, 1), (1, 1)))
        saved_values = network(row_block, weights[0], weights[1], weights[2], weights[3], weights[4])

        def advect_inputs(padded_in, coef_in):
            return advect(padded_in, coef_in, forcing)
        unused_out, advect_pull = jax.vjp(advect_inputs, row_block, saved_values[-1])
        grad_rows, grad_coef = advect_pull(grad_ext)
        grad_input, step_grads = network_backward(saved_values, weights[2], grad_coef)
        grad_rows = grad_rows + grad_input
        present = lax.dynamic_slice_in_dim(grad_padded, start_row, CX + 2 * RIM_WIDTH, 1)
        grad_padded = lax.dynamic_update_slice_in_dim(grad_padded, present + grad_rows, start_row, 1)
        grad_sums = jax.tree.map(jnp.add, grad_sums, step_grads)
        return ((grad_padded, grad_sums), None)
    zero_padded = jnp.zeros((2, NX + 2 * RIM_WIDTH, NY + 2 * RIM_WIDTH), jnp.float32)
    (grad_padded, grad_sums), unused_stack = lax.scan(one_block, (zero_padded, zero_grads), jnp.arange(N_GX, dtype=jnp.int32))
    return (fold_wrap(grad_padded), grad_sums)

def normalize(flat_grads, lengths):
    pieces = []
    offset = 0
    for length in lengths:
        segment = flat_grads[offset:offset + length]
        pieces.append(segment * (1.0 / jnp.sqrt(jnp.mean(jnp.square(segment)) + EPSILON)))
        offset += length
    return pieces

def reference(velocity, targets, weight_one, bias_one, weight_two, bias_two, weight_three):
    weights = (weight_one, bias_one, weight_two, bias_two, weight_three)
    col_ids = jnp.arange(NY + 2, dtype=jnp.int32) - 1
    phase_angle = col_ids.astype(jnp.float32) * (TWO_PI * FORCE_WAVES / NY)
    force_row = jnp.broadcast_to(jnp.sin(phase_angle)[None, :], (CX + 2, NY + 2))
    forcing = jnp.stack([force_row, jnp.zeros_like(force_row)])
    grad_totals = None
    loss_total = jnp.zeros((), jnp.float32)
    start_grads = []
    for member in range(TRAJ):
        current = velocity[member]
        history = [current]
        for step_index in range(STEPS):
            current = forward_step(current, weights, forcing)
            history.append(current)
            loss_total = loss_total + 0.5 * jnp.sum(jnp.square(current - targets[member, step_index]))
        grad_state = jnp.zeros_like(current)
        for step_index in range(STEPS - 1, -1, -1):
            grad_state = grad_state + (history[step_index + 1] - targets[member, step_index])
            grad_state, step_grads = backward_step(history[step_index], weights, forcing, grad_state)
            if grad_totals is None:
                grad_totals = step_grads
            else:
                grad_totals = jax.tree.map(jnp.add, grad_totals, step_grads)
        start_grads.append(grad_state)
    lengths = [int(tensor.size) for tensor in grad_totals]
    flat_grads = jnp.concatenate([tensor.reshape(-1) for tensor in grad_totals])
    pieces = normalize(flat_grads, lengths)
    outputs = [piece.reshape(tensor.shape) for piece, tensor in zip(pieces, grad_totals)]
    mean_loss = loss_total / float(TRAJ * STEPS * 2 * NX * NY)
    grad_velocity = jnp.stack(start_grads)
    return (outputs[0], outputs[1], outputs[2], outputs[3], outputs[4], mean_loss, grad_velocity)
```

```python
import functools

import jax
import jax.numpy as jnp
import numpy as np
from jax import lax
from jax.experimental import pallas as pl
from jax.experimental.pallas import tpu as pltpu
from jax.sharding import PartitionSpec as P

SWEEPS = 16
TIME_STEP = 0.2
VISCOSITY = 0.05
DRAG_RATE = 0.1
FORCE_WAVES = 4.0
COEF_SCALE = 0.1
EPSILON = 1e-06
OUTER_WEIGHT = -1.0 / 16.0
INNER_WEIGHT = 9.0 / 16.0
TWO_PI = 6.283185307179586

TOP = 40
LEFT = 64
CHUNK_ROWS = 16
LEAD = 384
BF16 = jnp.bfloat16
F32 = jnp.float32


def passed_along(block, axis, distance):
    size = lax.axis_size(axis)
    route = [(i, (i + distance) % size) for i in range(size)]
    return lax.ppermute(block, axis, route)


def exchange(own, rim):
    before = passed_along(own[:, -rim:], "gx", 1)
    after = passed_along(own[:, :rim], "gx", -1)
    tall = jnp.concatenate([before, own, after], axis=1)
    left = passed_along(jnp.swapaxes(tall[:, :, -rim:], 1, 2), "gy", 1)
    right = passed_along(jnp.swapaxes(tall[:, :, :rim], 1, 2), "gy", -1)
    wide = jnp.concatenate([jnp.swapaxes(left, 1, 2), tall, jnp.swapaxes(right, 1, 2)], axis=2)
    return jnp.pad(wide, ((0, 0), (TOP - rim, TOP - rim), (LEFT - rim, LEFT - rim)))


def total_over(value, axis):
    size = lax.axis_size(axis)
    if size <= 4:
        moved = [passed_along(value, axis, distance) for distance in range(1, size)]
        for other in moved:
            value = value + other
        return value
    return lax.psum(value, axis)


def at(field, rows, cols):
    if rows:
        field = pltpu.roll(field, (-rows) % field.shape[0], 0)
    if cols:
        field = pltpu.roll(field, (-cols) % field.shape[1], 1)
    return field


def project(first, second, work_ref, rhs_ref):
    quarter = -0.125 * (at(first, 1, 0) - at(first, -1, 0) + at(second, 0, 1) - at(second, 0, -1))
    rhs_ref[...] = quarter
    work_ref[...] = quarter

    def sweep(index, carried):
        p = work_ref[...]
        near = at(p, 1, 0) + at(p, -1, 0) + at(p, 0, 1) + at(p, 0, -1)
        work_ref[...] = 0.25 * near + rhs_ref[...]
        return carried

    lax.fori_loop(0, SWEEPS, sweep, 0)
    p = work_ref[...]
    return (
        first - 0.5 * (at(p, 1, 0) - at(p, -1, 0)),
        second - 0.5 * (at(p, 0, 1) - at(p, 0, -1)),
    )


def project_kernel(in_ref, out_ref, work_ref, rhs_ref):
    first, second = project(in_ref[0], in_ref[1], work_ref, rhs_ref)
    out_ref[0] = first
    out_ref[1] = second


def last_kernel(rows, cols, in_ref, goal_ref, out_ref, loss_ref, work_ref, rhs_ref):
    first, second = project(in_ref[0], in_ref[1], work_ref, rhs_ref)
    first = first - goal_ref[0]
    second = second - goal_ref[1]
    row = lax.broadcasted_iota(jnp.int32, first.shape, 0)
    col = lax.broadcasted_iota(jnp.int32, first.shape, 1)
    own = (row >= TOP) & (row < TOP + rows) & (col >= LEFT) & (col < LEFT + cols)
    square = jnp.where(own, first * first + second * second, 0.0)
    loss_ref[...] = jnp.sum(square, axis=0, keepdims=True)
    out_ref[0] = first
    out_ref[1] = second
    first, second = project(out_ref[0], out_ref[1], work_ref, rhs_ref)
    out_ref[0] = first
    out_ref[1] = second


def faces(field, c0, c1, c2, move):
    return (
        (OUTER_WEIGHT + c0) * move(field, -1)
        + (INNER_WEIGHT + c1) * field
        + (INNER_WEIGHT + c2) * move(field, 1)
        + (OUTER_WEIGHT - c0 - c1 - c2) * move(field, 2)
    )


def by_row(field, distance):
    return at(field, distance, 0)


def by_col(field, distance):
    return at(field, 0, distance)


def advect_kernel(v_ref, c_ref, force_ref, out_ref):
    speed_rows = 0.5 * (v_ref[0] + by_row(v_ref[0], 1))
    speed_cols = 0.5 * (v_ref[1] + by_col(v_ref[1], 1))
    for comp in range(2):
        q = v_ref[comp]
        flux = speed_rows * faces(q, c_ref[0], c_ref[1], c_ref[2], by_row)
        change = flux - by_row(flux, -1)
        flux = speed_cols * faces(q, c_ref[3], c_ref[4], c_ref[5], by_col)
        change = change + (flux - by_col(flux, -1))
        laplace = by_row(q, 1) + by_row(q, -1) + by_col(q, 1) + by_col(q, -1) - 4.0 * q
        drive = VISCOSITY * laplace - DRAG_RATE * q
        if comp == 0:
            drive = drive + force_ref[...]
        out_ref[comp] = q - TIME_STEP * change + TIME_STEP * drive


def advect_back_kernel(v_ref, c_ref, g_ref, taps_ref, out_ref):
    for axis in range(2):
        move = by_row if axis == 0 else by_col
        speed = 0.5 * (v_ref[axis] + move(v_ref[axis], 1))
        c0 = c_ref[3 * axis]
        c1 = c_ref[3 * axis + 1]
        c2 = c_ref[3 * axis + 2]
        grads = []
        grad_speed = None
        taps = None
        for comp in range(2):
            q = v_ref[comp]
            g = g_ref[comp]
            grad_flux = TIME_STEP * (move(g, 1) - g)
            term = grad_flux * faces(q, c0, c1, c2, move)
            grad_speed = term if grad_speed is None else grad_speed + term
            grad_face = grad_flux * speed
            behind = move(q, -1)
            ahead = move(q, 1)
            far = move(q, 2)
            new = (grad_face * (behind - far), grad_face * (q - far), grad_face * (ahead - far))
            taps = new if taps is None else tuple(a + b for a, b in zip(taps, new))
            grads.append(
                move(grad_face * (OUTER_WEIGHT + c0), 1)
                + grad_face * (INNER_WEIGHT + c1)
                + move(grad_face * (INNER_WEIGHT + c2), -1)
                + move(grad_face * (OUTER_WEIGHT - c0 - c1 - c2), -2)
            )
        grads[axis] = grads[axis] + 0.5 * (grad_speed + move(grad_speed, -1))
        for number in range(3):
            taps_ref[3 * axis + number] = COEF_SCALE * taps[number]
        for comp in range(2):
            if axis == 0:
                out_ref[comp] = grads[comp]
            else:
                g = g_ref[comp]
                near = by_row(g, 1) + by_row(g, -1) + by_col(g, 1) + by_col(g, -1) - 4.0 * g
                out_ref[comp] = (
                    out_ref[comp]
                    + grads[comp]
                    + g
                    + TIME_STEP * (VISCOSITY * near - DRAG_RATE * g)
                )


def tap_offsets(wide):
    return [row * wide + col for row in range(3) for col in range(3)]


def shifted(block, offset, length):
    if offset:
        block = pltpu.roll(block, block.shape[1] - offset, 1)
    return block[:, :length]


def gather_columns(x_ref, cols_ref, start, chunk, offsets):
    window = x_ref[:, pl.ds(start, chunk + LEAD)]
    for tap, offset in enumerate(offsets):
        cols_ref[2 * tap : 2 * tap + 2, :] = shifted(window, offset, chunk)[:2]


def product(left, right):
    return lax.dot_general(left, right, (((1,), (0,)), ((), ())), preferred_element_type=F32)


def product_over_cells(left, right):
    return lax.dot_general(left, right, (((1,), (1,)), ((), ())), preferred_element_type=F32)


def network_kernel(chunk, offsets, x_ref, w1_ref, b1_ref, w2_ref, b2_ref, w3_ref, out_ref, cols_ref, terms_ref):
    step = pl.program_id(0)
    start = pl.multiple_of(step * chunk, 128)

    @pl.when(step == 0)
    def _():
        cols_ref[...] = jnp.zeros_like(cols_ref)
        terms_ref[...] = jnp.zeros_like(terms_ref)

    gather_columns(x_ref, cols_ref, start, chunk, offsets)
    half = product(w1_ref[...], cols_ref[...].astype(BF16)) + b1_ref[...]
    hidden = (half * jnp.tanh(half) + half).astype(BF16)
    half = product(w2_ref[...], hidden) + b2_ref[...]
    hidden = (half * jnp.tanh(half) + half).astype(BF16)
    terms_ref[:, :LEAD] = terms_ref[:, chunk:]
    terms_ref[:, LEAD:] = product(w3_ref[...], hidden)
    total = None
    for tap, offset in enumerate(offsets):
        term = shifted(terms_ref[8 * tap : 8 * tap + 8, :], offset, chunk)
        total = term if total is None else total + term
    out_ref[...] = COEF_SCALE * total


def network_back_kernel(
    chunk, offsets, x_ref, taps_ref, own_ref, w1_ref, b1_ref, w2_ref, b2_ref, w1b_ref, w2b_ref, w3b_ref,
    out_ref, d1_ref, d2_ref, d3_ref, cols_ref, spread_ref, terms_ref,
):
    step = pl.program_id(0)
    start = pl.multiple_of(step * chunk, 128)

    @pl.when(step == 0)
    def _():
        cols_ref[...] = jnp.zeros_like(cols_ref)
        spread_ref[...] = jnp.zeros_like(spread_ref)
        terms_ref[...] = jnp.zeros_like(terms_ref)
        d1_ref[...] = jnp.zeros_like(d1_ref)
        d2_ref[...] = jnp.zeros_like(d2_ref)
        d3_ref[...] = jnp.zeros_like(d3_ref)

    own = own_ref[:, pl.ds(start, chunk)]
    gather_columns(x_ref, cols_ref, start, chunk, offsets)
    cols_ref[18:19, :] = jnp.ones((1, chunk), F32)
    window = taps_ref[:, pl.ds(start, chunk + LEAD)]
    for tap, offset in enumerate(offsets):
        spread_ref[8 * tap : 8 * tap + 8, :] = shifted(window, LEAD - offset, chunk)
    cols = cols_ref[...]
    half = product(w1_ref[...], cols.astype(BF16)) + b1_ref[...]
    bend = jnp.tanh(half)
    hidden_one = (half * bend + half).astype(BF16)
    slope_one = (0.5 + 0.5 * bend) * (1.0 + half * (1.0 - bend))
    half = product(w2_ref[...], hidden_one) + b2_ref[...]
    bend = jnp.tanh(half)
    hidden_two = (half * bend + half).astype(BF16)
    slope_two = (0.5 + 0.5 * bend) * (1.0 + half * (1.0 - bend))
    spread = spread_ref[...].astype(BF16)
    grad_two = (product(w3b_ref[...], spread) * slope_two).astype(BF16)
    grad_one = (product(w2b_ref[...], grad_two) * slope_one).astype(BF16)
    mask = own.astype(BF16)
    d3_ref[...] += product_over_cells(spread, hidden_two * mask)
    d2_ref[...] += product_over_cells(hidden_one, grad_two * mask)
    d1_ref[...] += product_over_cells((cols * own).astype(BF16), jnp.concatenate([grad_one, grad_two], axis=0))
    terms_ref[:, :LEAD] = terms_ref[:, chunk:]
    terms_ref[:, LEAD:] = product(w1b_ref[...], grad_one)
    total = None
    for tap, offset in enumerate(offsets):
        term = shifted(terms_ref[8 * tap : 8 * tap + 8, :], LEAD - offset, chunk)
        total = term if total is None else total + term
    out_ref[...] = total


def whole(shape):
    return pl.BlockSpec(shape, lambda *step: (0,) * len(shape))


def shards(velocity, targets, weight_one, bias_one, weight_two, bias_two, weight_three):
    rows, cols = velocity.shape[2], velocity.shape[3]
    step_count = targets.shape[1]
    frame = (rows + 2 * TOP, cols + 2 * LEFT)
    wide = cols + 8
    chunk = CHUNK_ROWS * wide
    chunks = -(-(rows + 8) // CHUNK_ROWS)
    length = chunks * chunk
    offsets = tap_offsets(wide)
    hid = weight_two.shape[0]
    nout = weight_three.shape[3]
    params = pltpu.CompilerParams(vmem_limit_bytes=56 << 20)

    def grid_call(kernel, outs, *args, scratch=()):
        return pl.pallas_call(
            kernel,
            out_shape=[jax.ShapeDtypeStruct(shape, F32) for shape in outs],
            scratch_shapes=[pltpu.VMEM(shape, F32) for shape in scratch],
            compiler_params=params,
        )(*args)

    w1 = weight_one.reshape(18, hid)
    w1_half = jnp.pad((0.5 * w1.astype(F32)).astype(BF16).T, ((0, 0), (0, 14)))
    w2_half = (0.5 * weight_two.astype(F32)).astype(BF16).T
    b1_half = 0.5 * bias_one[:, None]
    b2_half = 0.5 * bias_two[:, None]
    w3 = jnp.pad(weight_three.reshape(9, hid, nout), ((0, 0), (0, 0), (0, 8 - nout)))
    w3_out = jnp.transpose(w3, (0, 2, 1)).reshape(72, hid)
    w3_back = jnp.pad(jnp.transpose(w3, (1, 0, 2)).reshape(hid, 72), ((0, 0), (0, 8)))
    w1_back = jnp.pad(weight_one.reshape(9, 2, hid), ((0, 0), (0, 6), (0, 0))).reshape(72, hid)

    place = np.arange(length)
    place_row, place_col = place // wide, place % wide
    own_cells = (place_row >= 3) & (place_row < 3 + rows) & (place_col >= 3) & (place_col < 3 + cols)
    own_row = jnp.asarray(own_cells[None, :], F32)

    total_cols = cols * lax.axis_size("gy")
    col_ids = lax.axis_index("gy") * cols + jnp.arange(frame[1], dtype=jnp.int32) - LEFT
    forcing = jnp.sin(col_ids.astype(F32) * (TWO_PI * FORCE_WAVES / total_cols))[None, :]

    def flat_velocity(v):
        cells = v[:, TOP - 4 : TOP + rows + 4, LEFT - 4 : LEFT + cols + 4]
        cells = cells.astype(BF16).astype(F32).reshape(2, (rows + 8) * wide)
        return jnp.pad(cells, ((0, 0), (0, length + LEAD - (rows + 8) * wide)))

    def network(x):
        flat = pl.pallas_call(
            functools.partial(network_kernel, chunk, offsets),
            grid=(chunks,),
            in_specs=[
                whole((2, length + LEAD)),
                whole((hid, 32)),
                whole((hid, 1)),
                whole((hid, hid)),
                whole((hid, 1)),
                whole((72, hid)),
            ],
            out_specs=pl.BlockSpec((8, chunk), lambda step: (0, step)),
            out_shape=jax.ShapeDtypeStruct((8, length), F32),
            scratch_shapes=[pltpu.VMEM((32, chunk), F32), pltpu.VMEM((72, chunk + LEAD), F32)],
            compiler_params=params,
        )(x, w1_half, b1_half, w2_half, b2_half, w3_out)
        used = rows + 4
        cells = flat[:nout, LEAD : LEAD + used * wide].reshape(nout, used, wide)
        return jnp.pad(cells, ((0, 0), (TOP - 2, frame[0] - (TOP - 2) - used), (LEFT - 2, frame[1] - (LEFT - 2) - wide)))

    def network_back(x, taps):
        used = rows + 4
        cells = taps[:, TOP - 2 : TOP - 2 + used, LEFT - 2 : LEFT - 2 + wide].astype(BF16).astype(F32)
        cells = cells.reshape(nout, used * wide)
        cells = jnp.pad(cells, ((0, 8 - nout), (LEAD, length - used * wide)))
        flat, d1, d2, d3 = pl.pallas_call(
            functools.partial(network_back_kernel, chunk, offsets),
            grid=(chunks,),
            in_specs=[
                whole((2, length + LEAD)),
                whole((8, length + LEAD)),
                whole((1, length)),
                whole((hid, 32)),
                whole((hid, 1)),
                whole((hid, hid)),
                whole((hid, 1)),
                whole((72, hid)),
                whole((hid, hid)),
                whole((hid, 80)),
            ],
            out_specs=[
                pl.BlockSpec((8, chunk), lambda step: (0, step)),
                whole((32, 2 * hid)),
                whole((hid, hid)),
                whole((80, hid)),
            ],
            out_shape=[
                jax.ShapeDtypeStruct((8, length), F32),
                jax.ShapeDtypeStruct((32, 2 * hid), F32),
                jax.ShapeDtypeStruct((hid, hid), F32),
                jax.ShapeDtypeStruct((80, hid), F32),
            ],
            scratch_shapes=[
                pltpu.VMEM((32, chunk), F32),
                pltpu.VMEM((80, chunk), F32),
                pltpu.VMEM((72, chunk + LEAD), F32),
            ],
            compiler_params=params,
        )(x, cells, own_row, w1_half, b1_half, w2_half, b2_half, w1_back, weight_two, w3_back)
        grad_in = flat[:2, : (rows + 8) * wide].reshape(2, rows + 8, wide)[:, 4 : 4 + rows, 4 : 4 + cols]
        grad_three = d3[:72].reshape(9, 8, hid)[:, :nout].transpose(0, 2, 1)
        pieces = [d1[:18, :hid], d1[18, :hid], d2, d1[18, hid:], grad_three]
        return grad_in, jnp.concatenate([piece.reshape(-1) for piece in pieces])

    def own(framed):
        return framed[:, TOP : TOP + rows, LEFT : LEFT + cols]

    pair = (2,) + frame
    first = exchange(jnp.concatenate([velocity[0], targets[0, step_count - 1]], axis=0), 24)
    current = first[:2]
    last_goal = first[2:]
    loss = jnp.zeros((), F32)
    kept = []
    errors = []
    for step_index in range(step_count):
        x = flat_velocity(current)
        coefs = network(x)
        (provisional,) = grid_call(advect_kernel, [pair], current, coefs, forcing)
        kept.append((current, x, coefs))
        if step_index < step_count - 1:
            framed = exchange(own(provisional), 24)
            (current,) = grid_call(project_kernel, [pair], framed, scratch=[frame, frame])
            error = own(current) - targets[0, step_index]
            errors.append(error)
            loss = loss + jnp.sum(jnp.square(error))
        else:
            framed = exchange(own(provisional), 40)
            grad, squares = grid_call(
                functools.partial(last_kernel, rows, cols), [pair, (1, frame[1])], framed, last_goal,
                scratch=[frame, frame],
            )
            loss = loss + jnp.sum(squares)
    sums = None
    for step_index in range(step_count - 1, -1, -1):
        if step_index < step_count - 1:
            framed = exchange(grad_own + errors[step_index], 24)
            (grad,) = grid_call(project_kernel, [pair], framed, scratch=[frame, frame])
        current, x, coefs = kept[step_index]
        taps, moved = grid_call(advect_back_kernel, [(nout,) + frame, pair], current, coefs, grad)
        grad_in, step_sums = network_back(x, taps)
        grad_own = own(moved) + grad_in
        sums = step_sums if sums is None else sums + step_sums

    flat_sums = jnp.concatenate([sums, 0.5 * loss[None]])
    count = flat_sums.shape[0]
    tall = -(-count // 1024) * 8
    flat_sums = jnp.pad(flat_sums, (0, tall * 128 - count)).reshape(tall, 128)
    for axis in ("ens", "gx", "gy"):
        flat_sums = total_over(flat_sums, axis)
    flat_sums = flat_sums.reshape(-1)
    outputs = []
    offset = 0
    for shape in (weight_one.shape, bias_one.shape, weight_two.shape, bias_two.shape, weight_three.shape):
        size = int(np.prod(shape))
        segment = flat_sums[offset : offset + size]
        scaled = segment * (1.0 / jnp.sqrt(jnp.mean(jnp.square(segment)) + EPSILON))
        outputs.append(scaled.reshape(shape))
        offset += size
    device_count = lax.axis_size(("ens", "gx", "gy"))
    mean_loss = flat_sums[offset] * (1.0 / float(step_count * 2 * rows * cols * device_count))
    return (*outputs, mean_loss, grad_own[None])


def solution(mesh):
    return jax.shard_map(
        shards,
        mesh=mesh,
        in_specs=(P("ens", None, "gx", "gy"), P("ens", None, None, "gx", "gy"), P(), P(), P(), P(), P()),
        out_specs=(P(), P(), P(), P(), P(), P(), P("ens", None, "gx", "gy")),
        check_vma=False,
    )
```

```python
import functools

import jax
import jax.numpy as jnp
import numpy as np
from jax import lax
from jax.experimental import pallas as pl
from jax.experimental.pallas import tpu as pltpu
from jax.sharding import PartitionSpec as P

SWEEPS = 16
TIME_STEP = 0.2
VISCOSITY = 0.05
DRAG_RATE = 0.1
FORCE_WAVES = 4.0
COEF_SCALE = 0.1
EPSILON = 1e-06
OUTER_WEIGHT = -1.0 / 16.0
INNER_WEIGHT = 9.0 / 16.0
TWO_PI = 6.283185307179586

TOP = 40
LEFT = 64
CHUNK_ROWS = 16
LEAD = 384
GUARD = 8
BF16 = jnp.bfloat16
F32 = jnp.float32


def passed_along(block, axis, distance):
    size = lax.axis_size(axis)
    route = [(i, (i + distance) % size) for i in range(size)]
    return lax.ppermute(block, axis, route)


def exchange(own, rim):
    before = passed_along(own[:, -rim:], "gx", 1)
    after = passed_along(own[:, :rim], "gx", -1)
    tall = jnp.concatenate([before, own, after], axis=1)
    left = passed_along(jnp.swapaxes(tall[:, :, -rim:], 1, 2), "gy", 1)
    right = passed_along(jnp.swapaxes(tall[:, :, :rim], 1, 2), "gy", -1)
    wide = jnp.concatenate([jnp.swapaxes(left, 1, 2), tall, jnp.swapaxes(right, 1, 2)], axis=2)
    return jnp.pad(wide, ((0, 0), (TOP - rim, TOP - rim), (LEFT - rim, LEFT - rim)))


def total_over(value, axis):
    size = lax.axis_size(axis)
    if size <= 4:
        moved = [passed_along(value, axis, distance) for distance in range(1, size)]
        for other in moved:
            value = value + other
        return value
    return lax.psum(value, axis)


def at(field, rows, cols):
    if rows:
        field = pltpu.roll(field, (-rows) % field.shape[0], 0)
    if cols:
        field = pltpu.roll(field, (-cols) % field.shape[1], 1)
    return field


def project(first, second, buffers, rhs_ref, rim):
    height = first.shape[0]
    quarter = -0.125 * (at(first, 1, 0) - at(first, -1, 0) + at(second, 0, 1) - at(second, 0, -1))
    for half in range(2):
        part = quarter[:, 128 * half : 128 * half + 128]
        rhs_ref[half] = part
        for buffer in range(2):
            buffers[buffer, half, :GUARD] = jnp.zeros((GUARD, 128), F32)
            buffers[buffer, half, GUARD + height :] = jnp.zeros((GUARD, 128), F32)
            buffers[buffer, half, GUARD : GUARD + height] = part
    lane = lax.broadcasted_iota(jnp.int32, (8, 128), 1)
    at_start = lane == 0
    at_end = lane == 127

    def one_sweep(source, target):
        for row in range(TOP - rim, height - TOP + rim, 8):
            here = [buffers[source, half, GUARD + row : GUARD + row + 8] for half in range(2)]
            ahead = [pltpu.roll(part, 127, 1) for part in here]
            behind = [pltpu.roll(part, 1, 1) for part in here]
            for half in range(2):
                above = buffers[source, half, GUARD + row - 1 : GUARD + row + 7]
                below = buffers[source, half, GUARD + row + 1 : GUARD + row + 9]
                east = jnp.where(at_end, ahead[1 - half], ahead[half])
                west = jnp.where(at_start, behind[1 - half], behind[half])
                near = (above + below) + (east + west)
                buffers[target, half, GUARD + row : GUARD + row + 8] = 0.25 * near + rhs_ref[half, row : row + 8]

    def two_sweeps(index, carried):
        one_sweep(0, 1)
        one_sweep(1, 0)
        return carried

    lax.fori_loop(0, SWEEPS // 2, two_sweeps, 0)
    p = jnp.concatenate([buffers[0, half, GUARD : GUARD + height] for half in range(2)], axis=1)
    above = jnp.concatenate([buffers[0, half, GUARD - 1 : GUARD - 1 + height] for half in range(2)], axis=1)
    below = jnp.concatenate([buffers[0, half, GUARD + 1 : GUARD + 1 + height] for half in range(2)], axis=1)
    return first - 0.5 * (below - above), second - 0.5 * (at(p, 0, 1) - at(p, 0, -1))


def faces(field, c0, c1, c2, move):
    return (
        (OUTER_WEIGHT + c0) * move(field, -1)
        + (INNER_WEIGHT + c1) * field
        + (INNER_WEIGHT + c2) * move(field, 1)
        + (OUTER_WEIGHT - c0 - c1 - c2) * move(field, 2)
    )


def by_row(field, distance):
    return at(field, distance, 0)


def by_col(field, distance):
    return at(field, 0, distance)


def advect(v, coefs, forcing):
    speed_rows = 0.5 * (v[0] + by_row(v[0], 1))
    speed_cols = 0.5 * (v[1] + by_col(v[1], 1))
    results = []
    for comp in range(2):
        q = v[comp]
        flux = speed_rows * faces(q, coefs[0], coefs[1], coefs[2], by_row)
        change = flux - by_row(flux, -1)
        flux = speed_cols * faces(q, coefs[3], coefs[4], coefs[5], by_col)
        change = change + (flux - by_col(flux, -1))
        laplace = by_row(q, 1) + by_row(q, -1) + by_col(q, 1) + by_col(q, -1) - 4.0 * q
        drive = VISCOSITY * laplace - DRAG_RATE * q
        if comp == 0:
            drive = drive + forcing
        results.append(q - TIME_STEP * change + TIME_STEP * drive)
    return results


def advect_back(v, coefs, g, keep_taps):
    results = [None, None]
    for axis in range(2):
        move = by_row if axis == 0 else by_col
        speed = 0.5 * (v[axis] + move(v[axis], 1))
        c0, c1, c2 = coefs[3 * axis : 3 * axis + 3]
        grads = []
        grad_speed = None
        taps = None
        for comp in range(2):
            q = v[comp]
            grad_flux = TIME_STEP * (move(g[comp], 1) - g[comp])
            term = grad_flux * faces(q, c0, c1, c2, move)
            grad_speed = term if grad_speed is None else grad_speed + term
            grad_face = grad_flux * speed
            behind = move(q, -1)
            ahead = move(q, 1)
            far = move(q, 2)
            new = (grad_face * (behind - far), grad_face * (q - far), grad_face * (ahead - far))
            taps = new if taps is None else tuple(a + b for a, b in zip(taps, new))
            grads.append(
                move(grad_face * (OUTER_WEIGHT + c0), 1)
                + grad_face * (INNER_WEIGHT + c1)
                + move(grad_face * (INNER_WEIGHT + c2), -1)
                + move(grad_face * (OUTER_WEIGHT - c0 - c1 - c2), -2)
            )
        grads[axis] = grads[axis] + 0.5 * (grad_speed + move(grad_speed, -1))
        for number in range(3):
            keep_taps(3 * axis + number, COEF_SCALE * taps[number])
        for comp in range(2):
            results[comp] = grads[comp] if axis == 0 else results[comp] + grads[comp]
    for comp in range(2):
        near = by_row(g[comp], 1) + by_row(g[comp], -1) + by_col(g[comp], 1) + by_col(g[comp], -1)
        drive = VISCOSITY * (near - 4.0 * g[comp]) - DRAG_RATE * g[comp]
        results[comp] = results[comp] + g[comp] + TIME_STEP * drive
    return results


class Plan:
    def __init__(self, rows, cols, rim):
        self.rows, self.cols, self.rim = rows, cols, rim
        self.wide = -(-(cols + 2 * rim + 4) // 8) * 8
        self.chunk = CHUNK_ROWS * self.wide
        self.chunks = -(-(rows + 2 * rim + 2) // CHUNK_ROWS)
        self.offsets = [row * self.wide + col for row in range(3) for col in range(3)]
        self.in_row, self.in_lane = TOP - rim - 2, LEFT - rim - 2
        self.out_row, self.out_lane = TOP - rim, LEFT - rim
        self.window = -(-(CHUNK_ROWS + 2) * self.wide // 128) * 128


def rounded(field):
    return field.astype(BF16).astype(F32)


def shifted(block, offset, length):
    if offset % block.shape[1]:
        block = pltpu.roll(block, (-offset) % block.shape[1], 1)
    return block[:, :length]


def lay_rows(source_ref, first_row, lane, wide, target_ref):
    lanes = lax.broadcasted_iota(jnp.int32, (8, 128), 1)
    tiles = {}
    for number in range(CHUNK_ROWS + 2):
        place = pl.ds(pl.multiple_of(8 * (first_row + number), 8), 8)
        block = jnp.concatenate([source_ref[half, place] for half in range(2)], axis=1)
        start = number * wide
        tile, offset = start // 128, start % 128
        block = pltpu.roll(block, (offset - lane) % 256, 1)
        for part in range(-(-(offset + wide) // 128)):
            piece = block[:, 128 * (part % 2) : 128 * (part % 2) + 128]
            if part == 0 and offset:
                piece = jnp.where(lanes < offset, tiles[tile], piece)
            tiles[tile + part] = piece
    for tile in range(target_ref.shape[1] // 128):
        target_ref[:, 128 * tile : 128 * tile + 128] = tiles[tile]


def split_rows(flat, target_ref, first_row, lane, wide):
    for number in range(CHUNK_ROWS):
        start = number * wide
        tile, offset = start // 128, start % 128
        parts = max(2, -(-(offset + wide) // 128))
        if tile + parts > flat.shape[1] // 128:
            tile, offset = tile - 1, offset + 128
        block = flat[:, 128 * tile : 128 * (tile + parts)]
        block = shifted(block, offset - lane, 256)
        place = pl.ds(pl.multiple_of(8 * (first_row + number), 8), 8)
        for half in range(2):
            target_ref[half, place] = block[:, 128 * half : 128 * half + 128]


def channel(ref, number, first_row, rows):
    place = pl.ds(8 * first_row + number, rows, stride=8)
    return jnp.concatenate([ref[half, place] for half in range(2)], axis=1)


def keep_channel(ref, number, first_row, field):
    place = pl.ds(8 * first_row + number, field.shape[0], stride=8)
    for half in range(2):
        ref[half, place] = field[:, 128 * half : 128 * half + 128]


def keep_inputs(v, inputs_ref):
    inputs_ref[...] = jnp.zeros_like(inputs_ref)
    for comp in range(2):
        field = rounded(v[comp])
        for col in range(3):
            keep_channel(inputs_ref, 2 * col + comp, 0, by_col(field, col))
    keep_channel(inputs_ref, 6, 0, jnp.ones_like(v[0]))


def product(left, right):
    return lax.dot_general(left, right, (((1,), (0,)), ((), ())), preferred_element_type=F32)


def product_over_cells(left, right):
    return lax.dot_general(left, right, (((1,), (1,)), ((), ())), preferred_element_type=F32)


def columns(plan, step, inputs_ref, window_ref):
    lay_rows(inputs_ref, plan.in_row + CHUNK_ROWS * step, plan.in_lane, plan.wide, window_ref)
    window = window_ref[...]
    parts = [shifted(window, row * plan.wide, plan.chunk) for row in range(3)]
    return jnp.concatenate(parts + [jnp.zeros((8, plan.chunk), F32)], axis=0)


def add_taps(terms_ref, offsets, length):
    total = None
    for tap, offset in enumerate(offsets):
        term = shifted(terms_ref[8 * tap : 8 * tap + 8, :], offset, length)
        total = term if total is None else total + term
    return total


def network(plan, inputs_ref, weight_refs, coefs_ref, window_ref, terms_ref):
    w1_ref, b1_ref, w2_ref, b2_ref, w3_ref = weight_refs
    terms_ref[...] = jnp.zeros_like(terms_ref)
    lag = LEAD - 2 * plan.wide

    def one_chunk(step, carried):
        cols = columns(plan, step, inputs_ref, window_ref).astype(BF16)
        half = product(w1_ref[...], cols) + b1_ref[...]
        hidden = (half * jnp.tanh(half) + half).astype(BF16)
        half = product(w2_ref[...], hidden) + b2_ref[...]
        hidden = (half * jnp.tanh(half) + half).astype(BF16)
        terms_ref[:, :LEAD] = terms_ref[:, plan.chunk :]
        terms_ref[:, LEAD:] = product(w3_ref[...], hidden)
        total = COEF_SCALE * add_taps(terms_ref, [offset + lag for offset in plan.offsets], plan.chunk)
        split_rows(total, coefs_ref, plan.out_row - 2 + CHUNK_ROWS * step, plan.out_lane, plan.wide)
        return carried

    lax.fori_loop(0, plan.chunks, one_chunk, 0)


def network_back(plan, inputs_ref, taps_ref, weight_refs, place_ref, grads_ref, sums_ref, window_ref, terms_ref):
    w1_ref, b1_ref, w2_ref, b2_ref, w1b_ref, w2b_ref, w3b_ref = weight_refs
    terms_ref[...] = jnp.zeros_like(terms_ref)

    def one_chunk(step, carried):
        row = place_ref[...] + CHUNK_ROWS * step
        own = jnp.where((row >= plan.rim + 1) & (row < plan.rim + 1 + plan.rows), 1.0, 0.0)
        mask = own.astype(BF16)
        cols = columns(plan, step, inputs_ref, window_ref)
        half = product(w1_ref[...], cols.astype(BF16)) + b1_ref[...]
        bend = jnp.tanh(half)
        hidden_one = (half * bend + half).astype(BF16)
        slope_one = (0.5 + 0.5 * bend) * (1.0 + half * (1.0 - bend))
        half = product(w2_ref[...], hidden_one) + b2_ref[...]
        bend = jnp.tanh(half)
        hidden_two = (half * bend + half).astype(BF16)
        slope_two = (0.5 + 0.5 * bend) * (1.0 + half * (1.0 - bend))
        lay_rows(taps_ref, plan.out_row - 2 + CHUNK_ROWS * step, plan.out_lane, plan.wide, window_ref)
        window = window_ref[...]
        parts = [shifted(window, 2 * plan.wide - offset, plan.chunk) for offset in plan.offsets]
        spread = jnp.concatenate(parts + [jnp.zeros((8, plan.chunk), F32)], axis=0).astype(BF16)
        grad_two = (product(w3b_ref[...], spread) * slope_two).astype(BF16)
        grad_one = (product(w2b_ref[...], grad_two) * slope_one).astype(BF16)
        sums_ref[:80, :64] += product_over_cells(spread, hidden_two * mask)
        sums_ref[:64, 64:] += product_over_cells(hidden_one, grad_two * mask)
        both = jnp.concatenate([grad_one, grad_two], axis=0)
        sums_ref[80:, :] += product_over_cells((cols * own).astype(BF16), both)
        terms_ref[:, :LEAD] = terms_ref[:, plan.chunk :]
        terms_ref[:, LEAD:] = product(w1b_ref[...], grad_one)
        total = add_taps(terms_ref, [LEAD - offset for offset in plan.offsets], plan.chunk)
        split_rows(total, grads_ref, plan.in_row + CHUNK_ROWS * step, plan.in_lane, plan.wide)
        return carried

    lax.fori_loop(0, plan.chunks, one_chunk, 0)


def own_part(field, rows, cols, first_row):
    return pltpu.roll(field[TOP - first_row : TOP - first_row + rows], 256 - LEFT, 1)[:, :cols]


def lane_sums(squares):
    return jnp.sum(squares, axis=0, keepdims=True)


def first_kernel(plan, v_ref, goal_ref, force_ref, w1, b1, w2, b2, w3, v_out, coefs_ref, error_ref, loss_ref,
                 inputs_ref, window_ref, terms_ref, frame_ref, buffers, rhs_ref):
    keep_inputs([v_ref[0], v_ref[1]], inputs_ref)
    coefs_ref[...] = jnp.zeros_like(coefs_ref)
    network(plan, inputs_ref, (w1, b1, w2, b2, w3), coefs_ref, window_ref, terms_ref)
    height = v_ref.shape[1]
    result = advect(
        [v_ref[0], v_ref[1]], [channel(coefs_ref, number, 0, height) for number in range(6)], force_ref[...]
    )
    for comp in range(2):
        frame_ref[comp] = result[comp]
    result = project(frame_ref[0], frame_ref[1], buffers, rhs_ref, 24)
    loss = None
    for comp in range(2):
        v_out[comp] = result[comp]
        error = own_part(result[comp], plan.rows, plan.cols, 0) - goal_ref[comp]
        error_ref[comp] = error
        square = lane_sums(error * error)
        loss = square if loss is None else loss + square
    loss_ref[...] = loss


def second_kernel(plan, v_ref, force_ref, w1, b1, w2, b2, w3, out_ref, coefs_ref, inputs_ref, window_ref, terms_ref):
    keep_inputs([v_ref[0], v_ref[1]], inputs_ref)
    coefs_ref[...] = jnp.zeros_like(coefs_ref)
    network(plan, inputs_ref, (w1, b1, w2, b2, w3), coefs_ref, window_ref, terms_ref)
    low, tall = TOP - 8, plan.rows + 16
    v = [v_ref[comp, low : low + tall] for comp in range(2)]
    result = advect(v, [channel(coefs_ref, number, low, tall) for number in range(6)], force_ref[...])
    for comp in range(2):
        out_ref[comp] = own_part(result[comp], plan.rows, plan.cols, low)


def back_kernel(plan, last, in_ref, goal_ref, extra_ref, before_ref, v_ref, coefs_ref, place_ref,
                w1, b1, w2, b2, w1b, w2b, w3b, out_ref, sums_ref,
                inputs_ref, taps_ref, grads_ref, window_ref, terms_ref, frame_ref, buffers, rhs_ref):
    rows, cols = plan.rows, plan.cols
    sums_ref[...] = before_ref[...]
    first, second = project(in_ref[0], in_ref[1], buffers, rhs_ref, TOP if last else 24)
    if last:
        errors = (first - goal_ref[0], second - goal_ref[1])
        for error in errors:
            mine = own_part(error, rows, cols, 0)
            sums_ref[111:112, :] += lane_sums(mine * mine)
        for comp in range(2):
            frame_ref[comp] = errors[comp]
        first, second = project(frame_ref[0], frame_ref[1], buffers, rhs_ref, 24)
    frame_ref[0] = first
    frame_ref[1] = second
    keep_inputs([v_ref[0], v_ref[1]], inputs_ref)
    taps_ref[...] = jnp.zeros_like(taps_ref)
    low, tall = TOP - 8, rows + 16
    result = advect_back(
        [v_ref[comp, low : low + tall] for comp in range(2)],
        [channel(coefs_ref, number, low, tall) for number in range(6)],
        [frame_ref[comp, low : low + tall] for comp in range(2)],
        lambda number, field: keep_channel(taps_ref, number, low, rounded(field)),
    )
    for comp in range(2):
        frame_ref[comp, low : low + tall] = result[comp]
    weight_refs = (w1, b1, w2, b2, w1b, w2b, w3b)
    network_back(plan, inputs_ref, taps_ref, weight_refs, place_ref, grads_ref, sums_ref, window_ref, terms_ref)
    for comp in range(2):
        field = frame_ref[comp, low : low + tall] + channel(grads_ref, comp, low, tall)
        total = own_part(field, rows, cols, low)
        out_ref[comp] = total + extra_ref[comp] if last else total


def scaled(piece, count):
    return piece * (1.0 / jnp.sqrt(jnp.sum(piece * piece) / count + EPSILON))


def finish_kernel(loss_scale, in_ref, w1_ref, b1_ref, w2_ref, b2_ref, w3_ref, loss_ref):
    one = jnp.concatenate([in_ref[80 + 8 * row : 86 + 8 * row, :64] for row in range(3)], axis=0)
    w1_ref[...] = scaled(one, one.size)
    b1_ref[...] = scaled(in_ref[86:87, :64], 64)
    b2_ref[...] = scaled(in_ref[86:87, 64:], 64)
    w2_ref[...] = scaled(in_ref[:64, 64:], 64 * 64)
    w3_ref[...] = scaled(in_ref[:72, :64], 54 * 64)
    loss_ref[...] = (0.5 * loss_scale) * jnp.sum(in_ref[111:112, :], axis=1, keepdims=True)


def shards(velocity, targets, weight_one, bias_one, weight_two, bias_two, weight_three):
    rows, cols = velocity.shape[2], velocity.shape[3]
    step_count = targets.shape[1]
    height = rows + 2 * TOP
    frame = (height, cols + 2 * LEFT)
    pair = (2,) + frame
    own_pair = (2, rows, cols)
    packed = (2, 8 * height, 128)
    sums_shape = (112, 128)
    hid = weight_two.shape[0]
    nout = weight_three.shape[3]
    near = Plan(rows, cols, 2)
    far = Plan(rows, cols, 23)

    def call(kernel, outs, scratch, *args):
        return pl.pallas_call(
            kernel,
            out_shape=[jax.ShapeDtypeStruct(shape, F32) for shape in outs],
            scratch_shapes=[pltpu.VMEM(shape, F32) for shape in scratch],
            compiler_params=pltpu.CompilerParams(vmem_limit_bytes=60 << 20),
        )(*args)

    def net_scratch(plan):
        return [(8, plan.window), (72, plan.chunk + LEAD)]

    sweep_scratch = [pair, (2, 2, height + 2 * GUARD, 128), (2, height, 128)]

    w1 = jnp.pad(weight_one.reshape(3, 6, hid), ((0, 1), (0, 2), (0, 0))).reshape(32, hid)
    w1_half = (0.5 * w1.astype(F32)).astype(BF16).T
    w2_half = (0.5 * weight_two.astype(F32)).astype(BF16).T
    b1_half = 0.5 * bias_one[:, None]
    b2_half = 0.5 * bias_two[:, None]
    w3 = jnp.pad(weight_three.reshape(9, hid, nout), ((0, 0), (0, 0), (0, 8 - nout)))
    w3_out = jnp.transpose(w3, (0, 2, 1)).reshape(72, hid)
    w3_back = jnp.pad(jnp.transpose(w3, (1, 0, 2)).reshape(hid, 72), ((0, 0), (0, 8)))
    w1_back = jnp.pad(weight_one.reshape(9, 2, hid), ((0, 0), (0, 6), (0, 0))).reshape(72, hid)
    forward_weights = (w1_half, b1_half, w2_half, b2_half, w3_out)
    backward_weights = (w1_half, b1_half, w2_half, b2_half, w1_back, weight_two, w3_back)

    lane = np.arange(near.chunk)
    place_row, place_col = lane // near.wide, lane % near.wide
    mine = (place_col >= near.rim + 1) & (place_col < near.rim + 1 + cols)
    place = jnp.asarray(np.where(mine, place_row, -10 * height)[None, :], jnp.int32)

    total_cols = cols * lax.axis_size("gy")
    col_ids = lax.axis_index("gy") * cols + jnp.arange(frame[1], dtype=jnp.int32) - LEFT
    forcing = jnp.sin(col_ids.astype(F32) * (TWO_PI * FORCE_WAVES / total_cols))[None, :]

    both = exchange(jnp.concatenate([velocity[0], targets[0, step_count - 1]], axis=0), 32)
    v_first = both[:2]
    v_second, coefs_first, error_first, loss_first = call(
        functools.partial(first_kernel, far),
        [pair, packed, own_pair, (1, cols)],
        [packed] + net_scratch(far) + sweep_scratch,
        v_first, targets[0, 0], forcing, *forward_weights,
    )
    provisional, coefs_second = call(
        functools.partial(second_kernel, near),
        [own_pair, packed],
        [packed] + net_scratch(near),
        v_second, forcing, *forward_weights,
    )
    back_scratch = [packed, packed, packed] + net_scratch(near) + sweep_scratch
    start_sums = jnp.pad(loss_first, ((111, 0), (0, 128 - cols)))
    framed = exchange(provisional, 40)
    grad, sums = call(
        functools.partial(back_kernel, near, True), [own_pair, sums_shape], back_scratch,
        framed, both[2:], error_first, start_sums, v_second, coefs_second, place, *backward_weights,
    )
    framed = exchange(grad, 24)
    grad, sums = call(
        functools.partial(back_kernel, near, False), [own_pair, sums_shape], back_scratch,
        framed, forcing, forcing, sums, v_first, coefs_first, place, *backward_weights,
    )
    for axis in ("ens", "gx", "gy"):
        sums = total_over(sums, axis)
    device_count = lax.axis_size(("ens", "gx", "gy"))
    loss_scale = 1.0 / float(step_count * 2 * rows * cols * device_count)
    d1, db1, d2, db2, d3, loss = call(
        functools.partial(finish_kernel, loss_scale),
        [(18, hid), (1, hid), (hid, hid), (1, hid), (72, hid), (1, 1)], [], sums,
    )
    return (
        d1.reshape(weight_one.shape),
        db1[0],
        d2,
        db2[0],
        d3.reshape(9, 8, hid)[:, :nout].transpose(0, 2, 1).reshape(weight_three.shape),
        loss[0, 0],
        grad[None],
    )


def solution(mesh):
    return jax.shard_map(
        shards,
        mesh=mesh,
        in_specs=(P("ens", None, "gx", "gy"), P("ens", None, None, "gx", "gy"), P(), P(), P(), P(), P()),
        out_specs=(P(), P(), P(), P(), P(), P(), P("ens", None, "gx", "gy")),
        check_vma=False,
    )
```

```python
import functools

import jax
import jax.numpy as jnp
import numpy as np
from jax import lax
from jax.experimental import pallas as pl
from jax.experimental.pallas import tpu as pltpu
from jax.sharding import PartitionSpec as P

SWEEPS = 16
TIME_STEP = 0.2
VISCOSITY = 0.05
DRAG_RATE = 0.1
FORCE_WAVES = 4.0
COEF_SCALE = 0.1
EPSILON = 1e-06
OUTER_WEIGHT = -1.0 / 16.0
INNER_WEIGHT = 9.0 / 16.0
TWO_PI = 6.283185307179586

TOP = 40
LEFT = 64
CHUNK_ROWS = 16
LEAD = 384
GUARD = 8
BF16 = jnp.bfloat16
F32 = jnp.float32


def passed_along(block, axis, distance):
    size = lax.axis_size(axis)
    route = [(i, (i + distance) % size) for i in range(size)]
    return lax.ppermute(block, axis, route)


def exchange(owns, sides):
    rim, rows = sides[0].shape[1:]
    right = passed_along(sides[0], "gy", -1)
    left = passed_along(sides[1], "gy", 1)
    edges = []
    for first, tile, distance in ((rows - rim, rows - 128, 1), (0, 0, -1)):
        mine = jnp.concatenate([own[:, first : first + rim] for own in owns], axis=0)
        parts = [mine] + [part[:, :, tile : tile + 128] for part in (left, right)]
        edges.append(passed_along(jnp.concatenate(parts, axis=1), "gx", distance))
    return [left, right] + edges


def side_strips(field, rim):
    turned = field.T
    return turned[:rim], turned[turned.shape[0] - rim :]


def spread_out(middle, left, right, rows):
    rim = left.shape[0]
    lanes = left.shape[1]
    before = jnp.concatenate([jnp.zeros((LEFT - rim, lanes), F32), left, jnp.zeros((128 - LEFT, lanes), F32)], axis=0).T
    after = jnp.concatenate([jnp.zeros((LEFT, lanes), F32), right, jnp.zeros((128 - LEFT - rim, lanes), F32)], axis=0).T
    turned = pltpu.roll(middle, LEFT, 1)
    first_half = lax.broadcasted_iota(jnp.int32, middle.shape, 1) < LEFT
    return jnp.concatenate(
        [jnp.where(first_half, before[rows], turned), jnp.where(first_half, turned, after[rows])], axis=1
    )


def build_frame(own, pieces, comp, target_ref, target):
    left_ref, right_ref, above_ref, below_ref = pieces
    rim = left_ref.shape[1]
    rows = own.shape[0]
    if rim < TOP:
        target_ref[target, : TOP - rim] = jnp.zeros((TOP - rim, 256), F32)
        target_ref[target, TOP + rows + rim :] = jnp.zeros((TOP - rim, 256), F32)
    target_ref[target, TOP : TOP + rows] = spread_out(
        own, left_ref[comp], right_ref[comp], slice(0, rows)
    )
    for ref, first, kept in ((above_ref, TOP - rim, slice(128 - rim, 128)), (below_ref, TOP + rows, slice(0, rim))):
        target_ref[target, first : first + rim] = spread_out(
            ref[comp, :rim], ref[comp, rim : 2 * rim], ref[comp, 2 * rim :], kept
        )


def total_over(value, axis):
    size = lax.axis_size(axis)
    if size <= 4:
        moved = [passed_along(value, axis, distance) for distance in range(1, size)]
        for other in moved:
            value = value + other
        return value
    return lax.psum(value, axis)


def at(field, rows, cols):
    if rows:
        field = pltpu.roll(field, (-rows) % field.shape[0], 0)
    if cols:
        field = pltpu.roll(field, (-cols) % field.shape[1], 1)
    return field


def project(first, second, buffers, rhs_ref, rim):
    height = first.shape[0]
    quarter = -0.125 * (at(first, 1, 0) - at(first, -1, 0) + at(second, 0, 1) - at(second, 0, -1))
    for half in range(2):
        part = quarter[:, 128 * half : 128 * half + 128]
        rhs_ref[half] = part
        for buffer in range(2):
            buffers[buffer, half, :GUARD] = jnp.zeros((GUARD, 128), F32)
            buffers[buffer, half, GUARD + height :] = jnp.zeros((GUARD, 128), F32)
            buffers[buffer, half, GUARD : GUARD + height] = part
    lane = lax.broadcasted_iota(jnp.int32, (8, 128), 1)
    at_start = lane == 0
    at_end = lane == 127

    def one_sweep(source, target):
        for row in range(TOP - rim, height - TOP + rim, 8):
            here = [buffers[source, half, GUARD + row : GUARD + row + 8] for half in range(2)]
            ahead = [pltpu.roll(part, 127, 1) for part in here]
            behind = [pltpu.roll(part, 1, 1) for part in here]
            for half in range(2):
                above = buffers[source, half, GUARD + row - 1 : GUARD + row + 7]
                below = buffers[source, half, GUARD + row + 1 : GUARD + row + 9]
                east = jnp.where(at_end, ahead[1 - half], ahead[half])
                west = jnp.where(at_start, behind[1 - half], behind[half])
                near = (above + below) + (east + west)
                buffers[target, half, GUARD + row : GUARD + row + 8] = 0.25 * near + rhs_ref[half, row : row + 8]

    def two_sweeps(index, carried):
        one_sweep(0, 1)
        one_sweep(1, 0)
        return carried

    lax.fori_loop(0, SWEEPS // 2, two_sweeps, 0)
    p = jnp.concatenate([buffers[0, half, GUARD : GUARD + height] for half in range(2)], axis=1)
    above = jnp.concatenate([buffers[0, half, GUARD - 1 : GUARD - 1 + height] for half in range(2)], axis=1)
    below = jnp.concatenate([buffers[0, half, GUARD + 1 : GUARD + 1 + height] for half in range(2)], axis=1)
    return first - 0.5 * (below - above), second - 0.5 * (at(p, 0, 1) - at(p, 0, -1))


def faces(field, c0, c1, c2, move):
    return (
        (OUTER_WEIGHT + c0) * move(field, -1)
        + (INNER_WEIGHT + c1) * field
        + (INNER_WEIGHT + c2) * move(field, 1)
        + (OUTER_WEIGHT - c0 - c1 - c2) * move(field, 2)
    )


def by_row(field, distance):
    return at(field, distance, 0)


def by_col(field, distance):
    return at(field, 0, distance)


def advect(v, coefs, forcing):
    speed_rows = 0.5 * (v[0] + by_row(v[0], 1))
    speed_cols = 0.5 * (v[1] + by_col(v[1], 1))
    results = []
    for comp in range(2):
        q = v[comp]
        flux = speed_rows * faces(q, coefs[0], coefs[1], coefs[2], by_row)
        change = flux - by_row(flux, -1)
        flux = speed_cols * faces(q, coefs[3], coefs[4], coefs[5], by_col)
        change = change + (flux - by_col(flux, -1))
        laplace = by_row(q, 1) + by_row(q, -1) + by_col(q, 1) + by_col(q, -1) - 4.0 * q
        drive = VISCOSITY * laplace - DRAG_RATE * q
        if comp == 0:
            drive = drive + forcing
        results.append(q - TIME_STEP * change + TIME_STEP * drive)
    return results


def advect_back(v, coefs, g, keep_taps):
    results = [None, None]
    for axis in range(2):
        move = by_row if axis == 0 else by_col
        speed = 0.5 * (v[axis] + move(v[axis], 1))
        c0, c1, c2 = coefs[3 * axis : 3 * axis + 3]
        grads = []
        grad_speed = None
        taps = None
        for comp in range(2):
            q = v[comp]
            grad_flux = TIME_STEP * (move(g[comp], 1) - g[comp])
            term = grad_flux * faces(q, c0, c1, c2, move)
            grad_speed = term if grad_speed is None else grad_speed + term
            grad_face = grad_flux * speed
            behind = move(q, -1)
            ahead = move(q, 1)
            far = move(q, 2)
            new = (grad_face * (behind - far), grad_face * (q - far), grad_face * (ahead - far))
            taps = new if taps is None else tuple(a + b for a, b in zip(taps, new))
            grads.append(
                move(grad_face * (OUTER_WEIGHT + c0), 1)
                + grad_face * (INNER_WEIGHT + c1)
                + move(grad_face * (INNER_WEIGHT + c2), -1)
                + move(grad_face * (OUTER_WEIGHT - c0 - c1 - c2), -2)
            )
        grads[axis] = grads[axis] + 0.5 * (grad_speed + move(grad_speed, -1))
        for number in range(3):
            keep_taps(3 * axis + number, COEF_SCALE * taps[number])
        for comp in range(2):
            results[comp] = grads[comp] if axis == 0 else results[comp] + grads[comp]
    for comp in range(2):
        near = by_row(g[comp], 1) + by_row(g[comp], -1) + by_col(g[comp], 1) + by_col(g[comp], -1)
        drive = VISCOSITY * (near - 4.0 * g[comp]) - DRAG_RATE * g[comp]
        results[comp] = results[comp] + g[comp] + TIME_STEP * drive
    return results


class Plan:
    def __init__(self, rows, cols, rim):
        self.rows, self.cols, self.rim = rows, cols, rim
        self.wide = -(-(cols + 2 * rim + 4) // 8) * 8
        self.chunk = CHUNK_ROWS * self.wide
        self.chunks = -(-(rows + 2 * rim + 2) // CHUNK_ROWS)
        self.offsets = [row * self.wide + col for row in range(3) for col in range(3)]
        self.in_row, self.in_lane = TOP - rim - 2, LEFT - rim - 2
        self.out_row, self.out_lane = TOP - rim, LEFT - rim
        self.window = -(-(CHUNK_ROWS + 2) * self.wide // 128) * 128


def rounded(field):
    return field.astype(BF16).astype(F32)


def shifted(block, offset, length):
    if offset % block.shape[1]:
        block = pltpu.roll(block, (-offset) % block.shape[1], 1)
    return block[:, :length]


def lay_rows(source_ref, first_row, lane, wide, target_ref):
    lanes = lax.broadcasted_iota(jnp.int32, (8, 128), 1)
    tiles = {}
    for number in range(CHUNK_ROWS + 2):
        place = pl.ds(pl.multiple_of(8 * (first_row + number), 8), 8)
        block = jnp.concatenate([source_ref[half, place] for half in range(2)], axis=1)
        start = number * wide
        tile, offset = start // 128, start % 128
        block = pltpu.roll(block, (offset - lane) % 256, 1)
        for part in range(-(-(offset + wide) // 128)):
            piece = block[:, 128 * (part % 2) : 128 * (part % 2) + 128]
            if part == 0 and offset:
                piece = jnp.where(lanes < offset, tiles[tile], piece)
            tiles[tile + part] = piece
    for tile in range(target_ref.shape[1] // 128):
        target_ref[:, 128 * tile : 128 * tile + 128] = tiles[tile]


def split_rows(flat, target_ref, first_row, lane, wide):
    for number in range(CHUNK_ROWS):
        start = number * wide
        tile, offset = start // 128, start % 128
        parts = max(2, -(-(offset + wide) // 128))
        if tile + parts > flat.shape[1] // 128:
            tile, offset = tile - 1, offset + 128
        block = flat[:, 128 * tile : 128 * (tile + parts)]
        block = shifted(block, offset - lane, 256)
        place = pl.ds(pl.multiple_of(8 * (first_row + number), 8), 8)
        for half in range(2):
            target_ref[half, place] = block[:, 128 * half : 128 * half + 128]


def channel(ref, number, first_row, rows):
    place = pl.ds(8 * first_row + number, rows, stride=8)
    return jnp.concatenate([ref[half, place] for half in range(2)], axis=1)


def keep_channel(ref, number, first_row, field):
    place = pl.ds(8 * first_row + number, field.shape[0], stride=8)
    for half in range(2):
        ref[half, place] = field[:, 128 * half : 128 * half + 128]


def keep_inputs(v, inputs_ref):
    inputs_ref[...] = jnp.zeros_like(inputs_ref)
    for comp in range(2):
        field = rounded(v[comp])
        for col in range(3):
            keep_channel(inputs_ref, 2 * col + comp, 0, by_col(field, col))
    keep_channel(inputs_ref, 6, 0, jnp.ones_like(v[0]))


def product(left, right):
    return lax.dot_general(left, right, (((1,), (0,)), ((), ())), preferred_element_type=F32)


def product_over_cells(left, right):
    return lax.dot_general(left, right, (((1,), (1,)), ((), ())), preferred_element_type=F32)


def columns(plan, step, inputs_ref, window_ref):
    lay_rows(inputs_ref, plan.in_row + CHUNK_ROWS * step, plan.in_lane, plan.wide, window_ref)
    window = window_ref[...]
    parts = [shifted(window, row * plan.wide, plan.chunk) for row in range(3)]
    return jnp.concatenate(parts + [jnp.zeros((8, plan.chunk), F32)], axis=0)


def add_taps(terms_ref, offsets, length):
    total = None
    for tap, offset in enumerate(offsets):
        term = shifted(terms_ref[8 * tap : 8 * tap + 8, :], offset, length)
        total = term if total is None else total + term
    return total


def network(plan, inputs_ref, weight_refs, coefs_ref, window_ref, terms_ref):
    w1_ref, b1_ref, w2_ref, b2_ref, w3_ref = weight_refs
    terms_ref[...] = jnp.zeros_like(terms_ref)
    lag = LEAD - 2 * plan.wide

    def one_chunk(step, carried):
        cols = columns(plan, step, inputs_ref, window_ref).astype(BF16)
        half = product(w1_ref[...], cols) + b1_ref[...]
        hidden = (half * jnp.tanh(half) + half).astype(BF16)
        half = product(w2_ref[...], hidden) + b2_ref[...]
        hidden = (half * jnp.tanh(half) + half).astype(BF16)
        terms_ref[:, :LEAD] = terms_ref[:, plan.chunk :]
        terms_ref[:, LEAD:] = product(w3_ref[...], hidden)
        total = COEF_SCALE * add_taps(terms_ref, [offset + lag for offset in plan.offsets], plan.chunk)
        split_rows(total, coefs_ref, plan.out_row - 2 + CHUNK_ROWS * step, plan.out_lane, plan.wide)
        return carried

    lax.fori_loop(0, plan.chunks, one_chunk, 0)


def network_back(plan, inputs_ref, taps_ref, weight_refs, place_ref, grads_ref, sums_ref, cross_ref, window_ref, terms_ref):
    w1_ref, b1_ref, w2_ref, b2_ref, w1b_ref, w2b_ref, w3b_ref = weight_refs
    terms_ref[...] = jnp.zeros_like(terms_ref)
    cross_ref[...] = jnp.zeros_like(cross_ref)

    def one_chunk(step, carried):
        row = place_ref[...] + CHUNK_ROWS * step
        own = jnp.where((row >= plan.rim + 1) & (row < plan.rim + 1 + plan.rows), 1.0, 0.0)
        mask = own.astype(BF16)
        cols = columns(plan, step, inputs_ref, window_ref).astype(BF16)
        half = product(w1_ref[...], cols) + b1_ref[...]
        bend = jnp.tanh(half)
        hidden_one = (half * bend + half).astype(BF16)
        slope_one = (0.5 + 0.5 * bend) * (1.0 + half * (1.0 - bend))
        half = product(w2_ref[...], hidden_one) + b2_ref[...]
        bend = jnp.tanh(half)
        hidden_two = (half * bend + half).astype(BF16)
        slope_two = (0.5 + 0.5 * bend) * (1.0 + half * (1.0 - bend))
        lay_rows(taps_ref, plan.out_row - 2 + CHUNK_ROWS * step, plan.out_lane, plan.wide, window_ref)
        window = window_ref[...]
        parts = [shifted(window, 2 * plan.wide - offset, plan.chunk) for offset in plan.offsets]
        spread = jnp.concatenate(parts + [jnp.zeros((8, plan.chunk), F32)], axis=0).astype(BF16)
        grad_two = (product(w3b_ref[...], spread) * slope_two).astype(BF16)
        grad_one = (product(w2b_ref[...], grad_two) * slope_one).astype(BF16)
        left = jnp.concatenate([spread, hidden_one, cols], axis=0)
        right = jnp.concatenate([hidden_two * mask, grad_two * mask, grad_one * mask], axis=0)
        cross_ref[...] += product_over_cells(left, right)
        terms_ref[:, :LEAD] = terms_ref[:, plan.chunk :]
        terms_ref[:, LEAD:] = product(w1b_ref[...], grad_one)
        total = add_taps(terms_ref, [LEAD - offset for offset in plan.offsets], plan.chunk)
        split_rows(total, grads_ref, plan.in_row + CHUNK_ROWS * step, plan.in_lane, plan.wide)
        return carried

    lax.fori_loop(0, plan.chunks, one_chunk, 0)
    for tap in range(9):
        taken = 144 + 8 * (tap // 3) + 2 * (tap % 3)
        sums_ref[8 * tap : 8 * tap + 6, :64] += cross_ref[8 * tap : 8 * tap + 6, :64]
        sums_ref[8 * tap + 6 : 8 * tap + 8, :64] += cross_ref[taken : taken + 2, 128:192]
    sums_ref[:64, 64:] += cross_ref[80:144, 64:128]
    sums_ref[64:65, 64:] += cross_ref[150:151, 128:192]
    sums_ref[65:66, 64:] += cross_ref[150:151, 64:128]


def own_part(field, rows, cols, first_row):
    return pltpu.roll(field[TOP - first_row : TOP - first_row + rows], 256 - LEFT, 1)[:, :cols]


def lane_sums(squares):
    return jnp.sum(squares, axis=0, keepdims=True)


def strips_kernel(v_ref, goals_ref, low_ref, high_ref):
    rim = low_ref.shape[1]
    for number in range(4):
        field = v_ref[number] if number < 2 else goals_ref[goals_ref.shape[0] - 1, number - 2]
        low_ref[number], high_ref[number] = side_strips(field, rim)


def weights_kernel(w1_in, b1_in, w2_in, b2_in, w3_in, w1, b1, w2, b2, w3, w1b, w3b):
    hid = b1_in.shape[1]
    ahead, wide, back = [], [], []
    for row in range(3):
        parts = [w1_in[row, col].astype(F32) for col in range(3)]
        ahead += parts + [jnp.zeros((2, hid), F32)]
        for col in range(3):
            wide += [parts[col], jnp.zeros((6, hid), F32)]
            back += [w3_in[row, col].astype(F32), jnp.zeros((2, hid), F32)]
    ahead = jnp.concatenate(ahead + [jnp.zeros((8, hid), F32)], axis=0)
    back = jnp.concatenate(back, axis=0)
    w1[...] = (0.5 * ahead).T.astype(BF16)
    w1b[...] = jnp.concatenate(wide, axis=0).astype(BF16)
    w2[...] = (0.5 * w2_in[...].astype(F32)).T.astype(BF16)
    w3[...] = back.astype(BF16)
    w3b[...] = jnp.concatenate([back, jnp.zeros((8, hid), F32)], axis=0).T.astype(BF16)
    for source, target in ((b1_in, b1), (b2_in, b2)):
        target[...] = jnp.broadcast_to(0.5 * source[...], (8, hid)).T[:, :1]


def first_kernel(plan, left, right, above, below, own_ref, goals_ref, force_ref, w1, b1, w2, b2, w3,
                 v_ref, last_goal_ref, v_out, coefs_ref, error_ref, loss_ref, inputs_ref, window_ref, terms_ref, frame_ref, buffers, rhs_ref):
    pieces = (left, right, above, below)
    for comp in range(2):
        build_frame(own_ref[comp], pieces, comp, v_ref, comp)
        build_frame(goals_ref[goals_ref.shape[0] - 1, comp], pieces, comp + 2, last_goal_ref, comp)
    keep_inputs([v_ref[0], v_ref[1]], inputs_ref)
    coefs_ref[...] = jnp.zeros_like(coefs_ref)
    network(plan, inputs_ref, (w1, b1, w2, b2, w3), coefs_ref, window_ref, terms_ref)
    height = v_ref.shape[1]
    result = advect(
        [v_ref[0], v_ref[1]], [channel(coefs_ref, number, 0, height) for number in range(6)], force_ref[...]
    )
    for comp in range(2):
        frame_ref[comp] = result[comp]
    result = project(frame_ref[0], frame_ref[1], buffers, rhs_ref, 24)
    loss = None
    for comp in range(2):
        v_out[comp] = result[comp]
        error = own_part(result[comp], plan.rows, plan.cols, 0) - goals_ref[0, comp]
        error_ref[comp] = error
        square = lane_sums(error * error)
        loss = square if loss is None else loss + square
    loss_ref[...] = loss[:, :64] + loss[:, 64:]


def second_kernel(plan, v_ref, force_ref, w1, b1, w2, b2, w3, out_ref, low_ref, high_ref, coefs_ref, inputs_ref, window_ref, terms_ref):
    keep_inputs([v_ref[0], v_ref[1]], inputs_ref)
    coefs_ref[...] = jnp.zeros_like(coefs_ref)
    network(plan, inputs_ref, (w1, b1, w2, b2, w3), coefs_ref, window_ref, terms_ref)
    low, tall = TOP - 8, plan.rows + 16
    v = [v_ref[comp, low : low + tall] for comp in range(2)]
    result = advect(v, [channel(coefs_ref, number, low, tall) for number in range(6)], force_ref[...])
    for comp in range(2):
        mine = own_part(result[comp], plan.rows, plan.cols, low)
        out_ref[comp] = mine
        low_ref[comp], high_ref[comp] = side_strips(mine, low_ref.shape[1])


def back_kernel(plan, last, left, right, above, below, own_ref, goal_ref, extra_ref, before_ref, v_ref, coefs_ref,
                place_ref, w1, b1, w2, b2, w1b, w2b, w3b, out_ref, low_ref, high_ref, sums_ref, inputs_ref, taps_ref, grads_ref, cross_ref, window_ref, terms_ref, frame_ref, buffers, rhs_ref):
    rows, cols = plan.rows, plan.cols
    sums_ref[...] = before_ref[...]
    for comp in range(2):
        build_frame(own_ref[comp], (left, right, above, below), comp, frame_ref, comp)
    first, second = project(frame_ref[0], frame_ref[1], buffers, rhs_ref, TOP if last else 24)
    if last:
        errors = (first - goal_ref[0], second - goal_ref[1])
        for error in errors:
            mine = own_part(error, rows, cols, 0)
            loss = lane_sums(mine * mine)
            sums_ref[66:67, 64:] += loss[:, :64] + loss[:, 64:]
        for comp in range(2):
            frame_ref[comp] = errors[comp]
        first, second = project(frame_ref[0], frame_ref[1], buffers, rhs_ref, 24)
    frame_ref[0] = first
    frame_ref[1] = second
    keep_inputs([v_ref[0], v_ref[1]], inputs_ref)
    taps_ref[...] = jnp.zeros_like(taps_ref)
    low, tall = TOP - 8, rows + 16
    result = advect_back(
        [v_ref[comp, low : low + tall] for comp in range(2)],
        [channel(coefs_ref, number, low, tall) for number in range(6)],
        [frame_ref[comp, low : low + tall] for comp in range(2)],
        lambda number, field: keep_channel(taps_ref, number, low, rounded(field)),
    )
    for comp in range(2):
        frame_ref[comp, low : low + tall] = result[comp]
    weight_refs = (w1, b1, w2, b2, w1b, w2b, w3b)
    network_back(plan, inputs_ref, taps_ref, weight_refs, place_ref, grads_ref, sums_ref, cross_ref, window_ref, terms_ref)
    for comp in range(2):
        field = frame_ref[comp, low : low + tall] + channel(grads_ref, comp, low, tall)
        total = own_part(field, rows, cols, low)
        if last:
            total = total + extra_ref[comp]
            low_ref[comp], high_ref[comp] = side_strips(total, low_ref.shape[1])
        out_ref[comp] = total
    if not last:
        low_ref[...] = jnp.zeros_like(low_ref)
        high_ref[...] = jnp.zeros_like(high_ref)


def scaled(piece, count):
    return piece * (1.0 / jnp.sqrt(jnp.sum(piece * piece) / count + EPSILON))


def finish_kernel(loss_scale, in_ref, w1_ref, b1_ref, w2_ref, b2_ref, w3_ref, loss_ref):
    one = jnp.concatenate([in_ref[8 * tap + 6 : 8 * tap + 8, :64] for tap in range(9)], axis=0)
    three = jnp.concatenate([in_ref[8 * tap : 8 * tap + 6, :64] for tap in range(9)], axis=0)
    w1_ref[...] = scaled(one, one.size)
    b1_ref[...] = scaled(in_ref[64:65, 64:], 64)
    b2_ref[...] = scaled(in_ref[65:66, 64:], 64)
    w2_ref[...] = scaled(in_ref[:64, 64:], 64 * 64)
    w3_ref[...] = scaled(three, three.size)
    loss_ref[...] = (0.5 * loss_scale) * jnp.sum(in_ref[66:67, 64:], axis=1, keepdims=True)


def shards(velocity, targets, weight_one, bias_one, weight_two, bias_two, weight_three):
    rows, cols = velocity.shape[2], velocity.shape[3]
    step_count = targets.shape[1]
    height = rows + 2 * TOP
    frame = (height, cols + 2 * LEFT)
    pair = (2,) + frame
    own_pair = (2, rows, cols)
    packed = (2, 8 * height, 128)
    sums_shape = (72, 128)
    hid = weight_two.shape[0]
    nout = weight_three.shape[3]
    near = Plan(rows, cols, 2)
    far = Plan(rows, cols, 23)

    def call(kernel, outs, scratch, *args, kind=F32):
        return pl.pallas_call(
            kernel,
            out_shape=[jax.ShapeDtypeStruct(shape, F32 if shape[1] == 1 else kind) for shape in outs],
            scratch_shapes=[pltpu.VMEM(shape, F32) for shape in scratch],
            compiler_params=pltpu.CompilerParams(vmem_limit_bytes=60 << 20),
        )(*args)

    def net_scratch(plan):
        return [(8, plan.window), (72, plan.chunk + LEAD)]

    sweep_scratch = [pair, (2, 2, height + 2 * GUARD, 128), (2, height, 128)]

    w1, b1, w2, b2, w3, w1b, w3b = call(
        weights_kernel, [(hid, 32), (hid, 1), (hid, hid), (hid, 1), (72, hid), (72, hid), (hid, 80)], [],
        weight_one, bias_one[None, :], weight_two, bias_two[None, :], jnp.swapaxes(weight_three, 2, 3), kind=BF16,
    )
    forward_weights = (w1, b1, w2, b2, w3)
    backward_weights = (w1, b1, w2, b2, w1b, weight_two, w3b)

    lane = np.arange(near.chunk)
    place_row, place_col = lane // near.wide, lane % near.wide
    mine = (place_col >= near.rim + 1) & (place_col < near.rim + 1 + cols)
    place = jnp.asarray(np.where(mine, place_row, -10 * height)[None, :], jnp.int32)

    total_cols = cols * lax.axis_size("gy")
    col_ids = lax.axis_index("gy") * cols + jnp.arange(frame[1], dtype=jnp.int32) - LEFT
    forcing = jnp.sin(col_ids.astype(F32) * (TWO_PI * FORCE_WAVES / total_cols))[None, :]

    def strips(count, rim):
        return [(count, rim, rows)] * 2

    sides = call(strips_kernel, strips(4, 32), [], velocity[0], targets[0])
    pieces = exchange([velocity[0], targets[0, step_count - 1]], sides)
    v_first, last_goal, v_second, coefs_first, error_first, loss_first = call(
        functools.partial(first_kernel, far),
        [pair, pair, pair, packed, own_pair, (1, 64)],
        [packed] + net_scratch(far) + sweep_scratch,
        *pieces, velocity[0], targets[0], forcing, *forward_weights,
    )
    provisional, low, high, coefs_second = call(
        functools.partial(second_kernel, near),
        [own_pair] + strips(2, 40) + [packed],
        [packed] + net_scratch(near),
        v_second, forcing, *forward_weights,
    )
    back_scratch = [packed, packed, packed, (176, 192)] + net_scratch(near) + sweep_scratch
    start_sums = jnp.pad(loss_first, ((66, 5), (64, 0)))
    grad, low, high, sums = call(
        functools.partial(back_kernel, near, True),
        [own_pair] + strips(2, 24) + [sums_shape], back_scratch,
        *exchange([provisional], (low, high)), provisional, last_goal, error_first, start_sums, v_second, coefs_second, place,
        *backward_weights,
    )
    grad, _, _, sums = call(
        functools.partial(back_kernel, near, False),
        [own_pair] + [(1, 8, 128)] * 2 + [sums_shape], back_scratch,
        *exchange([grad], (low, high)), grad, forcing, forcing, sums, v_first, coefs_first, place, *backward_weights,
    )
    for axis in ("ens", "gx", "gy"):
        sums = total_over(sums, axis)
    device_count = lax.axis_size(("ens", "gx", "gy"))
    loss_scale = 1.0 / float(step_count * 2 * rows * cols * device_count)
    d1, db1, d2, db2, d3, loss = call(
        functools.partial(finish_kernel, loss_scale),
        [(18, hid), (1, hid), (hid, hid), (1, hid), (54, hid), (1, 1)], [], sums,
    )
    return (
        d1.reshape(weight_one.shape),
        db1[0],
        d2,
        db2[0],
        d3.reshape(3, 3, nout, hid).transpose(0, 1, 3, 2),
        loss[0, 0],
        grad[None],
    )


def solution(mesh):
    return jax.shard_map(
        shards,
        mesh=mesh,
        in_specs=(P("ens", None, "gx", "gy"), P("ens", None, None, "gx", "gy"), P(), P(), P(), P(), P()),
        out_specs=(P(), P(), P(), P(), P(), P(), P("ens", None, "gx", "gy")),
        check_vma=False,
    )
```

```python
import functools

import jax
import jax.numpy as jnp
import numpy as np
from jax import lax
from jax.experimental import pallas as pl
from jax.experimental.pallas import tpu as pltpu
from jax.sharding import PartitionSpec as P

SWEEPS = 16
TIME_STEP = 0.2
VISCOSITY = 0.05
DRAG_RATE = 0.1
FORCE_WAVES = 4.0
COEF_SCALE = 0.1
EPSILON = 1e-06
OUTER_WEIGHT = -1.0 / 16.0
INNER_WEIGHT = 9.0 / 16.0
TWO_PI = 6.283185307179586

TOP = 40
LEFT = 64
CHUNK_ROWS = 16
LEAD = 384
GUARD = 8
BF16 = jnp.bfloat16
F32 = jnp.float32


def passed_along(block, axis, distance):
    size = lax.axis_size(axis)
    route = [(i, (i + distance) % size) for i in range(size)]
    return lax.ppermute(block, axis, route)


def exchange(owns, sides):
    rim, rows = sides[0].shape[1:]
    right = passed_along(sides[0], "gy", -1)
    left = passed_along(sides[1], "gy", 1)
    edges = []
    for first, tile, distance in ((rows - rim, rows - 128, 1), (0, 0, -1)):
        mine = jnp.concatenate([own[:, first : first + rim] for own in owns], axis=0)
        parts = [mine] + [part[:, :, tile : tile + 128] for part in (left, right)]
        edges.append(passed_along(jnp.concatenate(parts, axis=1), "gx", distance))
    return [left, right] + edges


def side_strips(field, rim):
    turned = field.T
    return turned[:rim], turned[turned.shape[0] - rim :]


def spread_out(middle, left, right, rows):
    rim = left.shape[0]
    lanes = left.shape[1]
    before = jnp.concatenate([jnp.zeros((LEFT - rim, lanes), F32), left, jnp.zeros((128 - LEFT, lanes), F32)], axis=0).T
    after = jnp.concatenate([jnp.zeros((LEFT, lanes), F32), right, jnp.zeros((128 - LEFT - rim, lanes), F32)], axis=0).T
    turned = pltpu.roll(middle, LEFT, 1)
    first_half = lax.broadcasted_iota(jnp.int32, middle.shape, 1) < LEFT
    return jnp.concatenate(
        [jnp.where(first_half, before[rows], turned), jnp.where(first_half, turned, after[rows])], axis=1
    )


def build_frame(own, pieces, comp, target_ref, target):
    left_ref, right_ref, above_ref, below_ref = pieces
    rim = left_ref.shape[1]
    rows = own.shape[0]
    if rim < TOP:
        target_ref[target, : TOP - rim] = jnp.zeros((TOP - rim, 256), F32)
        target_ref[target, TOP + rows + rim :] = jnp.zeros((TOP - rim, 256), F32)
    target_ref[target, TOP : TOP + rows] = spread_out(
        own, left_ref[comp], right_ref[comp], slice(0, rows)
    )
    for ref, first, kept in ((above_ref, TOP - rim, slice(128 - rim, 128)), (below_ref, TOP + rows, slice(0, rim))):
        target_ref[target, first : first + rim] = spread_out(
            ref[comp, :rim], ref[comp, rim : 2 * rim], ref[comp, 2 * rim :], kept
        )


def total_over(value, axis):
    size = lax.axis_size(axis)
    if size <= 4:
        moved = [passed_along(value, axis, distance) for distance in range(1, size)]
        for other in moved:
            value = value + other
        return value
    return lax.psum(value, axis)


def at(field, rows, cols):
    if rows:
        field = pltpu.roll(field, (-rows) % field.shape[0], 0)
    if cols:
        field = pltpu.roll(field, (-cols) % field.shape[1], 1)
    return field


def project(first, second, buffers, rhs_ref, rim):
    height = first.shape[0]
    quarter = -0.125 * (at(first, 1, 0) - at(first, -1, 0) + at(second, 0, 1) - at(second, 0, -1))
    for half in range(2):
        part = quarter[:, 128 * half : 128 * half + 128]
        rhs_ref[half] = part
        for buffer in range(2):
            buffers[buffer, half, :GUARD] = jnp.zeros((GUARD, 128), F32)
            buffers[buffer, half, GUARD + height :] = jnp.zeros((GUARD, 128), F32)
            buffers[buffer, half, GUARD : GUARD + height] = part
    lane = lax.broadcasted_iota(jnp.int32, (8, 128), 1)
    at_start = lane == 0
    at_end = lane == 127

    def one_sweep(source, target):
        for row in range(TOP - rim, height - TOP + rim, 8):
            here = [buffers[source, half, GUARD + row : GUARD + row + 8] for half in range(2)]
            ahead = [pltpu.roll(part, 127, 1) for part in here]
            behind = [pltpu.roll(part, 1, 1) for part in here]
            for half in range(2):
                above = buffers[source, half, GUARD + row - 1 : GUARD + row + 7]
                below = buffers[source, half, GUARD + row + 1 : GUARD + row + 9]
                east = jnp.where(at_end, ahead[1 - half], ahead[half])
                west = jnp.where(at_start, behind[1 - half], behind[half])
                near = (above + below) + (east + west)
                buffers[target, half, GUARD + row : GUARD + row + 8] = 0.25 * near + rhs_ref[half, row : row + 8]

    def two_sweeps(index, carried):
        one_sweep(0, 1)
        one_sweep(1, 0)
        return carried

    lax.fori_loop(0, SWEEPS // 2, two_sweeps, 0)
    p = jnp.concatenate([buffers[0, half, GUARD : GUARD + height] for half in range(2)], axis=1)
    above = jnp.concatenate([buffers[0, half, GUARD - 1 : GUARD - 1 + height] for half in range(2)], axis=1)
    below = jnp.concatenate([buffers[0, half, GUARD + 1 : GUARD + 1 + height] for half in range(2)], axis=1)
    return first - 0.5 * (below - above), second - 0.5 * (at(p, 0, 1) - at(p, 0, -1))


def faces(field, c0, c1, c2, move):
    return (
        (OUTER_WEIGHT + c0) * move(field, -1)
        + (INNER_WEIGHT + c1) * field
        + (INNER_WEIGHT + c2) * move(field, 1)
        + (OUTER_WEIGHT - c0 - c1 - c2) * move(field, 2)
    )


def by_row(field, distance):
    return at(field, distance, 0)


def by_col(field, distance):
    return at(field, 0, distance)


def advect(v, coefs, forcing):
    speed_rows = 0.5 * (v[0] + by_row(v[0], 1))
    speed_cols = 0.5 * (v[1] + by_col(v[1], 1))
    results = []
    for comp in range(2):
        q = v[comp]
        flux = speed_rows * faces(q, coefs[0], coefs[1], coefs[2], by_row)
        change = flux - by_row(flux, -1)
        flux = speed_cols * faces(q, coefs[3], coefs[4], coefs[5], by_col)
        change = change + (flux - by_col(flux, -1))
        laplace = by_row(q, 1) + by_row(q, -1) + by_col(q, 1) + by_col(q, -1) - 4.0 * q
        drive = VISCOSITY * laplace - DRAG_RATE * q
        if comp == 0:
            drive = drive + forcing
        results.append(q - TIME_STEP * change + TIME_STEP * drive)
    return results


def advect_back(v, coefs, g, keep_taps):
    results = [None, None]
    for axis in range(2):
        move = by_row if axis == 0 else by_col
        speed = 0.5 * (v[axis] + move(v[axis], 1))
        c0, c1, c2 = coefs[3 * axis : 3 * axis + 3]
        grads = []
        grad_speed = None
        taps = None
        for comp in range(2):
            q = v[comp]
            grad_flux = TIME_STEP * (move(g[comp], 1) - g[comp])
            term = grad_flux * faces(q, c0, c1, c2, move)
            grad_speed = term if grad_speed is None else grad_speed + term
            grad_face = grad_flux * speed
            behind = move(q, -1)
            ahead = move(q, 1)
            far = move(q, 2)
            new = (grad_face * (behind - far), grad_face * (q - far), grad_face * (ahead - far))
            taps = new if taps is None else tuple(a + b for a, b in zip(taps, new))
            grads.append(
                move(grad_face * (OUTER_WEIGHT + c0), 1)
                + grad_face * (INNER_WEIGHT + c1)
                + move(grad_face * (INNER_WEIGHT + c2), -1)
                + move(grad_face * (OUTER_WEIGHT - c0 - c1 - c2), -2)
            )
        grads[axis] = grads[axis] + 0.5 * (grad_speed + move(grad_speed, -1))
        for number in range(3):
            keep_taps(3 * axis + number, COEF_SCALE * taps[number])
        for comp in range(2):
            results[comp] = grads[comp] if axis == 0 else results[comp] + grads[comp]
    for comp in range(2):
        near = by_row(g[comp], 1) + by_row(g[comp], -1) + by_col(g[comp], 1) + by_col(g[comp], -1)
        drive = VISCOSITY * (near - 4.0 * g[comp]) - DRAG_RATE * g[comp]
        results[comp] = results[comp] + g[comp] + TIME_STEP * drive
    return results


class Plan:
    def __init__(self, rows, cols, rim):
        self.rows, self.cols, self.rim = rows, cols, rim
        self.wide = -(-(cols + 2 * rim + 4) // 8) * 8
        self.chunk = CHUNK_ROWS * self.wide
        self.chunks = -(-(rows + 2 * rim + 2) // CHUNK_ROWS)
        self.offsets = [row * self.wide + col for row in range(3) for col in range(3)]
        self.in_row, self.in_lane = TOP - rim - 2, LEFT - rim - 2
        self.out_row, self.out_lane = TOP - rim, LEFT - rim
        self.window = -(-(CHUNK_ROWS + 2) * self.wide // 128) * 128


def rounded(field):
    return field.astype(BF16).astype(F32)


def shifted(block, offset, length):
    if offset % block.shape[1]:
        block = pltpu.roll(block, (-offset) % block.shape[1], 1)
    return block[:, :length]


def lay_rows(source_ref, first_row, lane, wide, target_ref):
    lanes = lax.broadcasted_iota(jnp.int32, (8, 128), 1)
    tiles = {}
    for number in range(CHUNK_ROWS + 2):
        place = pl.ds(pl.multiple_of(8 * (first_row + number), 8), 8)
        block = jnp.concatenate([source_ref[half, place] for half in range(2)], axis=1)
        start = number * wide
        tile, offset = start // 128, start % 128
        block = pltpu.roll(block, (offset - lane) % 256, 1)
        for part in range(-(-(offset + wide) // 128)):
            piece = block[:, 128 * (part % 2) : 128 * (part % 2) + 128]
            if part == 0 and offset:
                piece = jnp.where(lanes < offset, tiles[tile], piece)
            tiles[tile + part] = piece
    for tile in range(target_ref.shape[1] // 128):
        target_ref[:, 128 * tile : 128 * tile + 128] = tiles[tile]


def split_rows(flat, target_ref, first_row, lane, wide):
    for number in range(CHUNK_ROWS):
        start = number * wide
        tile, offset = start // 128, start % 128
        parts = max(2, -(-(offset + wide) // 128))
        if tile + parts > flat.shape[1] // 128:
            tile, offset = tile - 1, offset + 128
        block = flat[:, 128 * tile : 128 * (tile + parts)]
        block = shifted(block, offset - lane, 256)
        place = pl.ds(pl.multiple_of(8 * (first_row + number), 8), 8)
        for half in range(2):
            target_ref[half, place] = block[:, 128 * half : 128 * half + 128]


def channel(ref, number, first_row, rows):
    place = pl.ds(8 * first_row + number, rows, stride=8)
    return jnp.concatenate([ref[half, place] for half in range(2)], axis=1)


def keep_channel(ref, number, first_row, field):
    place = pl.ds(8 * first_row + number, field.shape[0], stride=8)
    for half in range(2):
        ref[half, place] = field[:, 128 * half : 128 * half + 128]


def keep_inputs(v, inputs_ref):
    inputs_ref[...] = jnp.zeros_like(inputs_ref)
    for comp in range(2):
        field = rounded(v[comp])
        for col in range(3):
            keep_channel(inputs_ref, 2 * col + comp, 0, by_col(field, col))
    keep_channel(inputs_ref, 6, 0, jnp.ones_like(v[0]))


def product(left, right):
    return lax.dot_general(left, right, (((1,), (0,)), ((), ())), preferred_element_type=F32)


def product_over_cells(left, right):
    return lax.dot_general(left, right, (((1,), (1,)), ((), ())), preferred_element_type=F32)


def columns(plan, row, inputs_ref, window_ref):
    lay_rows(inputs_ref, plan.in_row + row, plan.in_lane, plan.wide, window_ref)
    window = window_ref[...]
    parts = [shifted(window, row * plan.wide, plan.chunk) for row in range(3)]
    return jnp.concatenate(parts + [jnp.zeros((8, plan.chunk), F32)], axis=0)


def add_taps(terms_ref, offsets, length):
    total = None
    for tap, offset in enumerate(offsets):
        term = shifted(terms_ref[8 * tap : 8 * tap + 8, :], offset, length)
        total = term if total is None else total + term
    return total


def before_silu(weight_ref, inputs, bias_ref):
    bias = jnp.concatenate([bias_ref[...]] * (inputs.shape[1] // 128), axis=1)
    return product(weight_ref[...], inputs) + bias


def network(plan, inputs_ref, weight_refs, coefs_ref, window_ref, terms_ref, one_ref, two_ref):
    w1_ref, b1_ref, w2_ref, b2_ref, w3_ref = weight_refs
    terms_ref[...] = jnp.zeros_like(terms_ref)
    one_ref[...] = jnp.zeros_like(one_ref)
    two_ref[...] = jnp.zeros_like(two_ref)
    lag = LEAD - 2 * plan.wide

    def one_turn(turn, carried):
        last = jnp.maximum(turn - 2, 0)
        terms_ref[:, :LEAD] = terms_ref[:, plan.chunk :]
        cols = columns(plan, CHUNK_ROWS * jnp.minimum(turn, plan.chunks - 1), inputs_ref, window_ref).astype(BF16)
        terms_ref[:, LEAD:] = product(w3_ref[...], two_ref[...])
        half = before_silu(w2_ref, one_ref[...], b2_ref)
        two_ref[...] = (half * jnp.tanh(half) + half).astype(BF16)
        half = before_silu(w1_ref, cols, b1_ref)
        one_ref[...] = (half * jnp.tanh(half) + half).astype(BF16)
        total = COEF_SCALE * add_taps(terms_ref, [offset + lag for offset in plan.offsets], plan.chunk)
        split_rows(total, coefs_ref, plan.out_row - 2 + CHUNK_ROWS * last, plan.out_lane, plan.wide)
        return carried

    lax.fori_loop(0, plan.chunks + 2, one_turn, 0)


def with_slope(half):
    bend = jnp.tanh(half)
    return half * bend + half, (0.5 + 0.5 * bend) * (1.0 + half * (1.0 - bend))


def network_back(plan, inputs_ref, taps_ref, weight_refs, place_ref, grads_ref, sums_ref, net_refs):
    w1_ref, b1_ref, w2_ref, b2_ref, w1b_ref, w2b_ref, w3b_ref = weight_refs
    cross_ref, window_ref, terms_ref = net_refs
    terms_ref[...] = jnp.zeros_like(terms_ref)
    cross_ref[...] = jnp.zeros_like(cross_ref)

    def one_chunk(step, carried):
        row = CHUNK_ROWS * step
        place = place_ref[...] + row
        own = jnp.where((place >= plan.rim + 1) & (place < plan.rim + 1 + plan.rows), 1.0, 0.0).astype(BF16)
        own = jnp.concatenate([own] * 4, axis=0)
        cols = columns(plan, row, inputs_ref, window_ref).astype(BF16)
        hidden, slope_one = with_slope(before_silu(w1_ref, cols, b1_ref))
        hidden_one = hidden.astype(BF16)
        hidden, slope_two = with_slope(before_silu(w2_ref, hidden_one, b2_ref))
        hidden_two = hidden.astype(BF16)
        lay_rows(taps_ref, plan.out_row - 2 + row, plan.out_lane, plan.wide, window_ref)
        window = window_ref[...]
        parts = [shifted(window, 2 * plan.wide - offset, plan.chunk) for offset in plan.offsets]
        spread = jnp.concatenate(parts + [jnp.zeros((8, plan.chunk), F32)], axis=0).astype(BF16)
        grad_two = (product(w3b_ref[...], spread) * slope_two).astype(BF16)
        grad_one = (product(w2b_ref[...], grad_two) * slope_one).astype(BF16)
        left = jnp.concatenate([spread, hidden_one, cols], axis=0)
        right = jnp.concatenate([hidden_two * own, grad_two * own, grad_one * own], axis=0)
        cross_ref[...] += product_over_cells(left, right)
        terms_ref[:, :LEAD] = terms_ref[:, plan.chunk :]
        terms_ref[:, LEAD:] = product(w1b_ref[...], grad_one)
        total = add_taps(terms_ref, [LEAD - offset for offset in plan.offsets], plan.chunk)
        split_rows(total, grads_ref, plan.in_row + row, plan.in_lane, plan.wide)
        return carried

    lax.fori_loop(0, plan.chunks // 2, lambda pair, carried: one_chunk(2 * pair + 1, one_chunk(2 * pair, carried)), 0)
    if plan.chunks % 2:
        one_chunk(plan.chunks - 1, 0)
    for tap in range(9):
        taken = 144 + 8 * (tap // 3) + 2 * (tap % 3)
        sums_ref[8 * tap : 8 * tap + 6, :64] += cross_ref[8 * tap : 8 * tap + 6, :64]
        sums_ref[8 * tap + 6 : 8 * tap + 8, :64] += cross_ref[taken : taken + 2, 128:192]
    sums_ref[:64, 64:] += cross_ref[80:144, 64:128]
    sums_ref[64:65, 64:] += cross_ref[150:151, 128:192]
    sums_ref[65:66, 64:] += cross_ref[150:151, 64:128]


def own_part(field, rows, cols, first_row):
    return pltpu.roll(field[TOP - first_row : TOP - first_row + rows], 256 - LEFT, 1)[:, :cols]


def lane_sums(squares):
    return jnp.sum(squares, axis=0, keepdims=True)


def strips_kernel(v_ref, goals_ref, low_ref, high_ref):
    rim = low_ref.shape[1]
    for number in range(4):
        field = v_ref[number] if number < 2 else goals_ref[goals_ref.shape[0] - 1, number - 2]
        low_ref[number], high_ref[number] = side_strips(field, rim)


def weights_kernel(w1_in, b1_in, w2_in, b2_in, w3_in, w1, b1, w2, b2, w3, w1b, w3b):
    hid = b1_in.shape[1]
    ahead, wide, back = [], [], []
    for row in range(3):
        parts = [w1_in[row, col].astype(F32) for col in range(3)]
        ahead += parts + [jnp.zeros((2, hid), F32)]
        for col in range(3):
            wide += [parts[col], jnp.zeros((6, hid), F32)]
            back += [w3_in[row, col].astype(F32), jnp.zeros((2, hid), F32)]
    ahead = jnp.concatenate(ahead + [jnp.zeros((8, hid), F32)], axis=0)
    back = jnp.concatenate(back, axis=0)
    w1[...] = (0.5 * ahead).T.astype(BF16)
    w1b[...] = jnp.concatenate(wide, axis=0).astype(BF16)
    w2[...] = (0.5 * w2_in[...].astype(F32)).T.astype(BF16)
    w3[...] = back.astype(BF16)
    w3b[...] = jnp.concatenate([back, jnp.zeros((8, hid), F32)], axis=0).T.astype(BF16)
    for source, target in ((b1_in, b1), (b2_in, b2)):
        target[...] = jnp.broadcast_to(0.5 * source[...], (128, hid)).T


def first_kernel(plan, left, right, above, below, own_ref, goals_ref, force_ref, w1, b1, w2, b2, w3,
                 v_ref, last_goal_ref, v_out, coefs_ref, error_ref, loss_ref, inputs_ref, window_ref, terms_ref, one_ref, two_ref, frame_ref, buffers, rhs_ref):
    pieces = (left, right, above, below)
    for comp in range(2):
        build_frame(own_ref[comp], pieces, comp, v_ref, comp)
        build_frame(goals_ref[goals_ref.shape[0] - 1, comp], pieces, comp + 2, last_goal_ref, comp)
    keep_inputs([v_ref[0], v_ref[1]], inputs_ref)
    coefs_ref[...] = jnp.zeros_like(coefs_ref)
    network(plan, inputs_ref, (w1, b1, w2, b2, w3), coefs_ref, window_ref, terms_ref, one_ref, two_ref)
    height = v_ref.shape[1]
    result = advect(
        [v_ref[0], v_ref[1]], [channel(coefs_ref, number, 0, height) for number in range(6)], force_ref[...]
    )
    for comp in range(2):
        frame_ref[comp] = result[comp]
    result = project(frame_ref[0], frame_ref[1], buffers, rhs_ref, 24)
    loss = None
    for comp in range(2):
        v_out[comp] = result[comp]
        error = own_part(result[comp], plan.rows, plan.cols, 0) - goals_ref[0, comp]
        error_ref[comp] = error
        square = lane_sums(error * error)
        loss = square if loss is None else loss + square
    loss_ref[...] = loss[:, :64] + loss[:, 64:]


def second_kernel(plan, v_ref, force_ref, w1, b1, w2, b2, w3, out_ref, low_ref, high_ref, coefs_ref, inputs_ref, window_ref,
                  terms_ref, one_ref, two_ref):
    keep_inputs([v_ref[0], v_ref[1]], inputs_ref)
    coefs_ref[...] = jnp.zeros_like(coefs_ref)
    network(plan, inputs_ref, (w1, b1, w2, b2, w3), coefs_ref, window_ref, terms_ref, one_ref, two_ref)
    low, tall = TOP - 8, plan.rows + 16
    v = [v_ref[comp, low : low + tall] for comp in range(2)]
    result = advect(v, [channel(coefs_ref, number, low, tall) for number in range(6)], force_ref[...])
    for comp in range(2):
        mine = own_part(result[comp], plan.rows, plan.cols, low)
        out_ref[comp] = mine
        low_ref[comp], high_ref[comp] = side_strips(mine, low_ref.shape[1])


def back_kernel(plan, last, left, right, above, below, own_ref, goal_ref, extra_ref, before_ref, v_ref, coefs_ref,
                place_ref, w1, b1, w2, b2, w1b, w2b, w3b, out_ref, low_ref, high_ref, sums_ref, inputs_ref, taps_ref, grads_ref, frame_ref, buffers, rhs_ref, *net_refs):
    rows, cols = plan.rows, plan.cols
    sums_ref[...] = before_ref[...]
    for comp in range(2):
        build_frame(own_ref[comp], (left, right, above, below), comp, frame_ref, comp)
    first, second = project(frame_ref[0], frame_ref[1], buffers, rhs_ref, TOP if last else 24)
    if last:
        errors = (first - goal_ref[0], second - goal_ref[1])
        for error in errors:
            mine = own_part(error, rows, cols, 0)
            loss = lane_sums(mine * mine)
            sums_ref[66:67, 64:] += loss[:, :64] + loss[:, 64:]
        for comp in range(2):
            frame_ref[comp] = errors[comp]
        first, second = project(frame_ref[0], frame_ref[1], buffers, rhs_ref, 24)
    frame_ref[0] = first
    frame_ref[1] = second
    keep_inputs([v_ref[0], v_ref[1]], inputs_ref)
    taps_ref[...] = jnp.zeros_like(taps_ref)
    low, tall = TOP - 8, rows + 16
    result = advect_back(
        [v_ref[comp, low : low + tall] for comp in range(2)],
        [channel(coefs_ref, number, low, tall) for number in range(6)],
        [frame_ref[comp, low : low + tall] for comp in range(2)],
        lambda number, field: keep_channel(taps_ref, number, low, rounded(field)),
    )
    for comp in range(2):
        frame_ref[comp, low : low + tall] = result[comp]
    weight_refs = (w1, b1, w2, b2, w1b, w2b, w3b)
    network_back(plan, inputs_ref, taps_ref, weight_refs, place_ref, grads_ref, sums_ref, net_refs)
    for comp in range(2):
        field = frame_ref[comp, low : low + tall] + channel(grads_ref, comp, low, tall)
        total = own_part(field, rows, cols, low)
        if last:
            total = total + extra_ref[comp]
            low_ref[comp], high_ref[comp] = side_strips(total, low_ref.shape[1])
        out_ref[comp] = total
    if not last:
        low_ref[...] = jnp.zeros_like(low_ref)
        high_ref[...] = jnp.zeros_like(high_ref)


def scaled(piece, count):
    return piece * (1.0 / jnp.sqrt(jnp.sum(piece * piece) / count + EPSILON))


def finish_kernel(loss_scale, in_ref, w1_ref, b1_ref, w2_ref, b2_ref, w3_ref, loss_ref):
    one = jnp.concatenate([in_ref[8 * tap + 6 : 8 * tap + 8, :64] for tap in range(9)], axis=0)
    three = jnp.concatenate([in_ref[8 * tap : 8 * tap + 6, :64] for tap in range(9)], axis=0)
    w1_ref[...] = scaled(one, one.size)
    b1_ref[...] = scaled(in_ref[64:65, 64:], 64)
    b2_ref[...] = scaled(in_ref[65:66, 64:], 64)
    w2_ref[...] = scaled(in_ref[:64, 64:], 64 * 64)
    w3_ref[...] = scaled(three, three.size)
    loss_ref[...] = (0.5 * loss_scale) * jnp.sum(in_ref[66:67, 64:], axis=1, keepdims=True)


def shards(velocity, targets, weight_one, bias_one, weight_two, bias_two, weight_three):
    rows, cols = velocity.shape[2], velocity.shape[3]
    step_count = targets.shape[1]
    height = rows + 2 * TOP
    frame = (height, cols + 2 * LEFT)
    pair = (2,) + frame
    own_pair = (2, rows, cols)
    packed = (2, 8 * height, 128)
    sums_shape = (72, 128)
    hid = weight_two.shape[0]
    nout = weight_three.shape[3]
    near = Plan(rows, cols, 2)
    far = Plan(rows, cols, 23)

    def call(kernel, outs, scratch, *args, kind=F32):
        return pl.pallas_call(
            kernel,
            out_shape=[jax.ShapeDtypeStruct(shape, F32 if shape[1] == 128 else kind) for shape in outs],
            scratch_shapes=[pltpu.VMEM(item, F32) if isinstance(item, tuple) else item for item in scratch],
            compiler_params=pltpu.CompilerParams(vmem_limit_bytes=60 << 20),
        )(*args)

    def net_scratch(plan):
        return [(8, plan.window), (72, plan.chunk + LEAD)]

    def layers(plan):
        return [pltpu.VMEM((hid, plan.chunk), BF16)] * 2

    sweep_scratch = [pair, (2, 2, height + 2 * GUARD, 128), (2, height, 128)]

    w1, b1, w2, b2, w3, w1b, w3b = call(
        weights_kernel, [(hid, 32), (hid, 128), (hid, hid), (hid, 128), (72, hid), (72, hid), (hid, 80)], [],
        weight_one, bias_one[None, :], weight_two, bias_two[None, :], jnp.swapaxes(weight_three, 2, 3), kind=BF16,
    )
    forward_weights = (w1, b1, w2, b2, w3)
    backward_weights = (w1, b1, w2, b2, w1b, weight_two, w3b)

    lane = np.arange(near.chunk)
    place_row, place_col = lane // near.wide, lane % near.wide
    mine = (place_col >= near.rim + 1) & (place_col < near.rim + 1 + cols)
    place = jnp.asarray(np.tile(np.where(mine, place_row, -10 * height), (16, 1)), jnp.int32)

    total_cols = cols * lax.axis_size("gy")
    col_ids = lax.axis_index("gy") * cols + jnp.arange(frame[1], dtype=jnp.int32) - LEFT
    forcing = jnp.sin(col_ids.astype(F32) * (TWO_PI * FORCE_WAVES / total_cols))[None, :]

    def strips(count, rim):
        return [(count, rim, rows)] * 2

    sides = call(strips_kernel, strips(4, 32), [], velocity[0], targets[0])
    pieces = exchange([velocity[0], targets[0, step_count - 1]], sides)
    v_first, last_goal, v_second, coefs_first, error_first, loss_first = call(
        functools.partial(first_kernel, far),
        [pair, pair, pair, packed, own_pair, (1, 64)],
        [packed] + net_scratch(far) + layers(far) + sweep_scratch,
        *pieces, velocity[0], targets[0], forcing, *forward_weights,
    )
    provisional, low, high, coefs_second = call(
        functools.partial(second_kernel, near),
        [own_pair] + strips(2, 40) + [packed],
        [packed] + net_scratch(near) + layers(near),
        v_second, forcing, *forward_weights,
    )
    back_scratch = [packed, packed, packed] + sweep_scratch + [(176, 192)] + net_scratch(near)
    start_sums = jnp.pad(loss_first, ((66, 5), (64, 0)))
    grad, low, high, sums = call(
        functools.partial(back_kernel, near, True),
        [own_pair] + strips(2, 24) + [sums_shape], back_scratch,
        *exchange([provisional], (low, high)), provisional, last_goal, error_first, start_sums, v_second, coefs_second, place,
        *backward_weights,
    )
    grad, _, _, sums = call(
        functools.partial(back_kernel, near, False),
        [own_pair] + [(1, 8, 128)] * 2 + [sums_shape], back_scratch,
        *exchange([grad], (low, high)), grad, forcing, forcing, sums, v_first, coefs_first, place, *backward_weights,
    )
    for axis in ("ens", "gx", "gy"):
        sums = total_over(sums, axis)
    device_count = lax.axis_size(("ens", "gx", "gy"))
    loss_scale = 1.0 / float(step_count * 2 * rows * cols * device_count)
    d1, db1, d2, db2, d3, loss = call(
        functools.partial(finish_kernel, loss_scale),
        [(18, hid), (1, hid), (hid, hid), (1, hid), (54, hid), (1, 1)], [], sums,
    )
    return (
        d1.reshape(weight_one.shape),
        db1[0],
        d2,
        db2[0],
        d3.reshape(3, 3, nout, hid).transpose(0, 1, 3, 2),
        loss[0, 0],
        grad[None],
    )


def solution(mesh):
    return jax.shard_map(
        shards,
        mesh=mesh,
        in_specs=(P("ens", None, "gx", "gy"), P("ens", None, None, "gx", "gy"), P(), P(), P(), P(), P()),
        out_specs=(P(), P(), P(), P(), P(), P(), P("ens", None, "gx", "gy")),
        check_vma=False,
    )
```

```python
import functools

import jax
import jax.numpy as jnp
import numpy as np
from jax import lax
from jax.experimental import pallas as pl
from jax.experimental.pallas import tpu as pltpu
from jax.sharding import PartitionSpec as P

SWEEPS = 16
TIME_STEP = 0.2
VISCOSITY = 0.05
DRAG_RATE = 0.1
FORCE_WAVES = 4.0
COEF_SCALE = 0.1
EPSILON = 1e-06
OUTER_WEIGHT = -1.0 / 16.0
INNER_WEIGHT = 9.0 / 16.0
TWO_PI = 6.283185307179586

TOP = 40
LEFT = 64
CHUNK_ROWS = 16
LEAD = 384
GUARD = 8
VMEM_BYTES = 40 << 20
BF16 = jnp.bfloat16
F32 = jnp.float32


def passed_along(block, axis, distance):
    size = lax.axis_size(axis)
    route = [(i, (i + distance) % size) for i in range(size)]
    return lax.ppermute(block, axis, route)


def exchange(owns, sides):
    rim, rows = sides[0].shape[1:]
    right = passed_along(sides[0], "gy", -1)
    left = passed_along(sides[1], "gy", 1)
    edges = []
    for first, tile, distance in ((rows - rim, rows - 128, 1), (0, 0, -1)):
        mine = jnp.concatenate([own[:, first : first + rim] for own in owns], axis=0)
        parts = [mine] + [part[:, :, tile : tile + 128] for part in (left, right)]
        edges.append(passed_along(jnp.concatenate(parts, axis=1), "gx", distance))
    return [left, right] + edges


def side_strips(field, rim):
    turned = field.T
    return turned[:rim], turned[turned.shape[0] - rim :]


def spread_out(middle, left, right, rows):
    rim = left.shape[0]
    lanes = left.shape[1]
    before = jnp.concatenate([jnp.zeros((LEFT - rim, lanes), F32), left, jnp.zeros((128 - LEFT, lanes), F32)], axis=0).T
    after = jnp.concatenate([jnp.zeros((LEFT, lanes), F32), right, jnp.zeros((128 - LEFT - rim, lanes), F32)], axis=0).T
    turned = pltpu.roll(middle, LEFT, 1)
    first_half = lax.broadcasted_iota(jnp.int32, middle.shape, 1) < LEFT
    return jnp.concatenate(
        [jnp.where(first_half, before[rows], turned), jnp.where(first_half, turned, after[rows])], axis=1
    )


def build_frame(own, pieces, comp, target_ref, target):
    left_ref, right_ref, above_ref, below_ref = pieces
    rim = left_ref.shape[1]
    rows = own.shape[0]
    if rim < TOP:
        target_ref[target, : TOP - rim] = jnp.zeros((TOP - rim, 256), F32)
        target_ref[target, TOP + rows + rim :] = jnp.zeros((TOP - rim, 256), F32)
    target_ref[target, TOP : TOP + rows] = spread_out(
        own, left_ref[comp], right_ref[comp], slice(0, rows)
    )
    for ref, first, kept in ((above_ref, TOP - rim, slice(128 - rim, 128)), (below_ref, TOP + rows, slice(0, rim))):
        target_ref[target, first : first + rim] = spread_out(
            ref[comp, :rim], ref[comp, rim : 2 * rim], ref[comp, 2 * rim :], kept
        )


def total_over(value, axis):
    size = lax.axis_size(axis)
    if size <= 4:
        moved = [passed_along(value, axis, distance) for distance in range(1, size)]
        for other in moved:
            value = value + other
        return value
    return lax.psum(value, axis)


def at(field, rows, cols):
    if rows:
        field = pltpu.roll(field, (-rows) % field.shape[0], 0)
    if cols:
        field = pltpu.roll(field, (-cols) % field.shape[1], 1)
    return field


def project(first, second, buffers, rhs_ref, rim):
    height = first.shape[0]
    quarter = -0.125 * (at(first, 1, 0) - at(first, -1, 0) + at(second, 0, 1) - at(second, 0, -1))
    for half in range(2):
        part = quarter[:, 128 * half : 128 * half + 128]
        rhs_ref[half] = part
        for buffer in range(2):
            buffers[buffer, half, :GUARD] = jnp.zeros((GUARD, 128), F32)
            buffers[buffer, half, GUARD + height :] = jnp.zeros((GUARD, 128), F32)
            buffers[buffer, half, GUARD : GUARD + height] = part
    lane = lax.broadcasted_iota(jnp.int32, (8, 128), 1)
    at_start = lane == 0
    at_end = lane == 127

    def one_sweep(source, target):
        for row in range(TOP - rim, height - TOP + rim, 8):
            here = [buffers[source, half, GUARD + row : GUARD + row + 8] for half in range(2)]
            ahead = [pltpu.roll(part, 127, 1) for part in here]
            behind = [pltpu.roll(part, 1, 1) for part in here]
            for half in range(2):
                above = buffers[source, half, GUARD + row - 1 : GUARD + row + 7]
                below = buffers[source, half, GUARD + row + 1 : GUARD + row + 9]
                east = jnp.where(at_end, ahead[1 - half], ahead[half])
                west = jnp.where(at_start, behind[1 - half], behind[half])
                near = (above + below) + (east + west)
                buffers[target, half, GUARD + row : GUARD + row + 8] = 0.25 * near + rhs_ref[half, row : row + 8]

    def two_sweeps(index, carried):
        one_sweep(0, 1)
        one_sweep(1, 0)
        return carried

    lax.fori_loop(0, SWEEPS // 2, two_sweeps, 0)
    p = jnp.concatenate([buffers[0, half, GUARD : GUARD + height] for half in range(2)], axis=1)
    above = jnp.concatenate([buffers[0, half, GUARD - 1 : GUARD - 1 + height] for half in range(2)], axis=1)
    below = jnp.concatenate([buffers[0, half, GUARD + 1 : GUARD + 1 + height] for half in range(2)], axis=1)
    return first - 0.5 * (below - above), second - 0.5 * (at(p, 0, 1) - at(p, 0, -1))


def faces(field, c0, c1, c2, move):
    return (
        (OUTER_WEIGHT + c0) * move(field, -1)
        + (INNER_WEIGHT + c1) * field
        + (INNER_WEIGHT + c2) * move(field, 1)
        + (OUTER_WEIGHT - c0 - c1 - c2) * move(field, 2)
    )


def by_row(field, distance):
    return at(field, distance, 0)


def by_col(field, distance):
    return at(field, 0, distance)


def advect(v, coefs, forcing):
    speed_rows = 0.5 * (v[0] + by_row(v[0], 1))
    speed_cols = 0.5 * (v[1] + by_col(v[1], 1))
    results = []
    for comp in range(2):
        q = v[comp]
        flux = speed_rows * faces(q, coefs[0], coefs[1], coefs[2], by_row)
        change = flux - by_row(flux, -1)
        flux = speed_cols * faces(q, coefs[3], coefs[4], coefs[5], by_col)
        change = change + (flux - by_col(flux, -1))
        laplace = by_row(q, 1) + by_row(q, -1) + by_col(q, 1) + by_col(q, -1) - 4.0 * q
        drive = VISCOSITY * laplace - DRAG_RATE * q
        if comp == 0:
            drive = drive + forcing
        results.append(q - TIME_STEP * change + TIME_STEP * drive)
    return results


def advect_back(v, coefs, g, keep_taps):
    results = [None, None]
    for axis in range(2):
        move = by_row if axis == 0 else by_col
        speed = 0.5 * (v[axis] + move(v[axis], 1))
        c0, c1, c2 = coefs[3 * axis : 3 * axis + 3]
        grads = []
        grad_speed = None
        taps = None
        for comp in range(2):
            q = v[comp]
            grad_flux = TIME_STEP * (move(g[comp], 1) - g[comp])
            term = grad_flux * faces(q, c0, c1, c2, move)
            grad_speed = term if grad_speed is None else grad_speed + term
            grad_face = grad_flux * speed
            behind = move(q, -1)
            ahead = move(q, 1)
            far = move(q, 2)
            new = (grad_face * (behind - far), grad_face * (q - far), grad_face * (ahead - far))
            taps = new if taps is None else tuple(a + b for a, b in zip(taps, new))
            grads.append(
                move(grad_face * (OUTER_WEIGHT + c0), 1)
                + grad_face * (INNER_WEIGHT + c1)
                + move(grad_face * (INNER_WEIGHT + c2), -1)
                + move(grad_face * (OUTER_WEIGHT - c0 - c1 - c2), -2)
            )
        grads[axis] = grads[axis] + 0.5 * (grad_speed + move(grad_speed, -1))
        for number in range(3):
            keep_taps(3 * axis + number, COEF_SCALE * taps[number])
        for comp in range(2):
            results[comp] = grads[comp] if axis == 0 else results[comp] + grads[comp]
    for comp in range(2):
        near = by_row(g[comp], 1) + by_row(g[comp], -1) + by_col(g[comp], 1) + by_col(g[comp], -1)
        drive = VISCOSITY * (near - 4.0 * g[comp]) - DRAG_RATE * g[comp]
        results[comp] = results[comp] + g[comp] + TIME_STEP * drive
    return results


class Plan:
    def __init__(self, rows, cols, rim):
        self.rows, self.cols, self.rim = rows, cols, rim
        self.wide = -(-(cols + 2 * rim + 4) // 8) * 8
        self.chunk = CHUNK_ROWS * self.wide
        self.chunks = -(-(rows + 2 * rim + 2) // CHUNK_ROWS)
        self.offsets = [row * self.wide + col for row in range(3) for col in range(3)]
        self.in_row, self.in_lane = TOP - rim - 2, LEFT - rim - 2
        self.out_row, self.out_lane = TOP - rim, LEFT - rim
        self.window = -(-(CHUNK_ROWS + 2) * self.wide // 128) * 128


def rounded(field):
    return field.astype(BF16).astype(F32)


def shifted(block, offset, length):
    if offset % block.shape[1]:
        block = pltpu.roll(block, (-offset) % block.shape[1], 1)
    return block[:, :length]


def lay_rows(source_ref, first_row, lane, wide, target_ref):
    lanes = lax.broadcasted_iota(jnp.int32, (8, 128), 1)
    tiles = {}
    for number in range(CHUNK_ROWS + 2):
        place = pl.ds(pl.multiple_of(8 * (first_row + number), 8), 8)
        block = jnp.concatenate([source_ref[half, place] for half in range(2)], axis=1)
        start = number * wide
        tile, offset = start // 128, start % 128
        block = pltpu.roll(block, (offset - lane) % 256, 1)
        for part in range(-(-(offset + wide) // 128)):
            piece = block[:, 128 * (part % 2) : 128 * (part % 2) + 128]
            if part == 0 and offset:
                piece = jnp.where(lanes < offset, tiles[tile], piece)
            tiles[tile + part] = piece
    for tile in range(target_ref.shape[1] // 128):
        target_ref[:, 128 * tile : 128 * tile + 128] = tiles[tile]


def split_rows(flat, target_ref, first_row, lane, wide):
    for number in range(CHUNK_ROWS):
        start = number * wide
        tile, offset = start // 128, start % 128
        parts = max(2, -(-(offset + wide) // 128))
        if tile + parts > flat.shape[1] // 128:
            tile, offset = tile - 1, offset + 128
        block = flat[:, 128 * tile : 128 * (tile + parts)]
        block = shifted(block, offset - lane, 256)
        place = pl.ds(pl.multiple_of(8 * (first_row + number), 8), 8)
        for half in range(2):
            target_ref[half, place] = block[:, 128 * half : 128 * half + 128]


def channel(ref, number, first_row, rows):
    place = pl.ds(8 * first_row + number, rows, stride=8)
    return jnp.concatenate([ref[half, place] for half in range(2)], axis=1)


def keep_channel(ref, number, first_row, field):
    place = pl.ds(8 * first_row + number, field.shape[0], stride=8)
    for half in range(2):
        ref[half, place] = field[:, 128 * half : 128 * half + 128]


def keep_inputs(v, inputs_ref):
    inputs_ref[...] = jnp.zeros_like(inputs_ref)
    for comp in range(2):
        field = rounded(v[comp])
        for col in range(3):
            keep_channel(inputs_ref, 2 * col + comp, 0, by_col(field, col))
    keep_channel(inputs_ref, 6, 0, jnp.ones_like(v[0]))


def product(left, right):
    return lax.dot_general(left, right, (((1,), (0,)), ((), ())), preferred_element_type=F32)


def product_over_cells(left, right):
    return lax.dot_general(left, right, (((1,), (1,)), ((), ())), preferred_element_type=F32)


def columns(plan, row, inputs_ref, window_ref):
    lay_rows(inputs_ref, plan.in_row + row, plan.in_lane, plan.wide, window_ref)
    window = window_ref[...]
    parts = [shifted(window, row * plan.wide, plan.chunk) for row in range(3)]
    return jnp.concatenate(parts + [jnp.zeros((8, plan.chunk), F32)], axis=0)


def add_taps(terms_ref, offsets, length):
    total = None
    for tap, offset in enumerate(offsets):
        term = shifted(terms_ref[8 * tap : 8 * tap + 8, :], offset, length)
        total = term if total is None else total + term
    return total


def before_silu(weight_ref, inputs, bias_ref):
    bias = jnp.concatenate([bias_ref[...]] * (inputs.shape[1] // 128), axis=1)
    return product(weight_ref[...], inputs) + bias


def network(plan, inputs_ref, weight_refs, coefs_ref, window_ref, terms_ref, one_ref, two_ref):
    w1_ref, b1_ref, w2_ref, b2_ref, w3_ref = weight_refs
    terms_ref[...] = jnp.zeros_like(terms_ref)
    one_ref[...] = jnp.zeros_like(one_ref)
    two_ref[...] = jnp.zeros_like(two_ref)
    lag = LEAD - 2 * plan.wide

    def one_turn(turn, carried):
        last = jnp.maximum(turn - 2, 0)
        terms_ref[:, :LEAD] = terms_ref[:, plan.chunk :]
        cols = columns(plan, CHUNK_ROWS * jnp.minimum(turn, plan.chunks - 1), inputs_ref, window_ref).astype(BF16)
        terms_ref[:, LEAD:] = product(w3_ref[...], two_ref[...])
        half = before_silu(w2_ref, one_ref[...], b2_ref)
        two_ref[...] = (half * jnp.tanh(half) + half).astype(BF16)
        half = before_silu(w1_ref, cols, b1_ref)
        one_ref[...] = (half * jnp.tanh(half) + half).astype(BF16)
        total = COEF_SCALE * add_taps(terms_ref, [offset + lag for offset in plan.offsets], plan.chunk)
        split_rows(total, coefs_ref, plan.out_row - 2 + CHUNK_ROWS * last, plan.out_lane, plan.wide)
        return carried

    lax.fori_loop(0, plan.chunks + 2, one_turn, 0)


def with_slope(half):
    bend = jnp.tanh(half)
    return half * bend + half, (0.5 + 0.5 * bend) * (1.0 + half * (1.0 - bend))


def network_back(plan, inputs_ref, taps_ref, weight_refs, place_ref, grads_ref, sums_ref, net_refs):
    w1_ref, b1_ref, w2_ref, b2_ref, w1b_ref, w2b_ref, w3b_ref = weight_refs
    cross_ref, window_ref, terms_ref = net_refs
    terms_ref[...] = jnp.zeros_like(terms_ref)
    cross_ref[...] = jnp.zeros_like(cross_ref)

    def one_chunk(step, carried):
        row = CHUNK_ROWS * step
        place = place_ref[...] + row
        own = jnp.where((place >= plan.rim + 1) & (place < plan.rim + 1 + plan.rows), 1.0, 0.0).astype(BF16)
        own = jnp.concatenate([own] * 4, axis=0)
        cols = columns(plan, row, inputs_ref, window_ref).astype(BF16)
        hidden, slope_one = with_slope(before_silu(w1_ref, cols, b1_ref))
        hidden_one = hidden.astype(BF16)
        hidden, slope_two = with_slope(before_silu(w2_ref, hidden_one, b2_ref))
        hidden_two = hidden.astype(BF16)
        lay_rows(taps_ref, plan.out_row - 2 + row, plan.out_lane, plan.wide, window_ref)
        window = window_ref[...]
        parts = [shifted(window, 2 * plan.wide - offset, plan.chunk) for offset in plan.offsets]
        spread = jnp.concatenate(parts + [jnp.zeros((8, plan.chunk), F32)], axis=0).astype(BF16)
        grad_two = (product(w3b_ref[...], spread) * slope_two).astype(BF16)
        grad_one = (product(w2b_ref[...], grad_two) * slope_one).astype(BF16)
        left = jnp.concatenate([spread, hidden_one, cols], axis=0)
        right = jnp.concatenate([hidden_two * own, grad_two * own, grad_one * own], axis=0)
        cross_ref[...] += product_over_cells(left, right)
        terms_ref[:, :LEAD] = terms_ref[:, plan.chunk :]
        terms_ref[:, LEAD:] = product(w1b_ref[...], grad_one)
        total = add_taps(terms_ref, [LEAD - offset for offset in plan.offsets], plan.chunk)
        split_rows(total, grads_ref, plan.in_row + row, plan.in_lane, plan.wide)
        return carried

    lax.fori_loop(0, plan.chunks // 2, lambda pair, carried: one_chunk(2 * pair + 1, one_chunk(2 * pair, carried)), 0)
    if plan.chunks % 2:
        one_chunk(plan.chunks - 1, 0)
    for tap in range(9):
        taken = 144 + 8 * (tap // 3) + 2 * (tap % 3)
        sums_ref[8 * tap : 8 * tap + 6, :64] += cross_ref[8 * tap : 8 * tap + 6, :64]
        sums_ref[8 * tap + 6 : 8 * tap + 8, :64] += cross_ref[taken : taken + 2, 128:192]
    sums_ref[:64, 64:] += cross_ref[80:144, 64:128]
    sums_ref[64:65, 64:] += cross_ref[150:151, 128:192]
    sums_ref[65:66, 64:] += cross_ref[150:151, 64:128]


def own_part(field, rows, cols, first_row):
    return pltpu.roll(field[TOP - first_row : TOP - first_row + rows], 256 - LEFT, 1)[:, :cols]


def lane_sums(squares):
    return jnp.sum(squares, axis=0, keepdims=True)


def strips_kernel(v_ref, goals_ref, low_ref, high_ref):
    rim = low_ref.shape[1]
    for number in range(4):
        field = v_ref[number] if number < 2 else goals_ref[goals_ref.shape[0] - 1, number - 2]
        low_ref[number], high_ref[number] = side_strips(field, rim)


def weights_kernel(w1_in, b1_in, w2_in, b2_in, w3_in, w1, b1, w2, b2, w3, w1b, w3b):
    hid = b1_in.shape[1]
    ahead, wide, back = [], [], []
    for row in range(3):
        parts = [w1_in[row, col].astype(F32) for col in range(3)]
        ahead += parts + [jnp.zeros((2, hid), F32)]
        for col in range(3):
            wide += [parts[col], jnp.zeros((6, hid), F32)]
            back += [w3_in[row, col].astype(F32), jnp.zeros((2, hid), F32)]
    ahead = jnp.concatenate(ahead + [jnp.zeros((8, hid), F32)], axis=0)
    back = jnp.concatenate(back, axis=0)
    w1[...] = (0.5 * ahead).T.astype(BF16)
    w1b[...] = jnp.concatenate(wide, axis=0).astype(BF16)
    w2[...] = (0.5 * w2_in[...].astype(F32)).T.astype(BF16)
    w3[...] = back.astype(BF16)
    w3b[...] = jnp.concatenate([back, jnp.zeros((8, hid), F32)], axis=0).T.astype(BF16)
    for source, target in ((b1_in, b1), (b2_in, b2)):
        target[...] = jnp.broadcast_to(0.5 * source[...], (128, hid)).T


def first_kernel(plan, left, right, above, below, own_ref, goals_ref, force_ref, w1, b1, w2, b2, w3,
                 v_ref, last_goal_ref, v_out, coefs_ref, error_ref, loss_ref, inputs_ref, window_ref, terms_ref, one_ref, two_ref, frame_ref, buffers, rhs_ref):
    pieces = (left, right, above, below)
    for comp in range(2):
        build_frame(own_ref[comp], pieces, comp, v_ref, comp)
        build_frame(goals_ref[goals_ref.shape[0] - 1, comp], pieces, comp + 2, last_goal_ref, comp)
    keep_inputs([v_ref[0], v_ref[1]], inputs_ref)
    coefs_ref[...] = jnp.zeros_like(coefs_ref)
    network(plan, inputs_ref, (w1, b1, w2, b2, w3), coefs_ref, window_ref, terms_ref, one_ref, two_ref)
    height = v_ref.shape[1]
    result = advect(
        [v_ref[0], v_ref[1]], [channel(coefs_ref, number, 0, height) for number in range(6)], force_ref[...]
    )
    for comp in range(2):
        frame_ref[comp] = result[comp]
    result = project(frame_ref[0], frame_ref[1], buffers, rhs_ref, 24)
    loss = None
    for comp in range(2):
        v_out[comp] = result[comp]
        error = own_part(result[comp], plan.rows, plan.cols, 0) - goals_ref[0, comp]
        error_ref[comp] = error
        square = lane_sums(error * error)
        loss = square if loss is None else loss + square
    loss_ref[...] = loss[:, :64] + loss[:, 64:]


def second_kernel(plan, v_ref, force_ref, w1, b1, w2, b2, w3, out_ref, low_ref, high_ref, coefs_ref, inputs_ref, window_ref,
                  terms_ref, one_ref, two_ref):
    keep_inputs([v_ref[0], v_ref[1]], inputs_ref)
    coefs_ref[...] = jnp.zeros_like(coefs_ref)
    network(plan, inputs_ref, (w1, b1, w2, b2, w3), coefs_ref, window_ref, terms_ref, one_ref, two_ref)
    low, tall = TOP - 8, plan.rows + 16
    v = [v_ref[comp, low : low + tall] for comp in range(2)]
    result = advect(v, [channel(coefs_ref, number, low, tall) for number in range(6)], force_ref[...])
    for comp in range(2):
        mine = own_part(result[comp], plan.rows, plan.cols, low)
        out_ref[comp] = mine
        low_ref[comp], high_ref[comp] = side_strips(mine, low_ref.shape[1])


def back_kernel(plan, last, left, right, above, below, own_ref, goal_ref, extra_ref, before_ref, v_ref, coefs_ref,
                place_ref, w1, b1, w2, b2, w1b, w2b, w3b, out_ref, low_ref, high_ref, sums_ref, inputs_ref, taps_ref, grads_ref, frame_ref, buffers, rhs_ref, *net_refs):
    rows, cols = plan.rows, plan.cols
    if last:
        sums_ref[...] = jnp.zeros_like(sums_ref)
        sums_ref[66:67, 64:] = before_ref[...]
    else:
        sums_ref[...] = before_ref[...]
    for comp in range(2):
        build_frame(own_ref[comp], (left, right, above, below), comp, frame_ref, comp)
    first, second = project(frame_ref[0], frame_ref[1], buffers, rhs_ref, TOP if last else 24)
    if last:
        errors = (first - goal_ref[0], second - goal_ref[1])
        for error in errors:
            mine = own_part(error, rows, cols, 0)
            loss = lane_sums(mine * mine)
            sums_ref[66:67, 64:] += loss[:, :64] + loss[:, 64:]
        for comp in range(2):
            frame_ref[comp] = errors[comp]
        first, second = project(frame_ref[0], frame_ref[1], buffers, rhs_ref, 24)
    frame_ref[0] = first
    frame_ref[1] = second
    keep_inputs([v_ref[0], v_ref[1]], inputs_ref)
    taps_ref[...] = jnp.zeros_like(taps_ref)
    low, tall = TOP - 8, rows + 16
    result = advect_back(
        [v_ref[comp, low : low + tall] for comp in range(2)],
        [channel(coefs_ref, number, low, tall) for number in range(6)],
        [frame_ref[comp, low : low + tall] for comp in range(2)],
        lambda number, field: keep_channel(taps_ref, number, low, rounded(field)),
    )
    for comp in range(2):
        frame_ref[comp, low : low + tall] = result[comp]
    weight_refs = (w1, b1, w2, b2, w1b, w2b, w3b)
    network_back(plan, inputs_ref, taps_ref, weight_refs, place_ref, grads_ref, sums_ref, net_refs)
    for comp in range(2):
        field = frame_ref[comp, low : low + tall] + channel(grads_ref, comp, low, tall)
        total = own_part(field, rows, cols, low)
        if last:
            total = total + extra_ref[comp]
            low_ref[comp], high_ref[comp] = side_strips(total, low_ref.shape[1])
        out_ref[comp] = total
    if not last:
        low_ref[...] = jnp.zeros_like(low_ref)
        high_ref[...] = jnp.zeros_like(high_ref)


def scaled(piece, count):
    return piece * (1.0 / jnp.sqrt(jnp.sum(piece * piece) / count + EPSILON))


def finish_kernel(loss_scale, in_ref, w1_ref, b1_ref, w2_ref, b2_ref, w3_ref, loss_ref):
    one = jnp.concatenate([in_ref[8 * tap + 6 : 8 * tap + 8, :64] for tap in range(9)], axis=0)
    three = jnp.concatenate([in_ref[8 * tap : 8 * tap + 6, :64] for tap in range(9)], axis=0)
    one, three = scaled(one, one.size), scaled(three, three.size)
    for tap in range(9):
        w1_ref[tap // 3, tap % 3] = one[2 * tap : 2 * tap + 2]
        w3_ref[tap // 3, tap % 3] = three[6 * tap : 6 * tap + 6]
    b1_ref[...] = scaled(in_ref[64:65, 64:], 64)
    b2_ref[...] = scaled(in_ref[65:66, 64:], 64)
    w2_ref[...] = scaled(in_ref[:64, 64:], 64 * 64)
    loss_ref[...] = (0.5 * loss_scale) * jnp.sum(in_ref[66:67, 64:], axis=1, keepdims=True)


def shards(velocity, targets, weight_one, bias_one, weight_two, bias_two, weight_three):
    rows, cols = velocity.shape[2], velocity.shape[3]
    step_count = targets.shape[1]
    height = rows + 2 * TOP
    frame = (height, cols + 2 * LEFT)
    pair = (2,) + frame
    own_pair = (2, rows, cols)
    packed = (2, 8 * height, 128)
    sums_shape = (72, 128)
    hid = weight_two.shape[0]
    nout = weight_three.shape[3]
    near = Plan(rows, cols, 2)
    far = Plan(rows, cols, 23)

    def call(kernel, outs, scratch, *args, kind=F32):
        return pl.pallas_call(
            kernel,
            out_shape=[jax.ShapeDtypeStruct(shape, F32 if shape[1] == 128 else kind) for shape in outs],
            scratch_shapes=[pltpu.VMEM(item, F32) if isinstance(item, tuple) else item for item in scratch],
            compiler_params=pltpu.CompilerParams(vmem_limit_bytes=VMEM_BYTES),
        )(*args)

    def net_scratch(plan):
        return [(8, plan.window), (72, plan.chunk + LEAD)]

    def layers(plan):
        return [pltpu.VMEM((hid, plan.chunk), BF16)] * 2

    sweep_scratch = [pair, (2, 2, height + 2 * GUARD, 128), (2, height, 128)]

    w1, b1, w2, b2, w3, w1b, w3b = call(
        weights_kernel, [(hid, 32), (hid, 128), (hid, hid), (hid, 128), (72, hid), (72, hid), (hid, 80)], [],
        weight_one, bias_one[None, :], weight_two, bias_two[None, :], jnp.swapaxes(weight_three, 2, 3), kind=BF16,
    )
    forward_weights = (w1, b1, w2, b2, w3)
    backward_weights = (w1, b1, w2, b2, w1b, weight_two, w3b)

    lane = np.arange(near.chunk)
    place_row, place_col = lane // near.wide, lane % near.wide
    mine = (place_col >= near.rim + 1) & (place_col < near.rim + 1 + cols)
    place = jnp.asarray(np.tile(np.where(mine, place_row, -10 * height), (16, 1)), jnp.int32)

    total_cols = cols * lax.axis_size("gy")
    col_ids = lax.axis_index("gy") * cols + jnp.arange(frame[1], dtype=jnp.int32) - LEFT
    forcing = jnp.sin(col_ids.astype(F32) * (TWO_PI * FORCE_WAVES / total_cols))[None, :]

    def strips(count, rim):
        return [(count, rim, rows)] * 2

    sides = call(strips_kernel, strips(4, 32), [], velocity[0], targets[0])
    pieces = exchange([velocity[0], targets[0, step_count - 1]], sides)
    v_first, last_goal, v_second, coefs_first, error_first, loss_first = call(
        functools.partial(first_kernel, far),
        [pair, pair, pair, packed, own_pair, (1, 64)],
        [packed] + net_scratch(far) + layers(far) + sweep_scratch,
        *pieces, velocity[0], targets[0], forcing, *forward_weights,
    )
    provisional, low, high, coefs_second = call(
        functools.partial(second_kernel, near),
        [own_pair] + strips(2, 40) + [packed],
        [packed] + net_scratch(near) + layers(near),
        v_second, forcing, *forward_weights,
    )
    back_scratch = [packed, packed, packed] + sweep_scratch + [(176, 192)] + net_scratch(near)
    grad, low, high, sums = call(
        functools.partial(back_kernel, near, True),
        [own_pair] + strips(2, 24) + [sums_shape], back_scratch,
        *exchange([provisional], (low, high)), provisional, last_goal, error_first, loss_first, v_second, coefs_second, place,
        *backward_weights,
    )
    grad, _, _, sums = call(
        functools.partial(back_kernel, near, False),
        [own_pair] + [(1, 8, 128)] * 2 + [sums_shape], back_scratch,
        *exchange([grad], (low, high)), grad, forcing, forcing, sums, v_first, coefs_first, place, *backward_weights,
    )
    for axis in ("ens", "gx", "gy"):
        sums = total_over(sums, axis)
    device_count = lax.axis_size(("ens", "gx", "gy"))
    loss_scale = 1.0 / float(step_count * 2 * rows * cols * device_count)
    d1, db1, d2, db2, d3, loss = call(
        functools.partial(finish_kernel, loss_scale),
        [(3, 3, 2, hid), (1, hid), (hid, hid), (1, hid), (3, 3, nout, hid), (1, 1)], [], sums,
    )
    return (
        d1,
        db1[0],
        d2,
        db2[0],
        jnp.swapaxes(d3, 2, 3),
        loss[0, 0],
        grad[None],
    )


def solution(mesh):
    return jax.shard_map(
        shards,
        mesh=mesh,
        in_specs=(P("ens", None, "gx", "gy"), P("ens", None, None, "gx", "gy"), P(), P(), P(), P(), P()),
        out_specs=(P(), P(), P(), P(), P(), P(), P("ens", None, "gx", "gy")),
        check_vma=False,
    )
```

```python
import functools

import jax
import jax.numpy as jnp
import numpy as np
from jax import lax
from jax.experimental import pallas as pl
from jax.experimental.pallas import tpu as pltpu
from jax.sharding import PartitionSpec as P

SWEEPS = 16
TIME_STEP = 0.2
VISCOSITY = 0.05
DRAG_RATE = 0.1
FORCE_WAVES = 4.0
COEF_SCALE = 0.1
EPSILON = 1e-06
OUTER_WEIGHT = -1.0 / 16.0
INNER_WEIGHT = 9.0 / 16.0
TWO_PI = 6.283185307179586

TOP = 40
LEFT = 64
CHUNK_ROWS = 16
LEAD = 384
GUARD = 8
GROUP = 4
VMEM_BYTES = 40 << 20
BF16 = jnp.bfloat16
F32 = jnp.float32


def passed_along(block, axis, distance):
    size = lax.axis_size(axis)
    route = [(i, (i + distance) % size) for i in range(size)]
    return lax.ppermute(block, axis, route)


def exchange(owns, sides):
    rim, rows = sides[0].shape[1:]
    right = passed_along(sides[0], "gy", -1)
    left = passed_along(sides[1], "gy", 1)
    edges = []
    for first, tile, distance in ((rows - rim, rows - 128, 1), (0, 0, -1)):
        mine = jnp.concatenate([own[:, first : first + rim] for own in owns], axis=0)
        parts = [mine] + [part[:, :, tile : tile + 128] for part in (left, right)]
        edges.append(passed_along(jnp.concatenate(parts, axis=1), "gx", distance))
    return [left, right] + edges


def side_strips(field, rim):
    turned = field.T
    return turned[:rim], turned[turned.shape[0] - rim :]


def spread_out(middle, left, right, rows):
    rim = left.shape[0]
    lanes = left.shape[1]
    before = jnp.concatenate([jnp.zeros((LEFT - rim, lanes), F32), left, jnp.zeros((128 - LEFT, lanes), F32)], axis=0).T
    after = jnp.concatenate([jnp.zeros((LEFT, lanes), F32), right, jnp.zeros((128 - LEFT - rim, lanes), F32)], axis=0).T
    turned = pltpu.roll(middle, LEFT, 1)
    first_half = lax.broadcasted_iota(jnp.int32, middle.shape, 1) < LEFT
    return jnp.concatenate(
        [jnp.where(first_half, before[rows], turned), jnp.where(first_half, turned, after[rows])], axis=1
    )


def build_frame(own, pieces, comp, target_ref, target):
    left_ref, right_ref, above_ref, below_ref = pieces
    rim = left_ref.shape[1]
    rows = own.shape[0]
    if rim < TOP:
        target_ref[target, : TOP - rim] = jnp.zeros((TOP - rim, 256), F32)
        target_ref[target, TOP + rows + rim :] = jnp.zeros((TOP - rim, 256), F32)
    target_ref[target, TOP : TOP + rows] = spread_out(
        own, left_ref[comp], right_ref[comp], slice(0, rows)
    )
    for ref, first, kept in ((above_ref, TOP - rim, slice(128 - rim, 128)), (below_ref, TOP + rows, slice(0, rim))):
        target_ref[target, first : first + rim] = spread_out(
            ref[comp, :rim], ref[comp, rim : 2 * rim], ref[comp, 2 * rim :], kept
        )


def total_over(value, axis):
    size = lax.axis_size(axis)
    if size <= 4:
        moved = [passed_along(value, axis, distance) for distance in range(1, size)]
        for other in moved:
            value = value + other
        return value
    return lax.psum(value, axis)


def at(field, rows, cols):
    if rows:
        field = pltpu.roll(field, (-rows) % field.shape[0], 0)
    if cols:
        field = pltpu.roll(field, (-cols) % field.shape[1], 1)
    return field


def project(first, second, buffers, rhs_ref, rim):
    height = first.shape[0]
    quarter = -0.125 * (at(first, 1, 0) - at(first, -1, 0) + at(second, 0, 1) - at(second, 0, -1))
    for half in range(2):
        part = quarter[:, 128 * half : 128 * half + 128]
        rhs_ref[half] = part
        for buffer in range(2):
            buffers[buffer, half, :GUARD] = jnp.zeros((GUARD, 128), F32)
            buffers[buffer, half, GUARD + height :] = jnp.zeros((GUARD, 128), F32)
            buffers[buffer, half, GUARD : GUARD + height] = part
    lane = lax.broadcasted_iota(jnp.int32, (8, 128), 1)
    at_start = lane == 0
    at_end = lane == 127

    def one_sweep(source, target):
        for row in range(TOP - rim, height - TOP + rim, 8):
            here = [buffers[source, half, GUARD + row : GUARD + row + 8] for half in range(2)]
            ahead = [pltpu.roll(part, 127, 1) for part in here]
            behind = [pltpu.roll(part, 1, 1) for part in here]
            for half in range(2):
                above = buffers[source, half, GUARD + row - 1 : GUARD + row + 7]
                below = buffers[source, half, GUARD + row + 1 : GUARD + row + 9]
                east = jnp.where(at_end, ahead[1 - half], ahead[half])
                west = jnp.where(at_start, behind[1 - half], behind[half])
                near = (above + below) + (east + west)
                buffers[target, half, GUARD + row : GUARD + row + 8] = 0.25 * near + rhs_ref[half, row : row + 8]

    def two_sweeps(index, carried):
        one_sweep(0, 1)
        one_sweep(1, 0)
        return carried

    lax.fori_loop(0, SWEEPS // 2, two_sweeps, 0)
    p = jnp.concatenate([buffers[0, half, GUARD : GUARD + height] for half in range(2)], axis=1)
    above = jnp.concatenate([buffers[0, half, GUARD - 1 : GUARD - 1 + height] for half in range(2)], axis=1)
    below = jnp.concatenate([buffers[0, half, GUARD + 1 : GUARD + 1 + height] for half in range(2)], axis=1)
    return first - 0.5 * (below - above), second - 0.5 * (at(p, 0, 1) - at(p, 0, -1))


def faces(field, c0, c1, c2, move):
    return (
        (OUTER_WEIGHT + c0) * move(field, -1)
        + (INNER_WEIGHT + c1) * field
        + (INNER_WEIGHT + c2) * move(field, 1)
        + (OUTER_WEIGHT - c0 - c1 - c2) * move(field, 2)
    )


def by_row(field, distance):
    return at(field, distance, 0)


def by_col(field, distance):
    return at(field, 0, distance)


def advect(v, coefs, forcing):
    speed_rows = 0.5 * (v[0] + by_row(v[0], 1))
    speed_cols = 0.5 * (v[1] + by_col(v[1], 1))
    results = []
    for comp in range(2):
        q = v[comp]
        flux = speed_rows * faces(q, coefs[0], coefs[1], coefs[2], by_row)
        change = flux - by_row(flux, -1)
        flux = speed_cols * faces(q, coefs[3], coefs[4], coefs[5], by_col)
        change = change + (flux - by_col(flux, -1))
        laplace = by_row(q, 1) + by_row(q, -1) + by_col(q, 1) + by_col(q, -1) - 4.0 * q
        drive = VISCOSITY * laplace - DRAG_RATE * q
        if comp == 0:
            drive = drive + forcing
        results.append(q - TIME_STEP * change + TIME_STEP * drive)
    return results


def advect_back(v, coefs, g, keep_taps):
    results = [None, None]
    for axis in range(2):
        move = by_row if axis == 0 else by_col
        speed = 0.5 * (v[axis] + move(v[axis], 1))
        c0, c1, c2 = coefs[3 * axis : 3 * axis + 3]
        grads = []
        grad_speed = None
        taps = None
        for comp in range(2):
            q = v[comp]
            grad_flux = TIME_STEP * (move(g[comp], 1) - g[comp])
            term = grad_flux * faces(q, c0, c1, c2, move)
            grad_speed = term if grad_speed is None else grad_speed + term
            grad_face = grad_flux * speed
            behind = move(q, -1)
            ahead = move(q, 1)
            far = move(q, 2)
            new = (grad_face * (behind - far), grad_face * (q - far), grad_face * (ahead - far))
            taps = new if taps is None else tuple(a + b for a, b in zip(taps, new))
            grads.append(
                move(grad_face * (OUTER_WEIGHT + c0), 1)
                + grad_face * (INNER_WEIGHT + c1)
                + move(grad_face * (INNER_WEIGHT + c2), -1)
                + move(grad_face * (OUTER_WEIGHT - c0 - c1 - c2), -2)
            )
        grads[axis] = grads[axis] + 0.5 * (grad_speed + move(grad_speed, -1))
        for number in range(3):
            keep_taps(3 * axis + number, COEF_SCALE * taps[number])
        for comp in range(2):
            results[comp] = grads[comp] if axis == 0 else results[comp] + grads[comp]
    for comp in range(2):
        near = by_row(g[comp], 1) + by_row(g[comp], -1) + by_col(g[comp], 1) + by_col(g[comp], -1)
        drive = VISCOSITY * (near - 4.0 * g[comp]) - DRAG_RATE * g[comp]
        results[comp] = results[comp] + g[comp] + TIME_STEP * drive
    return results


class Plan:
    def __init__(self, rows, cols, rim):
        self.rows, self.cols, self.rim = rows, cols, rim
        self.wide = -(-(cols + 2 * rim + 4) // 8) * 8
        self.chunk = CHUNK_ROWS * self.wide
        self.chunks = -(-(rows + 2 * rim + 2) // CHUNK_ROWS)
        self.offsets = [row * self.wide + col for row in range(3) for col in range(3)]
        self.in_row, self.in_lane = TOP - rim - 2, LEFT - rim - 2
        self.out_row, self.out_lane = TOP - rim, LEFT - rim
        self.window = -(-(CHUNK_ROWS + 2) * self.wide // 128) * 128


def rounded(field):
    return field.astype(BF16).astype(F32)


def shifted(block, offset, length):
    if offset % block.shape[1]:
        block = pltpu.roll(block, (-offset) % block.shape[1], 1)
    return block[:, :length]


def lay_rows(source_ref, first_row, lane, wide, target_ref):
    lanes = lax.broadcasted_iota(jnp.int32, (8, 128), 1)
    tiles = {}
    for number in range(CHUNK_ROWS + 2):
        place = pl.ds(pl.multiple_of(8 * (first_row + number), 8), 8)
        block = jnp.concatenate([source_ref[half, place] for half in range(2)], axis=1)
        start = number * wide
        tile, offset = start // 128, start % 128
        block = pltpu.roll(block, (offset - lane) % 256, 1)
        for part in range(-(-(offset + wide) // 128)):
            piece = block[:, 128 * (part % 2) : 128 * (part % 2) + 128]
            if part == 0 and offset:
                piece = jnp.where(lanes < offset, tiles[tile], piece)
            tiles[tile + part] = piece
    for tile in range(target_ref.shape[1] // 128):
        target_ref[:, 128 * tile : 128 * tile + 128] = tiles[tile]


def split_rows(flat, target_ref, first_row, lane, wide):
    for number in range(CHUNK_ROWS):
        start = number * wide
        tile, offset = start // 128, start % 128
        parts = max(2, -(-(offset + wide) // 128))
        if tile + parts > flat.shape[1] // 128:
            tile, offset = tile - 1, offset + 128
        block = flat[:, 128 * tile : 128 * (tile + parts)]
        block = shifted(block, offset - lane, 256)
        place = pl.ds(pl.multiple_of(8 * (first_row + number), 8), 8)
        for half in range(2):
            target_ref[half, place] = block[:, 128 * half : 128 * half + 128]


def channel(ref, number, first_row, rows):
    place = pl.ds(8 * first_row + number, rows, stride=8)
    return jnp.concatenate([ref[half, place] for half in range(2)], axis=1)


def keep_channel(ref, number, first_row, field):
    place = pl.ds(8 * first_row + number, field.shape[0], stride=8)
    for half in range(2):
        ref[half, place] = field[:, 128 * half : 128 * half + 128]


def keep_inputs(v, inputs_ref):
    inputs_ref[...] = jnp.zeros_like(inputs_ref)
    for comp in range(2):
        field = rounded(v[comp])
        for col in range(3):
            keep_channel(inputs_ref, 2 * col + comp, 0, by_col(field, col))
    keep_channel(inputs_ref, 6, 0, jnp.ones_like(v[0]))


def product(left, right):
    return lax.dot_general(left, right, (((1,), (0,)), ((), ())), preferred_element_type=F32)


def product_over_cells(left, right):
    return lax.dot_general(left, right, (((1,), (1,)), ((), ())), preferred_element_type=F32)


def columns(plan, row, inputs_ref, window_ref):
    lay_rows(inputs_ref, plan.in_row + row, plan.in_lane, plan.wide, window_ref)
    window = window_ref[...]
    parts = [shifted(window, row * plan.wide, plan.chunk) for row in range(3)]
    return jnp.concatenate(parts + [jnp.zeros((8, plan.chunk), F32)], axis=0)


def add_taps(terms_ref, offsets, length):
    total = None
    for tap, offset in enumerate(offsets):
        term = shifted(terms_ref[8 * tap : 8 * tap + 8, :], offset, length)
        total = term if total is None else total + term
    return total


def before_silu(weight_ref, inputs, bias_ref):
    bias = jnp.concatenate([bias_ref[...]] * (inputs.shape[1] // 128), axis=1)
    return product(weight_ref[...], inputs) + bias


def network(plan, inputs_ref, weight_refs, coefs_ref, window_ref, terms_ref, one_ref, two_ref):
    w1_ref, b1_ref, w2_ref, b2_ref, w3_ref = weight_refs
    terms_ref[...] = jnp.zeros_like(terms_ref)
    one_ref[...] = jnp.zeros_like(one_ref)
    two_ref[...] = jnp.zeros_like(two_ref)
    lag = LEAD - 2 * plan.wide

    def one_turn(turn, carried):
        last = jnp.maximum(turn - 2, 0)
        terms_ref[:, :LEAD] = terms_ref[:, plan.chunk :]
        cols = columns(plan, CHUNK_ROWS * jnp.minimum(turn, plan.chunks - 1), inputs_ref, window_ref).astype(BF16)
        terms_ref[:, LEAD:] = product(w3_ref[...], two_ref[...])
        half = before_silu(w2_ref, one_ref[...], b2_ref)
        two_ref[...] = (half * jnp.tanh(half) + half).astype(BF16)
        half = before_silu(w1_ref, cols, b1_ref)
        one_ref[...] = (half * jnp.tanh(half) + half).astype(BF16)
        total = COEF_SCALE * add_taps(terms_ref, [offset + lag for offset in plan.offsets], plan.chunk)
        split_rows(total, coefs_ref, plan.out_row - 2 + CHUNK_ROWS * last, plan.out_lane, plan.wide)
        return carried

    lax.fori_loop(0, plan.chunks + 2, one_turn, 0)


def with_slope(half):
    bend = jnp.tanh(half)
    return half * bend + half, (0.5 + 0.5 * bend) * (1.0 + half * (1.0 - bend))


def network_back(plan, inputs_ref, taps_ref, weight_refs, place_ref, grads_ref, sums_ref, net_refs):
    w1_ref, b1_ref, w2_ref, b2_ref, w1b_ref, w2b_ref, w3b_ref = weight_refs
    cross_ref, window_ref, terms_ref = net_refs
    terms_ref[...] = jnp.zeros_like(terms_ref)
    cross_ref[...] = jnp.zeros_like(cross_ref)

    def one_chunk(step, carried):
        row = CHUNK_ROWS * step
        place = place_ref[...] + row
        own = jnp.where((place >= plan.rim + 1) & (place < plan.rim + 1 + plan.rows), 1.0, 0.0).astype(BF16)
        own = jnp.concatenate([own] * 4, axis=0)
        cols = columns(plan, row, inputs_ref, window_ref).astype(BF16)
        hidden, slope_one = with_slope(before_silu(w1_ref, cols, b1_ref))
        hidden_one = hidden.astype(BF16)
        hidden, slope_two = with_slope(before_silu(w2_ref, hidden_one, b2_ref))
        hidden_two = hidden.astype(BF16)
        lay_rows(taps_ref, plan.out_row - 2 + row, plan.out_lane, plan.wide, window_ref)
        window = window_ref[...]
        parts = [shifted(window, 2 * plan.wide - offset, plan.chunk) for offset in plan.offsets]
        spread = jnp.concatenate(parts + [jnp.zeros((8, plan.chunk), F32)], axis=0).astype(BF16)
        grad_two = (product(w3b_ref[...], spread) * slope_two).astype(BF16)
        grad_one = (product(w2b_ref[...], grad_two) * slope_one).astype(BF16)
        left = jnp.concatenate([spread, hidden_one, cols], axis=0)
        right = jnp.concatenate([hidden_two * own, grad_two * own, grad_one * own], axis=0)
        cross_ref[...] += product_over_cells(left, right)
        terms_ref[:, :LEAD] = terms_ref[:, plan.chunk :]
        terms_ref[:, LEAD:] = product(w1b_ref[...], grad_one)
        total = add_taps(terms_ref, [LEAD - offset for offset in plan.offsets], plan.chunk)
        split_rows(total, grads_ref, plan.in_row + row, plan.in_lane, plan.wide)
        return carried

    def one_group(group, carried):
        for number in range(GROUP):
            one_chunk(GROUP * group + number, carried)
        return carried

    lax.fori_loop(0, plan.chunks // GROUP, one_group, 0)
    for number in range(plan.chunks // GROUP * GROUP, plan.chunks):
        one_chunk(number, 0)
    for tap in range(9):
        taken = 144 + 8 * (tap // 3) + 2 * (tap % 3)
        sums_ref[8 * tap : 8 * tap + 6, :64] += cross_ref[8 * tap : 8 * tap + 6, :64]
        sums_ref[8 * tap + 6 : 8 * tap + 8, :64] += cross_ref[taken : taken + 2, 128:192]
    sums_ref[:64, 64:] += cross_ref[80:144, 64:128]
    sums_ref[64:65, 64:] += cross_ref[150:151, 128:192]
    sums_ref[65:66, 64:] += cross_ref[150:151, 64:128]


def own_part(field, rows, cols, first_row):
    return pltpu.roll(field[TOP - first_row : TOP - first_row + rows], 256 - LEFT, 1)[:, :cols]


def lane_sums(squares):
    return jnp.sum(squares, axis=0, keepdims=True)


def strips_kernel(v_ref, goals_ref, low_ref, high_ref):
    rim = low_ref.shape[1]
    for number in range(4):
        field = v_ref[number] if number < 2 else goals_ref[goals_ref.shape[0] - 1, number - 2]
        low_ref[number], high_ref[number] = side_strips(field, rim)


def weights_kernel(w1_in, b1_in, w2_in, b2_in, w3_in, w1, b1, w2, b2, w3, w1b, w3b):
    hid = b1_in.shape[1]
    ahead, wide, back = [], [], []
    for row in range(3):
        parts = [w1_in[row, col].astype(F32) for col in range(3)]
        ahead += parts + [jnp.zeros((2, hid), F32)]
        for col in range(3):
            wide += [parts[col], jnp.zeros((6, hid), F32)]
            back += [w3_in[row, col].astype(F32), jnp.zeros((2, hid), F32)]
    ahead = jnp.concatenate(ahead + [jnp.zeros((8, hid), F32)], axis=0)
    back = jnp.concatenate(back, axis=0)
    w1[...] = (0.5 * ahead).T.astype(BF16)
    w1b[...] = jnp.concatenate(wide, axis=0).astype(BF16)
    w2[...] = (0.5 * w2_in[...].astype(F32)).T.astype(BF16)
    w3[...] = back.astype(BF16)
    w3b[...] = jnp.concatenate([back, jnp.zeros((8, hid), F32)], axis=0).T.astype(BF16)
    for source, target in ((b1_in, b1), (b2_in, b2)):
        target[...] = jnp.broadcast_to(0.5 * source[...], (128, hid)).T


def first_kernel(plan, left, right, above, below, own_ref, goals_ref, force_ref, w1, b1, w2, b2, w3,
                 v_ref, last_goal_ref, v_out, coefs_ref, error_ref, loss_ref, inputs_ref, window_ref, terms_ref, one_ref, two_ref, frame_ref, buffers, rhs_ref):
    pieces = (left, right, above, below)
    for comp in range(2):
        build_frame(own_ref[comp], pieces, comp, v_ref, comp)
        build_frame(goals_ref[goals_ref.shape[0] - 1, comp], pieces, comp + 2, last_goal_ref, comp)
    keep_inputs([v_ref[0], v_ref[1]], inputs_ref)
    coefs_ref[...] = jnp.zeros_like(coefs_ref)
    network(plan, inputs_ref, (w1, b1, w2, b2, w3), coefs_ref, window_ref, terms_ref, one_ref, two_ref)
    height = v_ref.shape[1]
    result = advect(
        [v_ref[0], v_ref[1]], [channel(coefs_ref, number, 0, height) for number in range(6)], force_ref[...]
    )
    for comp in range(2):
        frame_ref[comp] = result[comp]
    result = project(frame_ref[0], frame_ref[1], buffers, rhs_ref, 24)
    loss = None
    for comp in range(2):
        v_out[comp] = result[comp]
        error = own_part(result[comp], plan.rows, plan.cols, 0) - goals_ref[0, comp]
        error_ref[comp] = error
        square = lane_sums(error * error)
        loss = square if loss is None else loss + square
    loss_ref[...] = loss[:, :64] + loss[:, 64:]


def second_kernel(plan, v_ref, force_ref, w1, b1, w2, b2, w3, out_ref, low_ref, high_ref, coefs_ref, inputs_ref, window_ref,
                  terms_ref, one_ref, two_ref):
    keep_inputs([v_ref[0], v_ref[1]], inputs_ref)
    coefs_ref[...] = jnp.zeros_like(coefs_ref)
    network(plan, inputs_ref, (w1, b1, w2, b2, w3), coefs_ref, window_ref, terms_ref, one_ref, two_ref)
    low, tall = TOP - 8, plan.rows + 16
    v = [v_ref[comp, low : low + tall] for comp in range(2)]
    result = advect(v, [channel(coefs_ref, number, low, tall) for number in range(6)], force_ref[...])
    for comp in range(2):
        mine = own_part(result[comp], plan.rows, plan.cols, low)
        out_ref[comp] = mine
        low_ref[comp], high_ref[comp] = side_strips(mine, low_ref.shape[1])


def back_kernel(plan, last, left, right, above, below, own_ref, goal_ref, extra_ref, before_ref, v_ref, coefs_ref,
                place_ref, w1, b1, w2, b2, w1b, w2b, w3b, out_ref, low_ref, high_ref, sums_ref, inputs_ref, taps_ref, grads_ref, frame_ref, buffers, rhs_ref, *net_refs):
    rows, cols = plan.rows, plan.cols
    if last:
        sums_ref[...] = jnp.zeros_like(sums_ref)
        sums_ref[66:67, 64:] = before_ref[...]
    else:
        sums_ref[...] = before_ref[...]
    for comp in range(2):
        build_frame(own_ref[comp], (left, right, above, below), comp, frame_ref, comp)
    first, second = project(frame_ref[0], frame_ref[1], buffers, rhs_ref, TOP if last else 24)
    if last:
        errors = (first - goal_ref[0], second - goal_ref[1])
        for error in errors:
            mine = own_part(error, rows, cols, 0)
            loss = lane_sums(mine * mine)
            sums_ref[66:67, 64:] += loss[:, :64] + loss[:, 64:]
        for comp in range(2):
            frame_ref[comp] = errors[comp]
        first, second = project(frame_ref[0], frame_ref[1], buffers, rhs_ref, 24)
    frame_ref[0] = first
    frame_ref[1] = second
    keep_inputs([v_ref[0], v_ref[1]], inputs_ref)
    taps_ref[...] = jnp.zeros_like(taps_ref)
    low, tall = TOP - 8, rows + 16
    result = advect_back(
        [v_ref[comp, low : low + tall] for comp in range(2)],
        [channel(coefs_ref, number, low, tall) for number in range(6)],
        [frame_ref[comp, low : low + tall] for comp in range(2)],
        lambda number, field: keep_channel(taps_ref, number, low, rounded(field)),
    )
    for comp in range(2):
        frame_ref[comp, low : low + tall] = result[comp]
    weight_refs = (w1, b1, w2, b2, w1b, w2b, w3b)
    network_back(plan, inputs_ref, taps_ref, weight_refs, place_ref, grads_ref, sums_ref, net_refs)
    for comp in range(2):
        field = frame_ref[comp, low : low + tall] + channel(grads_ref, comp, low, tall)
        total = own_part(field, rows, cols, low)
        if last:
            total = total + extra_ref[comp]
            low_ref[comp], high_ref[comp] = side_strips(total, low_ref.shape[1])
        out_ref[comp] = total
    if not last:
        low_ref[...] = jnp.zeros_like(low_ref)
        high_ref[...] = jnp.zeros_like(high_ref)


def scaled(piece, count):
    return piece * (1.0 / jnp.sqrt(jnp.sum(piece * piece) / count + EPSILON))


def finish_kernel(loss_scale, in_ref, w1_ref, b1_ref, w2_ref, b2_ref, w3_ref, loss_ref):
    one = jnp.concatenate([in_ref[8 * tap + 6 : 8 * tap + 8, :64] for tap in range(9)], axis=0)
    three = jnp.concatenate([in_ref[8 * tap : 8 * tap + 6, :64] for tap in range(9)], axis=0)
    one, three = scaled(one, one.size), scaled(three, three.size)
    for tap in range(9):
        w1_ref[tap // 3, tap % 3] = one[2 * tap : 2 * tap + 2]
        w3_ref[tap // 3, tap % 3] = three[6 * tap : 6 * tap + 6]
    b1_ref[...] = scaled(in_ref[64:65, 64:], 64)
    b2_ref[...] = scaled(in_ref[65:66, 64:], 64)
    w2_ref[...] = scaled(in_ref[:64, 64:], 64 * 64)
    loss_ref[...] = (0.5 * loss_scale) * jnp.sum(in_ref[66:67, 64:], axis=1, keepdims=True)


def shards(velocity, targets, weight_one, bias_one, weight_two, bias_two, weight_three):
    rows, cols = velocity.shape[2], velocity.shape[3]
    step_count = targets.shape[1]
    height = rows + 2 * TOP
    frame = (height, cols + 2 * LEFT)
    pair = (2,) + frame
    own_pair = (2, rows, cols)
    packed = (2, 8 * height, 128)
    sums_shape = (72, 128)
    hid = weight_two.shape[0]
    nout = weight_three.shape[3]
    near = Plan(rows, cols, 2)
    far = Plan(rows, cols, 23)

    def call(kernel, outs, scratch, *args, kind=F32):
        return pl.pallas_call(
            kernel,
            out_shape=[jax.ShapeDtypeStruct(shape, F32 if shape[1] == 128 else kind) for shape in outs],
            scratch_shapes=[pltpu.VMEM(item, F32) if isinstance(item, tuple) else item for item in scratch],
            compiler_params=pltpu.CompilerParams(vmem_limit_bytes=VMEM_BYTES),
        )(*args)

    def net_scratch(plan):
        return [(8, plan.window), (72, plan.chunk + LEAD)]

    def layers(plan):
        return [pltpu.VMEM((hid, plan.chunk), BF16)] * 2

    sweep_scratch = [pair, (2, 2, height + 2 * GUARD, 128), (2, height, 128)]

    w1, b1, w2, b2, w3, w1b, w3b = call(
        weights_kernel, [(hid, 32), (hid, 128), (hid, hid), (hid, 128), (72, hid), (72, hid), (hid, 80)], [],
        weight_one, bias_one[None, :], weight_two, bias_two[None, :], jnp.swapaxes(weight_three, 2, 3), kind=BF16,
    )
    forward_weights = (w1, b1, w2, b2, w3)
    backward_weights = (w1, b1, w2, b2, w1b, weight_two, w3b)

    lane = np.arange(near.chunk)
    place_row, place_col = lane // near.wide, lane % near.wide
    mine = (place_col >= near.rim + 1) & (place_col < near.rim + 1 + cols)
    place = jnp.asarray(np.tile(np.where(mine, place_row, -10 * height), (16, 1)), jnp.int32)

    total_cols = cols * lax.axis_size("gy")
    col_ids = lax.axis_index("gy") * cols + jnp.arange(frame[1], dtype=jnp.int32) - LEFT
    forcing = jnp.sin(col_ids.astype(F32) * (TWO_PI * FORCE_WAVES / total_cols))[None, :]

    def strips(count, rim):
        return [(count, rim, rows)] * 2

    sides = call(strips_kernel, strips(4, 32), [], velocity[0], targets[0])
    pieces = exchange([velocity[0], targets[0, step_count - 1]], sides)
    v_first, last_goal, v_second, coefs_first, error_first, loss_first = call(
        functools.partial(first_kernel, far),
        [pair, pair, pair, packed, own_pair, (1, 64)],
        [packed] + net_scratch(far) + layers(far) + sweep_scratch,
        *pieces, velocity[0], targets[0], forcing, *forward_weights,
    )
    provisional, low, high, coefs_second = call(
        functools.partial(second_kernel, near),
        [own_pair] + strips(2, 40) + [packed],
        [packed] + net_scratch(near) + layers(near),
        v_second, forcing, *forward_weights,
    )
    back_scratch = [packed, packed, packed] + sweep_scratch + [(176, 192)] + net_scratch(near)
    grad, low, high, sums = call(
        functools.partial(back_kernel, near, True),
        [own_pair] + strips(2, 24) + [sums_shape], back_scratch,
        *exchange([provisional], (low, high)), provisional, last_goal, error_first, loss_first, v_second, coefs_second, place,
        *backward_weights,
    )
    grad, _, _, sums = call(
        functools.partial(back_kernel, near, False),
        [own_pair] + [(1, 8, 128)] * 2 + [sums_shape], back_scratch,
        *exchange([grad], (low, high)), grad, forcing, forcing, sums, v_first, coefs_first, place, *backward_weights,
    )
    for axis in ("ens", "gx", "gy"):
        sums = total_over(sums, axis)
    device_count = lax.axis_size(("ens", "gx", "gy"))
    loss_scale = 1.0 / float(step_count * 2 * rows * cols * device_count)
    d1, db1, d2, db2, d3, loss = call(
        functools.partial(finish_kernel, loss_scale),
        [(3, 3, 2, hid), (1, hid), (hid, hid), (1, hid), (3, 3, nout, hid), (1, 1)], [], sums,
    )
    return (
        d1,
        db1[0],
        d2,
        db2[0],
        jnp.swapaxes(d3, 2, 3),
        loss[0, 0],
        grad[None],
    )


def solution(mesh):
    return jax.shard_map(
        shards,
        mesh=mesh,
        in_specs=(P("ens", None, "gx", "gy"), P("ens", None, None, "gx", "gy"), P(), P(), P(), P(), P()),
        out_specs=(P(), P(), P(), P(), P(), P(), P("ens", None, "gx", "gy")),
        check_vma=False,
    )
```

```python
import functools

import jax
import jax.numpy as jnp
import numpy as np
from jax import lax
from jax.experimental import pallas as pl
from jax.experimental.pallas import tpu as pltpu
from jax.sharding import PartitionSpec as P

SWEEPS = 16
TIME_STEP = 0.2
VISCOSITY = 0.05
DRAG_RATE = 0.1
FORCE_WAVES = 4.0
COEF_SCALE = 0.1
EPSILON = 1e-06
OUTER_WEIGHT = -1.0 / 16.0
INNER_WEIGHT = 9.0 / 16.0
TWO_PI = 6.283185307179586

TOP = 40
LEFT = 64
CHUNK_ROWS = 16
LEAD = 384
GUARD = 8
GROUP = 4
VMEM_BYTES = 40 << 20
BF16 = jnp.bfloat16
F32 = jnp.float32


def passed_along(block, axis, distance):
    size = lax.axis_size(axis)
    route = [(i, (i + distance) % size) for i in range(size)]
    return lax.ppermute(block, axis, route)


def exchange(owns, sides):
    rim, rows = sides[0].shape[1:]
    right = passed_along(sides[0], "gy", -1)
    left = passed_along(sides[1], "gy", 1)
    edges = []
    for first, tile, distance in ((rows - rim, rows - 128, 1), (0, 0, -1)):
        mine = jnp.concatenate([own[:, first : first + rim] for own in owns], axis=0)
        parts = [mine] + [part[:, :, tile : tile + 128] for part in (left, right)]
        edges.append(passed_along(jnp.concatenate(parts, axis=1), "gx", distance))
    return [left, right] + edges


def side_strips(field, rim):
    turned = field.T
    return turned[:rim], turned[turned.shape[0] - rim :]


def spread_out(middle, left, right, rows):
    rim = left.shape[0]
    lanes = left.shape[1]
    before = jnp.concatenate([jnp.zeros((LEFT - rim, lanes), F32), left, jnp.zeros((128 - LEFT, lanes), F32)], axis=0).T
    after = jnp.concatenate([jnp.zeros((LEFT, lanes), F32), right, jnp.zeros((128 - LEFT - rim, lanes), F32)], axis=0).T
    turned = pltpu.roll(middle, LEFT, 1)
    first_half = lax.broadcasted_iota(jnp.int32, middle.shape, 1) < LEFT
    return jnp.concatenate(
        [jnp.where(first_half, before[rows], turned), jnp.where(first_half, turned, after[rows])], axis=1
    )


def build_frame(own, pieces, comp, target_ref, target):
    left_ref, right_ref, above_ref, below_ref = pieces
    rim = left_ref.shape[1]
    rows = own.shape[0]
    if rim < TOP:
        target_ref[target, : TOP - rim] = jnp.zeros((TOP - rim, 256), F32)
        target_ref[target, TOP + rows + rim :] = jnp.zeros((TOP - rim, 256), F32)
    target_ref[target, TOP : TOP + rows] = spread_out(
        own, left_ref[comp], right_ref[comp], slice(0, rows)
    )
    for ref, first, kept in ((above_ref, TOP - rim, slice(128 - rim, 128)), (below_ref, TOP + rows, slice(0, rim))):
        target_ref[target, first : first + rim] = spread_out(
            ref[comp, :rim], ref[comp, rim : 2 * rim], ref[comp, 2 * rim :], kept
        )


def total_over(value, axis):
    size = lax.axis_size(axis)
    if size <= 4:
        moved = [passed_along(value, axis, distance) for distance in range(1, size)]
        for other in moved:
            value = value + other
        return value
    return lax.psum(value, axis)


def at(field, rows, cols):
    if rows:
        field = pltpu.roll(field, (-rows) % field.shape[0], 0)
    if cols:
        field = pltpu.roll(field, (-cols) % field.shape[1], 1)
    return field


def project(first, second, buffers, rhs_ref, rim):
    height = first.shape[0]
    quarter = -0.125 * (at(first, 1, 0) - at(first, -1, 0) + at(second, 0, 1) - at(second, 0, -1))
    for half in range(2):
        part = quarter[:, 128 * half : 128 * half + 128]
        rhs_ref[half] = part
        for buffer in range(2):
            buffers[buffer, half, :GUARD] = jnp.zeros((GUARD, 128), F32)
            buffers[buffer, half, GUARD + height :] = jnp.zeros((GUARD, 128), F32)
            buffers[buffer, half, GUARD : GUARD + height] = part
    lane = lax.broadcasted_iota(jnp.int32, (8, 128), 1)
    at_start = lane == 0
    at_end = lane == 127

    def one_sweep(source, target):
        for row in range(TOP - rim, height - TOP + rim, 8):
            here = [buffers[source, half, GUARD + row : GUARD + row + 8] for half in range(2)]
            ahead = [pltpu.roll(part, 127, 1) for part in here]
            behind = [pltpu.roll(part, 1, 1) for part in here]
            for half in range(2):
                above = buffers[source, half, GUARD + row - 1 : GUARD + row + 7]
                below = buffers[source, half, GUARD + row + 1 : GUARD + row + 9]
                east = jnp.where(at_end, ahead[1 - half], ahead[half])
                west = jnp.where(at_start, behind[1 - half], behind[half])
                near = (above + below) + (east + west)
                buffers[target, half, GUARD + row : GUARD + row + 8] = 0.25 * near + rhs_ref[half, row : row + 8]

    def two_sweeps(index, carried):
        one_sweep(0, 1)
        one_sweep(1, 0)
        return carried

    lax.fori_loop(0, SWEEPS // 2, two_sweeps, 0)
    p = jnp.concatenate([buffers[0, half, GUARD : GUARD + height] for half in range(2)], axis=1)
    above = jnp.concatenate([buffers[0, half, GUARD - 1 : GUARD - 1 + height] for half in range(2)], axis=1)
    below = jnp.concatenate([buffers[0, half, GUARD + 1 : GUARD + 1 + height] for half in range(2)], axis=1)
    return first - 0.5 * (below - above), second - 0.5 * (at(p, 0, 1) - at(p, 0, -1))


def faces(field, c0, c1, c2, move):
    return (
        (OUTER_WEIGHT + c0) * move(field, -1)
        + (INNER_WEIGHT + c1) * field
        + (INNER_WEIGHT + c2) * move(field, 1)
        + (OUTER_WEIGHT - c0 - c1 - c2) * move(field, 2)
    )


def by_row(field, distance):
    return at(field, distance, 0)


def by_col(field, distance):
    return at(field, 0, distance)


def advect(v, coefs, forcing):
    speed_rows = 0.5 * (v[0] + by_row(v[0], 1))
    speed_cols = 0.5 * (v[1] + by_col(v[1], 1))
    results = []
    for comp in range(2):
        q = v[comp]
        flux = speed_rows * faces(q, coefs[0], coefs[1], coefs[2], by_row)
        change = flux - by_row(flux, -1)
        flux = speed_cols * faces(q, coefs[3], coefs[4], coefs[5], by_col)
        change = change + (flux - by_col(flux, -1))
        laplace = by_row(q, 1) + by_row(q, -1) + by_col(q, 1) + by_col(q, -1) - 4.0 * q
        drive = VISCOSITY * laplace - DRAG_RATE * q
        if comp == 0:
            drive = drive + forcing
        results.append(q - TIME_STEP * change + TIME_STEP * drive)
    return results


def advect_back(v, coefs, g, keep_taps):
    results = [None, None]
    for axis in range(2):
        move = by_row if axis == 0 else by_col
        speed = 0.5 * (v[axis] + move(v[axis], 1))
        c0, c1, c2 = coefs[3 * axis : 3 * axis + 3]
        grads = []
        grad_speed = None
        taps = None
        for comp in range(2):
            q = v[comp]
            grad_flux = TIME_STEP * (move(g[comp], 1) - g[comp])
            term = grad_flux * faces(q, c0, c1, c2, move)
            grad_speed = term if grad_speed is None else grad_speed + term
            grad_face = grad_flux * speed
            behind = move(q, -1)
            ahead = move(q, 1)
            far = move(q, 2)
            new = (grad_face * (behind - far), grad_face * (q - far), grad_face * (ahead - far))
            taps = new if taps is None else tuple(a + b for a, b in zip(taps, new))
            grads.append(
                move(grad_face * (OUTER_WEIGHT + c0), 1)
                + grad_face * (INNER_WEIGHT + c1)
                + move(grad_face * (INNER_WEIGHT + c2), -1)
                + move(grad_face * (OUTER_WEIGHT - c0 - c1 - c2), -2)
            )
        grads[axis] = grads[axis] + 0.5 * (grad_speed + move(grad_speed, -1))
        for number in range(3):
            keep_taps(3 * axis + number, COEF_SCALE * taps[number])
        for comp in range(2):
            results[comp] = grads[comp] if axis == 0 else results[comp] + grads[comp]
    for comp in range(2):
        near = by_row(g[comp], 1) + by_row(g[comp], -1) + by_col(g[comp], 1) + by_col(g[comp], -1)
        drive = VISCOSITY * (near - 4.0 * g[comp]) - DRAG_RATE * g[comp]
        results[comp] = results[comp] + g[comp] + TIME_STEP * drive
    return results


class Plan:
    def __init__(self, rows, cols, rim):
        self.rows, self.cols, self.rim = rows, cols, rim
        self.wide = -(-(cols + 2 * rim + 4) // 8) * 8
        self.chunk = CHUNK_ROWS * self.wide
        self.chunks = -(-(rows + 2 * rim + 2) // CHUNK_ROWS)
        self.offsets = [row * self.wide + col for row in range(3) for col in range(3)]
        self.in_row, self.in_lane = TOP - rim - 2, LEFT - rim - 2
        self.out_row, self.out_lane = TOP - rim, LEFT - rim
        self.window = -(-(CHUNK_ROWS + 2) * self.wide // 128) * 128


def rounded(field):
    return field.astype(BF16).astype(F32)


def shifted(block, offset, length):
    if offset % block.shape[1]:
        block = pltpu.roll(block, (-offset) % block.shape[1], 1)
    return block[:, :length]


def lay_rows(source_ref, first_row, lane, wide, target_ref):
    lanes = lax.broadcasted_iota(jnp.int32, (8, 128), 1)
    tiles = {}
    for number in range(CHUNK_ROWS + 2):
        place = pl.ds(pl.multiple_of(8 * (first_row + number), 8), 8)
        block = jnp.concatenate([source_ref[half, place] for half in range(2)], axis=1)
        start = number * wide
        tile, offset = start // 128, start % 128
        block = pltpu.roll(block, (offset - lane) % 256, 1)
        for part in range(-(-(offset + wide) // 128)):
            piece = block[:, 128 * (part % 2) : 128 * (part % 2) + 128]
            if part == 0 and offset:
                piece = jnp.where(lanes < offset, tiles[tile], piece)
            tiles[tile + part] = piece
    for tile in range(target_ref.shape[1] // 128):
        target_ref[:, 128 * tile : 128 * tile + 128] = tiles[tile]


def split_rows(flat, target_ref, first_row, lane, wide):
    for number in range(CHUNK_ROWS):
        start = number * wide
        tile, offset = start // 128, start % 128
        parts = max(2, -(-(offset + wide) // 128))
        if tile + parts > flat.shape[1] // 128:
            tile, offset = tile - 1, offset + 128
        block = flat[:, 128 * tile : 128 * (tile + parts)]
        block = shifted(block, offset - lane, 256)
        place = pl.ds(pl.multiple_of(8 * (first_row + number), 8), 8)
        for half in range(2):
            target_ref[half, place] = block[:, 128 * half : 128 * half + 128]


def channel(ref, number, first_row, rows):
    place = pl.ds(8 * first_row + number, rows, stride=8)
    return jnp.concatenate([ref[half, place] for half in range(2)], axis=1)


def keep_channel(ref, number, first_row, field):
    place = pl.ds(8 * first_row + number, field.shape[0], stride=8)
    for half in range(2):
        ref[half, place] = field[:, 128 * half : 128 * half + 128]


def keep_inputs(v, inputs_ref):
    inputs_ref[...] = jnp.zeros_like(inputs_ref)
    for comp in range(2):
        field = rounded(v[comp])
        for col in range(3):
            keep_channel(inputs_ref, 2 * col + comp, 0, by_col(field, col))
    keep_channel(inputs_ref, 6, 0, jnp.ones_like(v[0]))


def product(left, right):
    return lax.dot_general(left, right, (((1,), (0,)), ((), ())), preferred_element_type=F32)


def product_over_cells(left, right):
    return lax.dot_general(left, right, (((1,), (1,)), ((), ())), preferred_element_type=F32)


def columns(plan, row, inputs_ref, window_ref):
    lay_rows(inputs_ref, plan.in_row + row, plan.in_lane, plan.wide, window_ref)
    window = window_ref[...]
    parts = [shifted(window, row * plan.wide, plan.chunk) for row in range(3)]
    return jnp.concatenate(parts + [jnp.zeros((8, plan.chunk), F32)], axis=0)


def add_taps(terms_ref, offsets, length):
    total = None
    for tap, offset in enumerate(offsets):
        term = shifted(terms_ref[8 * tap : 8 * tap + 8, :], offset, length)
        total = term if total is None else total + term
    return total


def before_silu(weight_ref, inputs, bias_ref):
    bias = jnp.concatenate([bias_ref[...]] * (inputs.shape[1] // 128), axis=1)
    return product(weight_ref[...], inputs) + bias


def network(plan, inputs_ref, weight_refs, coefs_ref, window_ref, terms_ref, one_ref, two_ref):
    w1_ref, b1_ref, w2_ref, b2_ref, w3_ref = weight_refs
    terms_ref[...] = jnp.zeros_like(terms_ref)
    one_ref[...] = jnp.zeros_like(one_ref)
    two_ref[...] = jnp.zeros_like(two_ref)
    lag = LEAD - 2 * plan.wide

    def one_turn(turn, carried):
        last = jnp.maximum(turn - 2, 0)
        terms_ref[:, :LEAD] = terms_ref[:, plan.chunk :]
        cols = columns(plan, CHUNK_ROWS * jnp.minimum(turn, plan.chunks - 1), inputs_ref, window_ref).astype(BF16)
        terms_ref[:, LEAD:] = product(w3_ref[...], two_ref[...])
        half = before_silu(w2_ref, one_ref[...], b2_ref)
        two_ref[...] = (half * jnp.tanh(half) + half).astype(BF16)
        half = before_silu(w1_ref, cols, b1_ref)
        one_ref[...] = (half * jnp.tanh(half) + half).astype(BF16)
        total = COEF_SCALE * add_taps(terms_ref, [offset + lag for offset in plan.offsets], plan.chunk)
        split_rows(total, coefs_ref, plan.out_row - 2 + CHUNK_ROWS * last, plan.out_lane, plan.wide)
        return carried

    lax.fori_loop(0, plan.chunks + 2, one_turn, 0)


def with_slope(half):
    bend = jnp.tanh(half)
    return half * bend + half, (0.5 + 0.5 * bend) * (1.0 + half * (1.0 - bend))


def network_back(plan, inputs_ref, taps_ref, weight_refs, place_ref, grads_ref, sums_ref, net_refs):
    w1_ref, b1_ref, w2_ref, b2_ref, w1b_ref, w2b_ref, w3b_ref = weight_refs
    cross_ref, window_ref, terms_ref = net_refs
    terms_ref[...] = jnp.zeros_like(terms_ref)
    cross_ref[...] = jnp.zeros_like(cross_ref)

    def one_chunk(step, carried):
        row = CHUNK_ROWS * step
        place = place_ref[...] + row
        own = jnp.where((place >= plan.rim + 1) & (place < plan.rim + 1 + plan.rows), 1.0, 0.0).astype(BF16)
        own = jnp.concatenate([own] * 4, axis=0)
        cols = columns(plan, row, inputs_ref, window_ref).astype(BF16)
        hidden, slope_one = with_slope(before_silu(w1_ref, cols, b1_ref))
        hidden_one = hidden.astype(BF16)
        hidden, slope_two = with_slope(before_silu(w2_ref, hidden_one, b2_ref))
        hidden_two = hidden.astype(BF16)
        lay_rows(taps_ref, plan.out_row - 2 + row, plan.out_lane, plan.wide, window_ref)
        window = window_ref[...]
        parts = [shifted(window, 2 * plan.wide - offset, plan.chunk) for offset in plan.offsets]
        spread = jnp.concatenate(parts + [jnp.zeros((8, plan.chunk), F32)], axis=0).astype(BF16)
        grad_two = (product(w3b_ref[...], spread) * slope_two).astype(BF16)
        grad_one = (product(w2b_ref[...], grad_two) * slope_one).astype(BF16)
        left = jnp.concatenate([spread, hidden_one, cols], axis=0)
        right = jnp.concatenate([hidden_two * own, grad_two * own, grad_one * own], axis=0)
        cross_ref[...] += product_over_cells(left, right)
        terms_ref[:, :LEAD] = terms_ref[:, plan.chunk :]
        terms_ref[:, LEAD:] = product(w1b_ref[...], grad_one)
        total = add_taps(terms_ref, [LEAD - offset for offset in plan.offsets], plan.chunk)
        split_rows(total, grads_ref, plan.in_row + row, plan.in_lane, plan.wide)
        return carried

    def one_group(group, carried):
        for number in range(GROUP):
            one_chunk(GROUP * group + number, carried)
        return carried

    lax.fori_loop(0, plan.chunks // GROUP, one_group, 0)
    for number in range(plan.chunks // GROUP * GROUP, plan.chunks):
        one_chunk(number, 0)
    for tap in range(9):
        taken = 144 + 8 * (tap // 3) + 2 * (tap % 3)
        sums_ref[8 * tap : 8 * tap + 6, :64] += cross_ref[8 * tap : 8 * tap + 6, :64]
        sums_ref[8 * tap + 6 : 8 * tap + 8, :64] += cross_ref[taken : taken + 2, 128:192]
    sums_ref[:64, 64:] += cross_ref[80:144, 64:128]
    sums_ref[64:65, 64:] += cross_ref[150:151, 128:192]
    sums_ref[65:66, 64:] += cross_ref[150:151, 64:128]


def own_part(field, rows, cols, first_row):
    return pltpu.roll(field[TOP - first_row : TOP - first_row + rows], 256 - LEFT, 1)[:, :cols]


def lane_sums(squares):
    return jnp.sum(squares, axis=0, keepdims=True)


def strips_kernel(v_ref, goals_ref, low_ref, high_ref):
    rim = low_ref.shape[1]
    for number in range(4):
        field = v_ref[number] if number < 2 else goals_ref[goals_ref.shape[0] - 1, number - 2]
        low_ref[number], high_ref[number] = side_strips(field, rim)


def weights_kernel(w1_in, b1_in, w2_in, b2_in, w3_in, w1, b1, w2, b2, w3, w1b, w3b):
    hid = b1_in.shape[1]
    ahead, wide, back = [], [], []
    for row in range(3):
        parts = [w1_in[row, col].astype(F32) for col in range(3)]
        ahead += parts + [jnp.zeros((2, hid), F32)]
        for col in range(3):
            wide += [parts[col], jnp.zeros((6, hid), F32)]
            back += [w3_in[row, col].astype(F32), jnp.zeros((2, hid), F32)]
    ahead = jnp.concatenate(ahead + [jnp.zeros((8, hid), F32)], axis=0)
    back = jnp.concatenate(back, axis=0)
    w1[...] = (0.5 * ahead).T.astype(BF16)
    w1b[...] = jnp.concatenate(wide, axis=0).astype(BF16)
    w2[...] = (0.5 * w2_in[...].astype(F32)).T.astype(BF16)
    w3[...] = back.astype(BF16)
    w3b[...] = jnp.concatenate([back, jnp.zeros((8, hid), F32)], axis=0).T.astype(BF16)
    for source, target in ((b1_in, b1), (b2_in, b2)):
        target[...] = jnp.broadcast_to(0.5 * source[...], (128, hid)).T


def first_kernel(plan, left, right, above, below, own_ref, goals_ref, force_ref, w1, b1, w2, b2, w3,
                 v_ref, last_goal_ref, v_out, coefs_ref, error_ref, loss_ref, inputs_ref, window_ref, terms_ref, one_ref, two_ref, frame_ref, buffers, rhs_ref):
    pieces = (left, right, above, below)
    for comp in range(2):
        build_frame(own_ref[comp], pieces, comp, v_ref, comp)
        build_frame(goals_ref[goals_ref.shape[0] - 1, comp], pieces, comp + 2, last_goal_ref, comp)
    keep_inputs([v_ref[0], v_ref[1]], inputs_ref)
    coefs_ref[...] = jnp.zeros_like(coefs_ref)
    network(plan, inputs_ref, (w1, b1, w2, b2, w3), coefs_ref, window_ref, terms_ref, one_ref, two_ref)
    height = v_ref.shape[1]
    result = advect(
        [v_ref[0], v_ref[1]], [channel(coefs_ref, number, 0, height) for number in range(6)], force_ref[...]
    )
    for comp in range(2):
        frame_ref[comp] = result[comp]
    result = project(frame_ref[0], frame_ref[1], buffers, rhs_ref, 24)
    loss = None
    for comp in range(2):
        v_out[comp] = result[comp]
        error = own_part(result[comp], plan.rows, plan.cols, 0) - goals_ref[0, comp]
        error_ref[comp] = error
        square = lane_sums(error * error)
        loss = square if loss is None else loss + square
    loss_ref[...] = loss[:, :64] + loss[:, 64:]


def second_kernel(plan, v_ref, force_ref, w1, b1, w2, b2, w3, out_ref, low_ref, high_ref, coefs_ref, inputs_ref, window_ref,
                  terms_ref, one_ref, two_ref):
    keep_inputs([v_ref[0], v_ref[1]], inputs_ref)
    network(plan, inputs_ref, (w1, b1, w2, b2, w3), coefs_ref, window_ref, terms_ref, one_ref, two_ref)
    low, tall = TOP - 8, plan.rows + 16
    v = [v_ref[comp, low : low + tall] for comp in range(2)]
    result = advect(v, [channel(coefs_ref, number, low, tall) for number in range(6)], force_ref[...])
    for comp in range(2):
        mine = own_part(result[comp], plan.rows, plan.cols, low)
        out_ref[comp] = mine
        low_ref[comp], high_ref[comp] = side_strips(mine, low_ref.shape[1])


def back_kernel(plan, last, left, right, above, below, own_ref, goal_ref, extra_ref, before_ref, v_ref, coefs_ref,
                place_ref, w1, b1, w2, b2, w1b, w2b, w3b, out_ref, low_ref, high_ref, sums_ref, inputs_ref, taps_ref, grads_ref, frame_ref, buffers, rhs_ref, *net_refs):
    rows, cols = plan.rows, plan.cols
    if last:
        sums_ref[...] = jnp.zeros_like(sums_ref)
        sums_ref[66:67, 64:] = before_ref[...]
    else:
        sums_ref[...] = before_ref[...]
    for comp in range(2):
        build_frame(own_ref[comp], (left, right, above, below), comp, frame_ref, comp)
    first, second = project(frame_ref[0], frame_ref[1], buffers, rhs_ref, TOP if last else 24)
    if last:
        errors = (first - goal_ref[0], second - goal_ref[1])
        for error in errors:
            mine = own_part(error, rows, cols, 0)
            loss = lane_sums(mine * mine)
            sums_ref[66:67, 64:] += loss[:, :64] + loss[:, 64:]
        for comp in range(2):
            frame_ref[comp] = errors[comp]
        first, second = project(frame_ref[0], frame_ref[1], buffers, rhs_ref, 24)
    frame_ref[0] = first
    frame_ref[1] = second
    keep_inputs([v_ref[0], v_ref[1]], inputs_ref)
    taps_ref[...] = jnp.zeros_like(taps_ref)
    low, tall = TOP - 8, rows + 16
    result = advect_back(
        [v_ref[comp, low : low + tall] for comp in range(2)],
        [channel(coefs_ref, number, low, tall) for number in range(6)],
        [frame_ref[comp, low : low + tall] for comp in range(2)],
        lambda number, field: keep_channel(taps_ref, number, low, rounded(field)),
    )
    for comp in range(2):
        frame_ref[comp, low : low + tall] = result[comp]
    weight_refs = (w1, b1, w2, b2, w1b, w2b, w3b)
    network_back(plan, inputs_ref, taps_ref, weight_refs, place_ref, grads_ref, sums_ref, net_refs)
    for comp in range(2):
        field = frame_ref[comp, low : low + tall] + channel(grads_ref, comp, low, tall)
        total = own_part(field, rows, cols, low)
        if last:
            total = total + extra_ref[comp]
            low_ref[comp], high_ref[comp] = side_strips(total, low_ref.shape[1])
        out_ref[comp] = total
    if not last:
        low_ref[...] = jnp.zeros_like(low_ref)
        high_ref[...] = jnp.zeros_like(high_ref)


def scaled(piece, count):
    return piece * (1.0 / jnp.sqrt(jnp.sum(piece * piece) / count + EPSILON))


def finish_kernel(loss_scale, in_ref, w1_ref, b1_ref, w2_ref, b2_ref, w3_ref, loss_ref):
    one = jnp.concatenate([in_ref[8 * tap + 6 : 8 * tap + 8, :64] for tap in range(9)], axis=0)
    three = jnp.concatenate([in_ref[8 * tap : 8 * tap + 6, :64] for tap in range(9)], axis=0)
    one, three = scaled(one, one.size), scaled(three, three.size)
    for tap in range(9):
        w1_ref[tap // 3, tap % 3] = one[2 * tap : 2 * tap + 2]
        w3_ref[tap // 3, tap % 3] = three[6 * tap : 6 * tap + 6]
    b1_ref[...] = scaled(in_ref[64:65, 64:], 64)
    b2_ref[...] = scaled(in_ref[65:66, 64:], 64)
    w2_ref[...] = scaled(in_ref[:64, 64:], 64 * 64)
    loss_ref[...] = (0.5 * loss_scale) * jnp.sum(in_ref[66:67, 64:], axis=1, keepdims=True)


def shards(velocity, targets, weight_one, bias_one, weight_two, bias_two, weight_three):
    rows, cols = velocity.shape[2], velocity.shape[3]
    step_count = targets.shape[1]
    height = rows + 2 * TOP
    frame = (height, cols + 2 * LEFT)
    pair = (2,) + frame
    own_pair = (2, rows, cols)
    packed = (2, 8 * height, 128)
    sums_shape = (72, 128)
    hid = weight_two.shape[0]
    nout = weight_three.shape[3]
    near = Plan(rows, cols, 2)
    far = Plan(rows, cols, 23)

    def call(kernel, outs, scratch, *args, kind=F32):
        return pl.pallas_call(
            kernel,
            out_shape=[jax.ShapeDtypeStruct(shape, F32 if shape[1] == 128 else kind) for shape in outs],
            scratch_shapes=[pltpu.VMEM(item, F32) if isinstance(item, tuple) else item for item in scratch],
            compiler_params=pltpu.CompilerParams(vmem_limit_bytes=VMEM_BYTES),
        )(*args)

    def net_scratch(plan):
        return [(8, plan.window), (72, plan.chunk + LEAD)]

    def layers(plan):
        return [pltpu.VMEM((hid, plan.chunk), BF16)] * 2

    sweep_scratch = [pair, (2, 2, height + 2 * GUARD, 128), (2, height, 128)]

    w1, b1, w2, b2, w3, w1b, w3b = call(
        weights_kernel, [(hid, 32), (hid, 128), (hid, hid), (hid, 128), (72, hid), (72, hid), (hid, 80)], [],
        weight_one, bias_one[None, :], weight_two, bias_two[None, :], jnp.swapaxes(weight_three, 2, 3), kind=BF16,
    )
    forward_weights = (w1, b1, w2, b2, w3)
    backward_weights = (w1, b1, w2, b2, w1b, weight_two, w3b)

    lane = np.arange(near.chunk)
    place_row, place_col = lane // near.wide, lane % near.wide
    mine = (place_col >= near.rim + 1) & (place_col < near.rim + 1 + cols)
    place = jnp.asarray(np.tile(np.where(mine, place_row, -10 * height), (16, 1)), jnp.int32)

    total_cols = cols * lax.axis_size("gy")
    col_ids = lax.axis_index("gy") * cols + jnp.arange(frame[1], dtype=jnp.int32) - LEFT
    forcing = jnp.sin(col_ids.astype(F32) * (TWO_PI * FORCE_WAVES / total_cols))[None, :]

    def strips(count, rim):
        return [(count, rim, rows)] * 2

    sides = call(strips_kernel, strips(4, 32), [], velocity[0], targets[0])
    pieces = exchange([velocity[0], targets[0, step_count - 1]], sides)
    v_first, last_goal, v_second, coefs_first, error_first, loss_first = call(
        functools.partial(first_kernel, far),
        [pair, pair, pair, packed, own_pair, (1, 64)],
        [packed] + net_scratch(far) + layers(far) + sweep_scratch,
        *pieces, velocity[0], targets[0], forcing, *forward_weights,
    )
    provisional, low, high, coefs_second = call(
        functools.partial(second_kernel, near),
        [own_pair] + strips(2, 40) + [packed],
        [packed] + net_scratch(near) + layers(near),
        v_second, forcing, *forward_weights,
    )
    back_scratch = [packed, packed, packed] + sweep_scratch + [(176, 192)] + net_scratch(near)
    grad, low, high, sums = call(
        functools.partial(back_kernel, near, True),
        [own_pair] + strips(2, 24) + [sums_shape], back_scratch,
        *exchange([provisional], (low, high)), provisional, last_goal, error_first, loss_first, v_second, coefs_second, place,
        *backward_weights,
    )
    grad, _, _, sums = call(
        functools.partial(back_kernel, near, False),
        [own_pair] + [(1, 8, 128)] * 2 + [sums_shape], back_scratch,
        *exchange([grad], (low, high)), grad, forcing, forcing, sums, v_first, coefs_first, place, *backward_weights,
    )
    for axis in ("ens", "gx", "gy"):
        sums = total_over(sums, axis)
    device_count = lax.axis_size(("ens", "gx", "gy"))
    loss_scale = 1.0 / float(step_count * 2 * rows * cols * device_count)
    d1, db1, d2, db2, d3, loss = call(
        functools.partial(finish_kernel, loss_scale),
        [(3, 3, 2, hid), (1, hid), (hid, hid), (1, hid), (3, 3, nout, hid), (1, 1)], [], sums,
    )
    return (
        d1,
        db1[0],
        d2,
        db2[0],
        jnp.swapaxes(d3, 2, 3),
        loss[0, 0],
        grad[None],
    )


def solution(mesh):
    return jax.shard_map(
        shards,
        mesh=mesh,
        in_specs=(P("ens", None, "gx", "gy"), P("ens", None, None, "gx", "gy"), P(), P(), P(), P(), P()),
        out_specs=(P(), P(), P(), P(), P(), P(), P("ens", None, "gx", "gy")),
        check_vma=False,
    )
```
